32 devices in a mesh: row: 16 (over z, x, core), col: 2 (over y).
Axes of the slice: x: 2, y: 2, z: 4, core: 2. Of those that a mesh axis runs over, the one named last changes fastest.
Arguments:
- tokens: bfloat16 [2, 16, 1024, 768], P(None, 'row', 'col'), may hold values from -6 to 6
- w_qkv: bfloat16 [768, 2304], P('row', 'col'), may hold values from -0.21875 to 0.21875
- w_out: bfloat16 [768, 768], P('row', 'col'), may hold values from -0.875 to 0.875
- w_mem: bfloat16 [768, 1536], P('row', 'col'), may hold values from -0.21875 to 0.21875
- w_fc: bfloat16 [768, 3072], P('row', 'col'), may hold values from -0.21875 to 0.21875
- w_proj: bfloat16 [3072, 768], P('row', 'col'), may hold values from -0.109375 to 0.109375
- gain_attn: bfloat16 [768], P(('row', 'col')), may hold values from 0.099609375 to 1.8984375
- bias_attn: bfloat16 [768], P(('row', 'col')), may hold values from -3 to 3
- gain_mlp: bfloat16 [768], P(('row', 'col')), may hold values from 0.099609375 to 1.8984375
- bias_mlp: bfloat16 [768], P(('row', 'col')), may hold values from -3 to 3
- b_out: bfloat16 [768], P(('row', 'col')), may hold values from -3 to 3
- b_fc: bfloat16 [3072], P(('row', 'col')), may hold values from -3 to 3
- b_proj: bfloat16 [768], P(('row', 'col')), may hold values from -3 to 3
- w_loc: bfloat16 [12, 256], P(None, ('row', 'col')), may hold values from -0.375 to 0.375
- w_spread: bfloat16 [12, 256], P(None, ('row', 'col')), may hold values from -0.1875 to 0.1875
- past_states: bfloat16 [2, 16, 1024, 768], P(None, 'row', 'col'), may hold values from -6 to 6
- sticky_pos: int32 [2, 16, 512], P(None, 'row'), may hold values from 0 to 1023, as said below
- seq_lengths: int32 [2, 16], P(None, 'row'), may hold values from 256 to 1024, as said below
- d_out: bfloat16 [2, 16, 1024, 768], P(None, 'row', 'col'), may hold values from -6 to 6
Outputs:
- output: bfloat16 [2, 16, 1024, 768], P(None, 'row', 'col')
- grad_tokens: float32 [2, 16, 1024, 768], P(None, 'row', 'col')
- grad_qkv: float32 [768, 2304], P('row', 'col')
- output_weight_gradient: float32 [768, 768], P('row', 'col')
- grad_mem: float32 [768, 1536], P('row', 'col')
- grad_fc: float32 [768, 3072], P('row', 'col')
- grad_proj: float32 [3072, 768], P('row', 'col')
- grad_gain_attn: float32 [768], P(('row', 'col'))
- grad_bias_attn: float32 [768], P(('row', 'col'))
- grad_gain_mlp: float32 [768], P(('row', 'col'))
- grad_bias_mlp: float32 [768], P(('row', 'col'))
- grad_b_out: float32 [768], P(('row', 'col'))
- grad_b_fc: float32 [3072], P(('row', 'col'))
- grad_b_proj: float32 [768], P(('row', 'col'))
- grad_loc: float32 [12, 256], P(None, ('row', 'col'))
- grad_spread: float32 [12, 256], P(None, ('row', 'col'))
The draws below stay inside these ranges and needn't reach their ends.
Inputs may be any that keep to these rules, and one draw needn't show every extreme that they name: `seq_lengths`: for every sequence index, at least one micro-batch holds a sequence of all 1024 positions; some slot holds exactly 256. `sticky_pos`: each row is non-decreasing; half of its 512 entries are the evenly spaced positions floor(m * 1023 / 255), the others are sampled.
All inputs are finite; a program needn't handle non-finite values.
Results may differ from the reference program's by a relative error of at most 0.024.
Values may be sent and summed in bfloat16 or wider, within the bound.
No kernel may reach another device: no remote copies, remote signals or barrier semaphores. Data moves between devices by JAX's collectives and lax.ppermute only.
A program may use at most 256 MiB of HBM per device.

```python
import math
import jax
import jax.numpy as jnp
from jax import lax

D = 768
H = 12
DH = 64
FF = 3072
NB = 256
FIT_NODE_COUNT = 512
WINDOW = 512
MB = 2
SEQS = 16
SLOT = 1024


def draw_seq_lengths(key, part):
    key_base = jax.random.fold_in(key, 11)
    key_len = jax.random.fold_in(key_base, 1)
    key_full = jax.random.fold_in(key_base, 2)
    key_short = jax.random.fold_in(key_base, 3)
    drawn = jax.random.randint(key_len, (MB, SEQS), SLOT // 4, SLOT + 1)
    full_batch = jax.random.randint(key_full, (SEQS,), 0, MB)
    batch_ids = jnp.arange(MB, dtype=jnp.int32)[:, None]
    seq_ids = jnp.arange(SEQS, dtype=jnp.int32)[None, :]
    lengths = jnp.where(batch_ids == full_batch[None, :], SLOT, drawn)
    short_seq = jax.random.randint(key_short, (), 0, SEQS)
    short_batch = (full_batch[short_seq] + 1) % MB
    chosen = (batch_ids == short_batch) & (seq_ids == short_seq)
    return jnp.where(chosen, SLOT // 4, lengths).astype(jnp.int32)


def draw_sticky_pos(key, part):
    half_count = FIT_NODE_COUNT // 2
    grid_pos = jnp.arange(half_count, dtype=jnp.int32) * (SLOT - 1) // (half_count - 1)
    key_pos = jax.random.fold_in(key, 23)
    sampled = jax.random.randint(key_pos, (MB, SEQS, half_count), 0, SLOT)
    merged = jnp.concatenate([jnp.broadcast_to(grid_pos, (MB, SEQS, half_count)), sampled], axis=2)
    return jnp.sort(merged, axis=2).astype(jnp.int32)


def block_levels(stream_key, dims, cuts, least, top_value):
    level = 1.0
    for dim, blocks in cuts:
        steps = jax.random.uniform(jax.random.fold_in(jax.random.fold_in(stream_key, 6), dim), (blocks,), jnp.float32, least / len(cuts), top_value / len(cuts))
        level = level * jnp.repeat(jnp.exp(steps), dims[dim] // blocks).reshape((-1,) + (1,) * (len(dims) - 1 - dim))
    return level


def scatter_about(stream_key, extent, scale, limit, split=(), kind=jnp.bfloat16):
    entries = scale * jax.random.normal(stream_key, extent, jnp.float32)
    if split:
        entries = entries * block_levels(stream_key, extent, split, -0.22, 0.18)
    return jnp.clip(entries, -limit, limit).astype(kind)


def setup_inputs(seed: int = 0) -> dict:
    seeds = jax.random.split(jax.random.key(seed), 20)
    tokens = scatter_about(seeds[0], (MB, SEQS, SLOT, D), 1.0, 6.0, ((1, 16), (2, 2)))
    w_qkv = scatter_about(seeds[1], (D, 3 * D), D ** -0.5, 0.21875, ((0, 16), (1, 2)))
    w_out = scatter_about(seeds[2], (D, D), (D // 16) ** -0.5, 0.875, ((0, 16), (1, 2)))
    w_mem = scatter_about(seeds[3], (D, 2 * D), D ** -0.5, 0.21875, ((0, 16), (1, 2)))
    w_fc = scatter_about(seeds[4], (D, FF), D ** -0.5, 0.21875, ((0, 16), (1, 2)))
    w_proj = scatter_about(seeds[5], (FF, D), FF ** -0.5, 0.109375, ((0, 16), (1, 2)))
    gain_attn = jnp.clip(1.0 + 0.18 * jax.random.normal(seeds[6], (D,), jnp.float32), 0.099609375, 1.8984375).astype(jnp.bfloat16)
    bias_attn = scatter_about(seeds[7], (D,), 0.5, 3.0, ((0, 32),))
    gain_mlp = jnp.clip(1.0 + 0.18 * jax.random.normal(seeds[8], (D,), jnp.float32), 0.099609375, 1.8984375).astype(jnp.bfloat16)
    bias_mlp = scatter_about(seeds[9], (D,), 0.5, 3.0, ((0, 32),))
    b_out = scatter_about(seeds[10], (D,), 0.5, 3.0, ((0, 32),))
    b_fc = scatter_about(seeds[11], (FF,), 0.5, 3.0, ((0, 32),))
    b_proj = scatter_about(seeds[12], (D,), 0.5, 3.0, ((0, 32),))
    w_loc = scatter_about(seeds[13], (H, NB), 0.0625, 0.375, ((1, 32),))
    w_spread = scatter_about(seeds[14], (H, NB), 0.03125, 0.1875, ((1, 32),))
    past_states = scatter_about(seeds[15], (MB, SEQS, SLOT, D), 1.0, 6.0, ((1, 16), (2, 2)))
    sticky_pos = draw_sticky_pos(jax.random.fold_in(seeds[19], 71), 0)
    seq_lengths = draw_seq_lengths(jax.random.fold_in(seeds[19], 71), 0)
    d_out = scatter_about(seeds[18], (MB, SEQS, SLOT, D), 1.0, 6.0, ((1, 16), (2, 2)))
    return {"tokens": tokens, "w_qkv": w_qkv, "w_out": w_out, "w_mem": w_mem, "w_fc": w_fc, "w_proj": w_proj, "gain_attn": gain_attn, "bias_attn": bias_attn, "gain_mlp": gain_mlp, "bias_mlp": bias_mlp, "b_out": b_out, "b_fc": b_fc, "b_proj": b_proj, "w_loc": w_loc, "w_spread": w_spread, "past_states": past_states, "sticky_pos": sticky_pos, "seq_lengths": seq_lengths, "d_out": d_out}


eps = 1e-05
ridge = 0.5
var_scale = 0.01
masked = -1e+30
maximal_accuracy = lax.Precision.HIGHEST

@jax.custom_vjp
def low(v):
    return lax.optimization_barrier(v.astype(jnp.bfloat16)).astype(jnp.float32)

@jax.custom_vjp
def low_back(v):
    return v

def low_keep(v):
    return (low(v), None)

def low_pass(kept, grad):
    return (grad,)

def back_keep(v):
    return (v, None)

def back_low(kept, grad):
    return (low(grad),)
low.defvjp(low_keep, low_pass)
low_back.defvjp(back_keep, back_low)

def layer_norm(values, gain_vec, bias_vec):
    center = lax.optimization_barrier(jnp.mean(values, axis=-1, keepdims=True))
    offset = values - center
    variance = lax.optimization_barrier(jnp.mean(offset * offset, axis=-1, keepdims=True))
    return offset * lax.rsqrt(variance + eps) * gain_vec + bias_vec

def gelu_tanh(values):
    return jax.nn.gelu(values, approximate=True)

def basis_tables():
    radial_means = (jnp.arange(NB, dtype=jnp.float32) + 0.5) / NB
    fit_moments = (jnp.arange(FIT_NODE_COUNT, dtype=jnp.float32) + 0.5) / FIT_NODE_COUNT
    mean_shifts = fit_moments[None, :] - radial_means[:, None]
    design = jnp.exp(-0.5 * mean_shifts * mean_shifts * (NB * NB))
    normal_mat = jnp.dot(design, design.T, precision=maximal_accuracy) + ridge * jnp.eye(NB, dtype=jnp.float32)
    factor = jnp.linalg.cholesky(normal_mat)
    fit_table = jax.scipy.linalg.cho_solve((factor, True), design)
    return (fit_table, radial_means)

def memory_density(mem_scores, loc_weights, spread_weights, radial_means):
    basis_count = radial_means.shape[0]
    location = jax.nn.sigmoid(jnp.einsum('thj,hj->th', mem_scores, loc_weights, precision=maximal_accuracy))
    spread = var_scale * jax.nn.softplus(jnp.einsum('thj,hj->th', mem_scores, spread_weights, precision=maximal_accuracy)) + 1.0 / (basis_count * basis_count)
    mean_shifts = location[..., None] - radial_means
    spread = spread[..., None]
    return jnp.exp(-0.5 * mean_shifts * mean_shifts / spread) * lax.rsqrt(2.0 * math.pi * spread) / basis_count

def slot_forward(params, slot_x, slot_past, slot_sticky, slot_len, fit_table, radial_means):
    w_qkv, w_out, w_mem, w_fc, w_proj, gain_attn, bias_attn, gain_mlp, bias_mlp, b_out, b_fc, b_proj, w_loc, w_spread = params
    scale_qk = DH ** (-0.5)
    token_positions = jnp.arange(SLOT, dtype=jnp.int32)
    valid_row = (token_positions < slot_len).astype(jnp.float32)[:, None]
    normed1 = low(layer_norm(slot_x, gain_attn, bias_attn))
    qkv_low = low(low_back(jnp.dot(normed1, w_qkv, precision=maximal_accuracy)))
    queries = qkv_low[:, :D]
    blank_rows = jnp.zeros((WINDOW, 2 * D), jnp.float32)
    padded_kv = jnp.concatenate([blank_rows, qkv_low[:, D:]], axis=0)

    def attend_block(block_num):
        begin_row = block_num * WINDOW
        query_blk = lax.dynamic_slice_in_dim(queries, begin_row, WINDOW, 0).reshape(WINDOW, H, DH)
        kv_blk = lax.dynamic_slice_in_dim(padded_kv, begin_row, 2 * WINDOW, 0)
        key_blk = kv_blk[:, :D].reshape(2 * WINDOW, H, DH)
        value_blk = kv_blk[:, D:].reshape(2 * WINDOW, H, DH)
        query_pos = begin_row + jnp.arange(WINDOW, dtype=jnp.int32)
        key_pos = begin_row - WINDOW + jnp.arange(2 * WINDOW, dtype=jnp.int32)
        distance = query_pos[:, None] - key_pos[None, :]
        allowed = (distance >= 0) & (distance < WINDOW) & (key_pos[None, :] >= 0) & ((key_pos[None, :] < slot_len) | (distance == 0))
        scores = low_back(jnp.einsum('qhd,khd->hqk', query_blk, key_blk, precision=maximal_accuracy) * scale_qk)
        scores = jnp.where(allowed[None], scores, masked)
        expo_terms = jnp.exp(scores - lax.optimization_barrier(jnp.max(scores, axis=-1, keepdims=True)))
        prob_low = low(expo_terms / lax.optimization_barrier(jnp.sum(expo_terms, axis=-1, keepdims=True)))
        return jnp.einsum('hqk,khd->qhd', prob_low, value_blk, precision=maximal_accuracy).reshape(WINDOW, D)
    attended = lax.map(jax.checkpoint(attend_block), jnp.arange(SLOT // WINDOW, dtype=jnp.int32)).reshape(SLOT, D)
    memory_basis = low(jnp.dot(fit_table, slot_past[slot_sticky], precision=maximal_accuracy))
    mem_kv = low(low_back(jnp.dot(memory_basis, w_mem, precision=maximal_accuracy)))
    mem_keys = mem_kv[:, :D].reshape(NB, H, DH)
    mem_values = mem_kv[:, D:].reshape(NB, H, DH)
    query_heads = queries.reshape(SLOT, H, DH)
    mem_scores = low_back(jnp.einsum('thd,jhd->thj', query_heads, mem_keys, precision=maximal_accuracy) * scale_qk)
    density = low(memory_density(mem_scores, w_loc, w_spread, radial_means))
    recalled = jnp.einsum('thj,jhd->thd', density, mem_values, precision=maximal_accuracy).reshape(SLOT, D)
    context = low(low_back(attended + recalled))
    branch_attn = low_back(jnp.dot(context, w_out, precision=maximal_accuracy) + b_out)
    middle = slot_x + valid_row * branch_attn
    normed2 = low(layer_norm(middle, gain_mlp, bias_mlp))
    pre_act = low_back(jnp.dot(normed2, w_fc, precision=maximal_accuracy) + b_fc)
    hidden = low(gelu_tanh(pre_act))
    branch_mlp = low_back(jnp.dot(hidden, w_proj, precision=maximal_accuracy) + b_proj)
    return middle + valid_row * branch_mlp

def reference(tokens, w_qkv, w_out, w_mem, w_fc, w_proj, gain_attn, bias_attn, gain_mlp, bias_mlp, b_out, b_fc, b_proj, w_loc, w_spread, past_states, sticky_pos, seq_lengths, d_out):
    fit_table, radial_means = basis_tables()
    params = tuple((piece.astype(jnp.float32) for piece in (w_qkv, w_out, w_mem, w_fc, w_proj, gain_attn, bias_attn, gain_mlp, bias_mlp, b_out, b_fc, b_proj, w_loc, w_spread)))
    slots = MB * SEQS
    x_float = tokens.astype(jnp.float32).reshape(slots, SLOT, D)
    past_float = past_states.astype(jnp.float32).reshape(slots, SLOT, D)
    sticky_flat = sticky_pos.reshape(slots, FIT_NODE_COUNT).astype(jnp.int32)
    length_flat = seq_lengths.reshape(slots).astype(jnp.int32)

    def forward(x_in, param_in):

        def slot_step(carry, slot_item):
            slot_x, slot_past, slot_sticky, slot_len = slot_item
            result = jax.checkpoint(slot_forward)(param_in, slot_x, slot_past, slot_sticky, slot_len, fit_table, radial_means)
            return (carry, result)
        _, slot_outs = lax.scan(slot_step, jnp.int32(0), (x_in, past_float, sticky_flat, length_flat))
        return slot_outs
    slot_outs, pullback = jax.vjp(forward, x_float, params)
    valid_all = (jnp.arange(SLOT, dtype=jnp.int32)[None, :] < length_flat[:, None]).astype(jnp.float32)
    cotangent = d_out.astype(jnp.float32).reshape(slots, SLOT, D) * valid_all[..., None]
    grad_x, grads = pullback(cotangent)
    output = slot_outs.astype(jnp.bfloat16).reshape(MB, SEQS, SLOT, D)
    grad_x = grad_x.reshape(MB, SEQS, SLOT, D)
    return (output, grad_x, grads[0], grads[1], grads[2], grads[3], grads[4], grads[5], grads[6], grads[7], grads[8], grads[9], grads[10], grads[11], grads[12], grads[13])
```

```python
import functools
import math

import jax
import jax.numpy as jnp
import numpy as np
from jax import lax
from jax.experimental import pallas as pl
from jax.experimental.pallas import tpu as pltpu
from jax.sharding import PartitionSpec as P

WINDOW=512; TILE=256; masked=-1e30
var_scale=0.01
NT=(((1,),(1,)),((),()))
NN=(((1,),(0,)),((),()))

def dot_nt(a,b): return lax.dot_general(a,b,NT,preferred_element_type=jnp.float32)
def dot_nn(a,b): return lax.dot_general(a,b,NN,preferred_element_type=jnp.float32)

def split3(v):
    hi=v.astype(jnp.bfloat16); r=v-hi.astype(jnp.float32)
    mid=r.astype(jnp.bfloat16); lo=(r-mid.astype(jnp.float32)).astype(jnp.bfloat16)
    return hi,mid,lo

def lane_is_first(shape,half):
    return lax.broadcasted_iota(jnp.int32,shape,1)<half

def tile_biases(info_ref,first_key,has_far,has_mid):
    key=lax.broadcasted_iota(jnp.int32,(TILE,TILE),0)
    qry=lax.broadcasted_iota(jnp.int32,(TILE,TILE),1)
    tri=key<=qry
    length=info_ref[0]
    diag_pos=first_key+key
    far_pos=diag_pos-WINDOW
    near=jnp.where((diag_pos<length)|(key==qry),0.0,masked)
    far=jnp.where((far_pos>=0)&(far_pos<length),0.0,masked) if has_far else masked
    comb=jnp.where(tri,near,far)
    mid_pos=diag_pos-TILE
    mid=jnp.where((mid_pos>=0)&(mid_pos<length),0.0,masked)
    return comb,mid

def density_rows(wls,mk,half):
    vec=dot_nn(wls,mk)
    row=lax.broadcasted_iota(jnp.int32,vec.shape,0)
    lane=lax.broadcasted_iota(jnp.int32,vec.shape,1)
    return jnp.where((row%2==0)==(lane<half),vec,0.0)

def logits_of(vec,qb):
    hi,mid,lo=split3(vec)
    parts=dot_nt(jnp.concatenate([hi,mid,lo,lo],axis=0),qb)
    return (parts[16:24]+parts[8:16])+parts[0:8]

def spreads(logits,nb):
    location=1.0/(1.0+jnp.exp(-logits))
    soft=jnp.maximum(logits,0.0)+jnp.log1p(jnp.exp(-jnp.abs(logits)))
    spread=var_scale*soft+1.0/(nb*nb)
    return location,spread

def fwd_kernel(halo,half,info_ref,q_ref,k_ref,v_ref,mk_ref,mv_ref,wls_ref,ctx_ref,lse_ref,bias_ref):
    S=q_ref.shape[0]; nblk=S//TILE; nb=mk_ref.shape[0]; ht=halo//TILE
    @pl.when(pl.program_id(0)==0)
    def _():
        for i in range(nblk):
            comb,mid=tile_biases(info_ref,info_ref[1]+i*TILE,ht+i>=2,ht+i>=1)
            bias_ref[2*i]=comb; bias_ref[2*i+1]=mid
    tri=lax.broadcasted_iota(jnp.int32,(TILE,TILE),0)<=lax.broadcasted_iota(jnp.int32,(TILE,TILE),1)
    trib=jnp.where(tri,1.0,0.0).astype(jnp.bfloat16)
    lane=lax.broadcasted_iota(jnp.int32,(16,2*half),1)
    sides=[jnp.where(lane<half,1.0,0.0)[0:1].astype(jnp.bfloat16),jnp.where(lane<half,0.0,1.0)[0:1].astype(jnp.bfloat16)]
    centers=(lax.broadcasted_iota(jnp.int32,(nb,TILE),0).astype(jnp.float32)+0.5)/nb
    vec=density_rows(wls_ref[0],mk_ref[...],half)
    vT=v_ref[...].T
    mvT=mv_ref[...].T
    lse_ref[...]=jnp.zeros_like(lse_ref)
    for i in range(nblk):
        rows=slice(i*TILE,(i+1)*TILE)
        qb=q_ref[rows,:]*jnp.bfloat16(half**-0.5)
        d0=halo+i*TILE
        has_mid=ht+i>=1; has_far=ht+i>=2
        kd=k_ref[d0:d0+TILE,:]
        logits=logits_of(vec,qb)
        location,spread=spreads(logits,nb)
        nis=-0.5/spread
        norm=lax.rsqrt(2.0*math.pi*spread)*(1.0/nb)
        outs=[]
        for x in range(2):
            qx=qb*sides[x]
            vx=vT[x*half:(x+1)*half,:]
            sd=dot_nt(kd,qx)
            if has_far:
                sf=dot_nt(k_ref[d0-2*TILE:d0-TILE,:],qx)
                sc=jnp.where(tri,sd,sf)+bias_ref[2*i]
            else:
                sc=sd+bias_ref[2*i]
            top=jnp.max(sc,axis=0,keepdims=True)
            if has_mid:
                sm=dot_nt(k_ref[d0-TILE:d0,:],qx)+bias_ref[2*i+1]
                top=jnp.maximum(top,jnp.max(sm,axis=0,keepdims=True))
            ec=jnp.exp(sc-top)
            tot=jnp.sum(ec,axis=0,keepdims=True)
            ecl=ec.astype(jnp.bfloat16)
            if has_far:
                near=ecl*trib
                o=dot_nn(vx[:,d0:d0+TILE],near)+dot_nn(vx[:,d0-2*TILE:d0-TILE],ecl-near)
            else:
                o=dot_nn(vx[:,d0:d0+TILE],ecl)
            if has_mid:
                em=jnp.exp(sm-top)
                tot=tot+jnp.sum(em,axis=0,keepdims=True)
                o=o+dot_nn(vx[:,d0-TILE:d0],em.astype(jnp.bfloat16))
            lse_ref[0,x:x+1,rows]=top+jnp.log(tot)
            o=o*(1.0/tot)
            z=location[x:x+1]-centers
            e=jnp.exp(nis[2+x:3+x]*(z*z))
            r=dot_nn(mvT[x*half:(x+1)*half,:],e.astype(jnp.bfloat16))*norm[2+x:3+x]
            outs.append(o+r)
        ctx_ref[rows,:]=jnp.concatenate(outs,axis=0).T.astype(jnp.bfloat16)

def bwd_kernel(halo,half,info_ref,q_ref,k_ref,v_ref,mk_ref,mv_ref,wls_ref,lse_ref,do_ref,
               dq_ref,dk_ref,dv_ref,dmk_ref,dmv_ref,gls_ref,bias_ref,dk_acc,dv_acc):
    S=q_ref.shape[0]; nblk=S//TILE; nb=mk_ref.shape[0]; ht=halo//TILE
    @pl.when(pl.program_id(0)==0)
    def _():
        for i in range(nblk):
            comb,mid=tile_biases(info_ref,info_ref[1]+i*TILE,ht+i>=2,ht+i>=1)
            bias_ref[2*i]=comb; bias_ref[2*i+1]=mid
    tri=lax.broadcasted_iota(jnp.int32,(TILE,TILE),0)<=lax.broadcasted_iota(jnp.int32,(TILE,TILE),1)
    trib=jnp.where(tri,1.0,0.0).astype(jnp.bfloat16)
    lane=lax.broadcasted_iota(jnp.int32,(16,2*half),1)
    sides=[jnp.where(lane<half,1.0,0.0)[0:1].astype(jnp.bfloat16),jnp.where(lane<half,0.0,1.0)[0:1].astype(jnp.bfloat16)]
    centers=(lax.broadcasted_iota(jnp.int32,(nb,TILE),0).astype(jnp.float32)+0.5)/nb
    mk=mk_ref[...]; mv=mv_ref[...]
    vec=density_rows(wls_ref[0],mk,half)
    vecT=vec.T
    kT=k_ref[...].T
    dk_acc[...]=jnp.zeros_like(dk_acc); dv_acc[...]=jnp.zeros_like(dv_acc)
    dmv=jnp.zeros((nb,2*half),jnp.float32)
    dvec=jnp.zeros((8,2*half),jnp.float32)
    for i in range(nblk):
        rows=slice(i*TILE,(i+1)*TILE)
        qb=q_ref[rows,:]*jnp.bfloat16(half**-0.5)
        dob=do_ref[rows,:]
        d0=halo+i*TILE
        has_mid=ht+i>=1; has_far=ht+i>=2
        dg=slice(d0,d0+TILE); md=slice(d0-TILE,d0); fr=slice(d0-2*TILE,d0-TILE)
        logits=logits_of(vec,qb)
        location,spread=spreads(logits,nb)
        inv=1.0/spread
        nis=-0.5*inv
        norm=lax.rsqrt(2.0*math.pi*spread)*(1.0/nb)
        outs=[]; s0s=[]; s1s=[]; s2s=[]
        for x in range(2):
            qx=qb*sides[x]
            dox=dob*sides[x]
            kx=kT[x*half:(x+1)*half,:]
            lse=lse_ref[0,x:x+1,rows]
            sc=dot_nt(k_ref[dg,:],qx)
            dpc=dot_nt(v_ref[dg,:],dox)
            if has_far:
                sc=jnp.where(tri,sc,dot_nt(k_ref[fr,:],qx))
                dpc=jnp.where(tri,dpc,dot_nt(v_ref[fr,:],dox))
            pc=jnp.exp(sc+bias_ref[2*i]-lse)
            delta=jnp.sum(pc*dpc,axis=0,keepdims=True)
            if has_mid:
                sm=dot_nt(k_ref[md,:],qx)
                dpm=dot_nt(v_ref[md,:],dox)
                pm=jnp.exp(sm+bias_ref[2*i+1]-lse)
                delta=delta+jnp.sum(pm*dpm,axis=0,keepdims=True)
                dsm=(pm*(dpm-delta)).astype(jnp.bfloat16)
                dv_acc[md,:]+=dot_nn(pm.astype(jnp.bfloat16),dox)
                dk_acc[md,:]+=dot_nn(dsm,qx)
            dsc=(pc*(dpc-delta)).astype(jnp.bfloat16)
            pcl=pc.astype(jnp.bfloat16)
            if has_far:
                dsd=dsc*trib; dsf=dsc-dsd
                near=pcl*trib
                dv_acc[dg,:]+=dot_nn(near,dox)
                dv_acc[fr,:]+=dot_nn(pcl-near,dox)
                dk_acc[dg,:]+=dot_nn(dsd,qx)
                dk_acc[fr,:]+=dot_nn(dsf,qx)
                dq=dot_nn(kx[:,dg],dsd)+dot_nn(kx[:,fr],dsf)
            else:
                dv_acc[dg,:]+=dot_nn(pcl,dox)
                dk_acc[dg,:]+=dot_nn(dsc,qx)
                dq=dot_nn(kx[:,dg],dsc)
            if has_mid:
                dq=dq+dot_nn(kx[:,md],dsm)
            outs.append(dq)
            z=location[x:x+1]-centers
            e=jnp.exp(nis[2+x:3+x]*(z*z))
            g=dot_nt(mv,dox)*e
            gz=g*z
            s0s.append(jnp.sum(g,axis=0,keepdims=True))
            s1s.append(jnp.sum(gz,axis=0,keepdims=True))
            s2s.append(jnp.sum(gz*z,axis=0,keepdims=True))
            dmv=dmv+dot_nn((e*norm[2+x:3+x]).astype(jnp.bfloat16),dox)
        n2=norm[2:4]; i2=inv[2:4]
        s0=jnp.concatenate(s0s,axis=0); s1=jnp.concatenate(s1s,axis=0); s2=jnp.concatenate(s2s,axis=0)
        dloc=-(n2*i2)*s1
        dspr=n2*(0.5*i2)*(s2*i2-s0)
        l2=location[0:2]
        dll=dloc*l2*(1.0-l2)
        dsl=dspr*var_scale*location[2:4]
        dl=jnp.concatenate([dll,dsl,jnp.zeros((4,TILE),jnp.float32)],axis=0)
        hi=dl.astype(jnp.bfloat16); lo=(dl-hi.astype(jnp.float32)).astype(jnp.bfloat16)
        both=dot_nn(jnp.concatenate([hi,lo],axis=0),qb)
        dvec=dvec+(both[0:8]+both[8:16])
        for x in range(2):
            seg=slice(x*half,(x+1)*half)
            outs[x]=outs[x]+vecT[seg,x:x+1]*dl[x:x+1]+vecT[seg,2+x:3+x]*dl[2+x:3+x]
        dq_ref[rows,:]=(jnp.concatenate(outs,axis=0)*(half**-0.5)).T.astype(jnp.bfloat16)
    dk_ref[...]=dk_acc[...].astype(jnp.bfloat16)
    dv_ref[...]=dv_acc[...].astype(jnp.bfloat16)
    dmv_ref[...]=dmv.astype(jnp.bfloat16)
    row=lax.broadcasted_iota(jnp.int32,dvec.shape,0)
    lane=lax.broadcasted_iota(jnp.int32,dvec.shape,1)
    dvec=jnp.where((row%2==0)==(lane<half),dvec,0.0)
    hi=dvec.astype(jnp.bfloat16); lo=(dvec-hi.astype(jnp.float32)).astype(jnp.bfloat16)
    stack=jnp.concatenate([hi,lo],axis=0)
    gl=dot_nt(stack,mk)
    gls_ref[0]=gl[0:8]+gl[8:16]
    wT=wls_ref[0].astype(jnp.float32).T.astype(jnp.bfloat16)
    dmk_ref[...]=dot_nn(jnp.concatenate([wT,wT],axis=1),stack).astype(jnp.bfloat16)

def col_block(rows,width,first):
    return pl.BlockSpec((rows,width),lambda p,info: (0,first+p))

def attention_forward(info,qkv,kv,halo,mem_kv,wls,heads,vmem):
    S=qkv.shape[0]; pairs=heads//2; width=kv[0].shape[1]
    nb=mem_kv.shape[0]; feat=mem_kv.shape[1]//2; w=feat//pairs; half=w//2
    karr,koff,varr,voff=kv[0],kv[1],kv[2],kv[3]
    nblk=S//TILE
    spec=pltpu.PrefetchScalarGridSpec(num_scalar_prefetch=1,grid=(pairs,),
        in_specs=[col_block(S,w,0),col_block(halo+S,w,koff),col_block(halo+S,w,voff),col_block(nb,w,0),col_block(nb,w,pairs),
                  pl.BlockSpec((1,8,nb),lambda p,info:(p,0,0))],
        out_specs=[col_block(S,w,0),pl.BlockSpec((1,8,S),lambda p,info:(p,0,0))],
        scratch_shapes=[pltpu.VMEM((2*nblk,TILE,TILE),jnp.float32)])
    return pl.pallas_call(functools.partial(fwd_kernel,halo,half),grid_spec=spec,
        out_shape=[jax.ShapeDtypeStruct((S,feat),jnp.bfloat16),jax.ShapeDtypeStruct((pairs,8,S),jnp.float32)],
        compiler_params=pltpu.CompilerParams(vmem_limit_bytes=vmem,dimension_semantics=("arbitrary",)),
        cost_estimate=pl.CostEstimate(flops=24*S*S*feat//4,bytes_accessed=10*S*feat,transcendentals=heads*S*768),
        name="mix_forward")(info,qkv,karr,varr,mem_kv,mem_kv,wls)

def attention_backward(info,qkv,kv,halo,mem_kv,wls,lse,d_context,heads,vmem):
    S=qkv.shape[0]; pairs=heads//2
    nb=mem_kv.shape[0]; feat=mem_kv.shape[1]//2; w=feat//pairs; half=w//2
    karr,koff,varr,voff=kv
    nblk=S//TILE; bf=jnp.bfloat16
    spec=pltpu.PrefetchScalarGridSpec(num_scalar_prefetch=1,grid=(pairs,),
        in_specs=[col_block(S,w,0),col_block(halo+S,w,koff),col_block(halo+S,w,voff),col_block(nb,w,0),col_block(nb,w,pairs),
                  pl.BlockSpec((1,8,nb),lambda p,info:(p,0,0)),pl.BlockSpec((1,8,S),lambda p,info:(p,0,0)),col_block(S,w,0)],
        out_specs=[col_block(S,w,0),col_block(halo+S,w,0),col_block(halo+S,w,0),col_block(nb,w,0),col_block(nb,w,0),
                   pl.BlockSpec((1,8,nb),lambda p,info:(p,0,0))],
        scratch_shapes=[pltpu.VMEM((2*nblk,TILE,TILE),jnp.float32),pltpu.VMEM((halo+S,w),jnp.float32),pltpu.VMEM((halo+S,w),jnp.float32)])
    return pl.pallas_call(functools.partial(bwd_kernel,halo,half),grid_spec=spec,
        out_shape=[jax.ShapeDtypeStruct((S,feat),bf),jax.ShapeDtypeStruct((halo+S,feat),bf),jax.ShapeDtypeStruct((halo+S,feat),bf),
                   jax.ShapeDtypeStruct((nb,feat),bf),jax.ShapeDtypeStruct((nb,feat),bf),jax.ShapeDtypeStruct((pairs,8,nb),jnp.float32)],
        compiler_params=pltpu.CompilerParams(vmem_limit_bytes=vmem,dimension_semantics=("arbitrary",)),
        cost_estimate=pl.CostEstimate(flops=60*S*S*feat//4,bytes_accessed=20*S*feat,transcendentals=heads*S*768),
        name="mix_backward")(info,qkv,karr,varr,mem_kv,mem_kv,wls,lse,d_context)


eps=1e-5
TN=(((0,),(0,)),((),()))
def dot_tn(a,b): return lax.dot_general(a,b,TN,preferred_element_type=jnp.float32)

def norm_parts(v):
    center=jnp.mean(v,axis=-1,keepdims=True)
    off=v-center
    rstd=lax.rsqrt(jnp.mean(off*off,axis=-1,keepdims=True)+eps)
    return off*rstd,rstd

def norm_back(gd,xhat,rstd):
    return rstd*(gd-jnp.mean(gd,axis=-1,keepdims=True)-xhat*jnp.mean(gd*xhat,axis=-1,keepdims=True))

def whole(shape): return pl.BlockSpec(shape,lambda *a: (0,)*len(shape),pipeline_mode=pl.Buffered(1))

def qkv_kernel(x_ref,gain_ref,bias_ref,w_ref,n_ref,o_ref):
    xhat,_=norm_parts(x_ref[...].astype(jnp.float32))
    n=(xhat*gain_ref[...]+bias_ref[...]).astype(jnp.bfloat16)
    n_ref[...]=n
    o_ref[...]=dot_nn(n,w_ref[...]).astype(jnp.bfloat16)

def project_qkv(x,gain,bias,w,vmem,rows=256):
    S,D=x.shape; N=w.shape[1]
    return pl.pallas_call(qkv_kernel,grid=(S//rows,),
        in_specs=[pl.BlockSpec((rows,D),lambda i:(i,0)),whole((1,D)),whole((1,D)),whole((D,N))],
        out_specs=[pl.BlockSpec((rows,D),lambda i:(i,0)),pl.BlockSpec((rows,N),lambda i:(i,0))],
        out_shape=[jax.ShapeDtypeStruct((S,D),jnp.bfloat16),jax.ShapeDtypeStruct((S,N),jnp.bfloat16)],
        compiler_params=pltpu.CompilerParams(vmem_limit_bytes=vmem),
        cost_estimate=pl.CostEstimate(flops=2*S*D*N,bytes_accessed=2*(S*D*2+S*N+D*N),transcendentals=0),name="project_qkv")(x,gain,bias,w)

def mlp_kernel(steps,chunk,info_ref,c_ref,x_ref,g_ref,wo_ref,wf_ref,wp_ref,vec_ref,bf_ref,
               out_ref,dmid_ref,dctx_ref,go_ref,gf_ref,gp_ref,gv_ref,gb_ref,
               n_s,nT_s,dm_s,mid_s,acc_s,dn_s,hid_s,dp_s):
    f=pl.program_id(0); S,D=x_ref.shape
    length=info_ref[0]; base=info_ref[1]
    nchunk=S//chunk
    def valid_of(i):
        pos=base+i*chunk+lax.broadcasted_iota(jnp.int32,(chunk,1),0)
        return jnp.where(pos<length,1.0,0.0)
    @pl.when(f==0)
    def _():
        for i in range(nchunk):
            rs=slice(i*chunk,(i+1)*chunk)
            valid=valid_of(i)
            branch=dot_nn(c_ref[rs,:],wo_ref[...])+vec_ref[0:1]
            mid=x_ref[rs,:].astype(jnp.float32)+valid*branch
            mid_s[rs,:]=mid
            xhat,_=norm_parts(mid)
            n=(xhat*vec_ref[1:2]+vec_ref[2:3]).astype(jnp.bfloat16)
            n_s[rs,:]=n
            nT_s[:,rs]=n.T
            dm_s[rs,:]=(g_ref[rs,:].astype(jnp.float32)*valid).astype(jnp.bfloat16)
        acc_s[...]=jnp.zeros_like(acc_s); dn_s[...]=jnp.zeros_like(dn_s)
    wf=wf_ref[...]; wp=wp_ref[...]
    c0=math.sqrt(2.0/math.pi)
    gb=jnp.zeros((1,wf.shape[1]),jnp.float32)
    for i in range(nchunk):
        rs=slice(i*chunk,(i+1)*chunk)
        pre=dot_nn(n_s[rs,:],wf)+bf_ref[...]
        sq=pre*pre
        t=jnp.tanh(c0*pre*(1.0+0.044715*sq))
        hp=0.5*pre
        hid=hp+hp*t
        dgel=0.5+0.5*t+hp*(1.0-t*t)*(c0*(1.0+(3*0.044715)*sq))
        hidb=hid.astype(jnp.bfloat16)
        hid_s[rs,:]=hidb
        acc_s[rs,:]+=dot_nn(hidb,wp)
        dp=dot_nt(dm_s[rs,:],wp)*dgel
        dpb=dp.astype(jnp.bfloat16)
        dp_s[rs,:]=dpb
        gb=gb+jnp.sum(dpb.astype(jnp.float32),axis=0,keepdims=True)
        dn_s[rs,:]+=dot_nt(dpb,wf)
    gb_ref[...]=jnp.broadcast_to(gb,gb_ref.shape)
    gf_ref[...]=dot_nn(nT_s[...],dp_s[...]).astype(jnp.bfloat16)
    gp_ref[...]=dot_tn(hid_s[...],dm_s[...]).astype(jnp.bfloat16)
    @pl.when(f==steps-1)
    def _():
        gg=jnp.zeros((1,D),jnp.float32); gbi=gg; gbo=gg; gbp=gg
        for i in range(nchunk):
            rs=slice(i*chunk,(i+1)*chunk)
            valid=valid_of(i)
            mid=mid_s[rs,:]
            out_ref[rs,:]=(mid+valid*(acc_s[rs,:]+vec_ref[3:4])).astype(jnp.bfloat16)
            xhat,rstd=norm_parts(mid)
            dn=dn_s[rs,:]
            cot=dm_s[rs,:].astype(jnp.float32)
            dmid=cot+norm_back(dn*vec_ref[1:2],xhat,rstd)
            dmid_ref[rs,:]=dmid
            db=(valid*dmid).astype(jnp.bfloat16)
            dn_b=db.astype(jnp.float32)
            gg=gg+jnp.sum(dn*xhat,axis=0,keepdims=True)
            gbi=gbi+jnp.sum(dn,axis=0,keepdims=True)
            gbo=gbo+jnp.sum(dn_b,axis=0,keepdims=True)
            gbp=gbp+jnp.sum(cot,axis=0,keepdims=True)
            dctx_ref[rs,:]=dot_nt(db,wo_ref[...]).astype(jnp.bfloat16)
            n_s[rs,:]=db
        go_ref[...]=dot_tn(c_ref[...],n_s[...]).astype(jnp.bfloat16)
        gv_ref[...]=jnp.concatenate([gbo,gg,gbi,gbp,jnp.zeros((4,D),jnp.float32)],axis=0)

def mlp_block(info,context,x,d_out,w_out,w_fc,w_proj,vec,b_fc,vmem,fb=512,chunk=256):
    S,D=x.shape; FF=w_fc.shape[1]; steps=FF//fb; bf=jnp.bfloat16; f32=jnp.float32
    spec=pltpu.PrefetchScalarGridSpec(num_scalar_prefetch=1,grid=(steps,),
        in_specs=[whole((S,D)),whole((S,D)),whole((S,D)),whole((D,D)),pl.BlockSpec((D,fb),lambda f,i:(0,f)),pl.BlockSpec((fb,D),lambda f,i:(f,0)),
                  whole((8,D)),pl.BlockSpec((1,fb),lambda f,i:(0,f))],
        out_specs=[whole((S,D)),whole((S,D)),whole((S,D)),whole((D,D)),pl.BlockSpec((D,fb),lambda f,i:(0,f)),pl.BlockSpec((fb,D),lambda f,i:(f,0)),
                   whole((8,D)),pl.BlockSpec((8,fb),lambda f,i:(0,f))],
        scratch_shapes=[pltpu.VMEM((S,D),bf),pltpu.VMEM((D,S),bf),pltpu.VMEM((S,D),bf),pltpu.VMEM((S,D),f32),pltpu.VMEM((S,D),f32),pltpu.VMEM((S,D),f32),
                        pltpu.VMEM((S,fb),bf),pltpu.VMEM((S,fb),bf)])
    sd=jax.ShapeDtypeStruct
    return pl.pallas_call(functools.partial(mlp_kernel,steps,chunk),grid_spec=spec,
        out_shape=[sd((S,D),bf),sd((S,D),f32),sd((S,D),bf),sd((D,D),bf),sd((D,FF),bf),sd((FF,D),bf),sd((8,D),f32),sd((8,FF),f32)],
        compiler_params=pltpu.CompilerParams(vmem_limit_bytes=vmem,dimension_semantics=("arbitrary",)),
        cost_estimate=pl.CostEstimate(flops=12*S*D*FF+6*S*D*D,bytes_accessed=8*D*FF+20*S*D,transcendentals=S*FF),
        name="mlp_block")(info,context,x,d_out,w_out,w_fc,w_proj,vec,b_fc)

def wgrad_kernel(n_ref,d_ref,o_ref):
    o_ref[...]=dot_tn(n_ref[...],d_ref[0]).astype(jnp.bfloat16)

def qkv_weight_grad(n,d3,vmem,cb=384):
    S,D=n.shape; per=D//cb
    return pl.pallas_call(wgrad_kernel,grid=(3*per,),
        in_specs=[whole((S,D)),pl.BlockSpec((1,S,cb),lambda j:(j//per,0,j%per))],
        out_specs=pl.BlockSpec((D,cb),lambda j:(0,j)),
        out_shape=jax.ShapeDtypeStruct((D,3*D),jnp.bfloat16),
        compiler_params=pltpu.CompilerParams(vmem_limit_bytes=vmem),
        cost_estimate=pl.CostEstimate(flops=6*S*D*D,bytes_accessed=8*S*D+6*D*D,transcendentals=0),name="qkv_weight_grad")(n,d3)

def tokens_kernel(d_ref,w_ref,x_ref,dm_ref,gain_ref,extra_ref,o_ref,gv_ref):
    i=pl.program_id(0); D=x_ref.shape[1]
    dn=dot_nt(d_ref[0],w_ref[:,0:D])+dot_nt(d_ref[1],w_ref[:,D:2*D])+dot_nt(d_ref[2],w_ref[:,2*D:3*D])
    xhat,rstd=norm_parts(x_ref[...].astype(jnp.float32))
    o_ref[...]=dm_ref[...]+norm_back(dn*gain_ref[...],xhat,rstd)
    @pl.when(i==0)
    def _(): gv_ref[...]=jnp.zeros_like(gv_ref)
    gv_ref[0:1]+=jnp.sum(dn*xhat,axis=0,keepdims=True)
    gv_ref[1:2]+=jnp.sum(dn,axis=0,keepdims=True)

def token_grad(d3,w,x,d_middle,gain,vmem,rows=256):
    S,D=x.shape
    return pl.pallas_call(lambda d,w,x,m,g,o,v: tokens_kernel(d,w,x,m,g,None,o,v),grid=(S//rows,),
        in_specs=[pl.BlockSpec((3,rows,D),lambda i:(0,i,0)),whole((D,3*D)),pl.BlockSpec((rows,D),lambda i:(i,0)),pl.BlockSpec((rows,D),lambda i:(i,0)),whole((1,D))],
        out_specs=[pl.BlockSpec((rows,D),lambda i:(i,0)),pl.BlockSpec((8,D),lambda i:(0,0))],
        out_shape=[jax.ShapeDtypeStruct((S,D),jnp.float32),jax.ShapeDtypeStruct((8,D),jnp.float32)],
        compiler_params=pltpu.CompilerParams(vmem_limit_bytes=vmem),
        cost_estimate=pl.CostEstimate(flops=6*S*D*D,bytes_accessed=16*S*D+6*D*D,transcendentals=0),name="token_grad")(d3,w,x,d_middle,gain)


VMEM_BYTES = 58 << 20
FIT_NODE_COUNT = 512
ridge = 0.5


def fit_constant(nb):
    centers = (np.arange(nb, dtype=np.float64) + 0.5) / nb
    times = (np.arange(FIT_NODE_COUNT, dtype=np.float64) + 0.5) / FIT_NODE_COUNT
    design = np.exp(-0.5 * (times[None, :] - centers[:, None]) ** 2 * (nb * nb))
    table = np.linalg.solve(design @ design.T + ridge * np.eye(nb), design).astype(np.float32)
    hi = table.astype(jnp.bfloat16)
    lo = (table - hi.astype(np.float32)).astype(jnp.bfloat16)
    return np.concatenate([hi, lo], axis=0)


def bits_of(n):
    count = n.bit_length() - 1
    assert 1 << count == n
    return count


def swap(block, stage):
    axis, bit = stage
    n = lax.axis_size(axis)
    return lax.ppermute(block, axis, [(i, i ^ (1 << bit)) for i in range(n)])


def after(x, *deps):
    return lax.optimization_barrier((x,) + deps)[0]


def stage_orders():
    rows = bits_of(lax.axis_size("row"))
    cols = bits_of(lax.axis_size("col"))
    far = [("row", b) for b in range(rows - 1, 1, -1)]
    col = [("col", b) for b in range(cols - 1, -1, -1)]
    near = [("row", 1)] if rows > 1 else []
    return far + col + near + [("row", 0)], far + near + col + [("row", 0)]


def slot_offsets(order):
    table = []
    for slot in range(1 << len(order)):
        flips = {"row": 0, "col": 0}
        for i, (axis, bit) in enumerate(order):
            if slot >> i & 1:
                flips[axis] ^= 1 << bit
        table.append((flips["row"], flips["col"]))
    return table


def gather_steps(block, order, first=None):
    held = block[None]
    for stage in order[:-1]:
        held = jnp.concatenate([held, swap(held, stage)], axis=0)
    return held, swap(held, order[-1])


def place_bits():
    rows, cols = bits_of(lax.axis_size("row")), bits_of(lax.axis_size("col"))
    return [("row", b) for b in range(rows - 1, -1, -1)] + [("col", b) for b in range(cols - 1, -1, -1)]


def by_place(slots, order):
    seen = order[::-1]
    dims = [seen.index(p) for p in place_bits()]
    split = slots.reshape((2,) * len(order) + slots.shape[1:])
    tail = range(len(order), split.ndim)
    return split.transpose(dims + list(tail)).reshape(slots.shape)


def by_slot(blocks, order):
    places = place_bits()
    dims = [places.index(p) for p in order[::-1]]
    split = blocks.reshape((2,) * len(order) + blocks.shape[1:])
    tail = range(len(order), split.ndim)
    return split.transpose(dims + list(tail)).reshape(blocks.shape)


def flipped(blocks, row, col):
    places = place_bits()
    split = blocks.reshape((2,) * len(places) + blocks.shape[1:])
    for dim, (axis, bit) in enumerate(places):
        mine = (row if axis == "row" else col) >> bit & 1
        split = jnp.where(mine == 1, jnp.flip(split, dim), split)
    return split.reshape(blocks.shape)


def placed_spec(shape):
    return jax.ShapeDtypeStruct(shape, jnp.bfloat16)


def assemble_kernel(tables, cols, place_ref, *refs):
    pieces, out, sem = refs[:-2], refs[-2], refs[-1]
    copies = []
    for piece, (table, offset) in zip(pieces, tables):
        rows, width = piece.shape[1], piece.shape[2]
        for slot, (fr, fc) in enumerate(table):
            r = place_ref[0] ^ fr
            c = place_ref[1] ^ fc
            start = pl.multiple_of(c * cols + offset, 128)
            copies.append(
                pltpu.make_async_copy(
                    piece.at[slot],
                    out.at[pl.ds(pl.multiple_of(r * rows, 8), rows), pl.ds(start, width)],
                    sem.at[len(copies)],
                )
            )
    for copy in copies:
        copy.start()
    for copy in copies:
        copy.wait()


def assemble(place, parts, n_rows, n_cols):
    rows = parts[0][0].shape[1]
    cols = sum(p[0].shape[2] for p in parts)
    shape = (rows * n_rows, cols * n_cols)
    pieces, tables = [], []
    for held, came, order, offset in parts:
        table = slot_offsets(order)
        half = len(table) // 2
        pieces += [held, came]
        tables += [(table[:half], offset), (table[half:], offset)]
    if any(p.shape[2] % 128 for p in pieces) or rows % 8:
        full = []
        for held, came, order, offset in parts:
            slots = jnp.concatenate([held, came], axis=0)
            full.append(flipped(by_place(slots, order), place[0], place[1]))
        whole_cols = jnp.concatenate(full, axis=2).reshape(n_rows, n_cols, rows, cols)
        return whole_cols.transpose(0, 2, 1, 3).reshape(shape)
    count = sum(len(t) for t, _ in tables)
    return pl.pallas_call(
        functools.partial(assemble_kernel, tables, cols),
        grid_spec=pltpu.PrefetchScalarGridSpec(
            num_scalar_prefetch=1,
            grid=(1,),
            in_specs=[pl.BlockSpec(memory_space=pl.ANY)] * len(pieces),
            out_specs=pl.BlockSpec(shape, lambda i, place: (0, 0), pipeline_mode=pl.Buffered(1)),
            scratch_shapes=[pltpu.SemaphoreType.DMA((count,))],
        ),
        out_shape=jax.ShapeDtypeStruct(shape, jnp.bfloat16),
        compiler_params=pltpu.CompilerParams(vmem_limit_bytes=16 << 20),
        cost_estimate=pl.CostEstimate(flops=0, bytes_accessed=shape[0] * shape[1] * 4, transcendentals=0),
        name="assemble",
    )(place, *pieces)


def disperse_kernel(tables, rows, cols, place_ref, grad, *refs):
    outs, sem = refs[:-1], refs[-1]
    copies = []
    for out, (table, offset) in zip(outs, tables):
        width = out.shape[2]
        for slot, (fr, fc) in enumerate(table):
            r = place_ref[0] ^ fr
            c = place_ref[1] ^ fc
            start = pl.multiple_of(c * cols + offset, 128)
            copies.append(
                pltpu.make_async_copy(
                    grad.at[pl.ds(pl.multiple_of(r * rows, 8), rows), pl.ds(start, width)],
                    out.at[slot],
                    sem.at[len(copies)],
                )
            )
    for copy in copies:
        copy.start()
    for copy in copies:
        copy.wait()


def disperse(place, grad, n_rows, n_cols, parts):
    rows, cols = grad.shape[0] // n_rows, grad.shape[1] // n_cols
    outs, tables = [], []
    for offset, width, order in parts:
        table = slot_offsets(order)
        half = len(table) // 2
        outs += [placed_spec((half, rows, width))] * 2
        tables += [(table[:half], offset), (table[half:], offset)]
    if any(w % 128 for _, w, _ in parts) or rows % 8:
        cut = grad.reshape(n_rows, rows, n_cols, cols).transpose(0, 2, 1, 3)
        cut = flipped(cut.reshape(n_rows * n_cols, rows, cols), place[0], place[1])
        res = []
        for offset, width, order in parts:
            slots = by_slot(cut[:, :, offset : offset + width], order)
            res += [slots[: len(slots) // 2], slots[len(slots) // 2 :]]
        return res
    count = sum(len(t) for t, _ in tables)
    hbm = pl.BlockSpec(memory_space=pl.ANY)
    return pl.pallas_call(
        functools.partial(disperse_kernel, tables, rows, cols),
        grid_spec=pltpu.PrefetchScalarGridSpec(
            num_scalar_prefetch=1,
            grid=(1,),
            in_specs=[hbm],
            out_specs=[hbm] * len(outs),
            scratch_shapes=[pltpu.SemaphoreType.DMA((count,))],
        ),
        out_shape=outs,
        compiler_params=pltpu.CompilerParams(vmem_limit_bytes=16 << 20),
        cost_estimate=pl.CostEstimate(flops=0, bytes_accessed=grad.size * 4, transcendentals=0),
        name="disperse",
    )(place, grad)


def scatter_steps(keep, send, order):
    came = swap(send, order[-1])
    terms = [keep, came]
    for stage in order[-2::-1]:
        half = terms[0].shape[0] // 2
        total = sum(t[half:].astype(jnp.float32) for t in terms)
        came = swap(total.astype(jnp.bfloat16), stage)
        terms = [t[:half] for t in terms] + [came]
    return sum(t.astype(jnp.float32) for t in terms)[0]


def shards(
    tokens, w_qkv, w_out, w_mem, w_fc, w_proj, gain_attn, bias_attn, gain_mlp, bias_mlp, b_out, b_fc, b_proj,
    w_loc, w_spread, past_states, sticky_pos, seq_lengths, d_out,
):
    bf, f32 = jnp.bfloat16, jnp.float32
    n_rows, n_cols = lax.axis_size("row"), lax.axis_size("col")
    row, col = lax.axis_index("row"), lax.axis_index("col")
    place = jnp.stack([row, col]).astype(jnp.int32)
    batches, _, span, feat = tokens.shape
    heads, nb = w_loc.shape[0], w_loc.shape[1] * n_rows * n_cols
    hidden = w_fc.shape[1] * n_cols
    assert batches == 2 and n_cols % 2 == 0
    side = col % 2
    own, other = side, 1 - side
    first = (col - side) * span
    order_a, order_b = stage_orders()

    def pick(a, i):
        return lax.dynamic_index_in_dim(a, i, 0, keepdims=False)

    def to_chunk(mine, came):
        two = jnp.stack([mine, came])
        return jnp.where(side == 0, two, two[::-1]).reshape((2 * span,) + mine.shape[1:])

    def trade(a):
        return swap(a, ("col", 0))

    tokens, past, d_out = tokens[:, 0], past_states[:, 0], d_out[:, 0]
    sticky, lengths = sticky_pos[:, 0], seq_lengths[:, 0]
    length = pick(lengths, own)
    info = jnp.stack([length, first]).astype(jnp.int32)

    x = to_chunk(pick(tokens, own), trade(pick(tokens, other)))

    small = [gain_attn, bias_attn, gain_mlp, bias_mlp, b_out, b_proj, b_fc, w_loc.reshape(-1), w_spread.reshape(-1)]
    sizes = [s.shape[0] for s in small]
    used = sum(sizes)
    padded = -(-used // 1024) * 1024
    flat = jnp.concatenate(small + [jnp.zeros((padded - used,), bf)]).reshape(padded // 128, 128)
    held, came = gather_steps(flat, order_a)
    every = jnp.concatenate([held, came], axis=0)
    every = flipped(by_place(every, order_a), row, col).reshape(n_rows * n_cols, padded)
    vectors, at = [], 0
    for size in sizes:
        vectors.append(every[:, at : at + size])
        at += size
    gain1, bias1, gain2, bias2, bo, bp, bfc = [v.astype(f32).reshape(1, -1) for v in vectors[:7]]
    loc, spr = [
        v.reshape(n_rows * n_cols, heads, -1).transpose(1, 0, 2).reshape(heads // 2, 2, nb) for v in vectors[7:]
    ]
    wls = jnp.concatenate([loc, spr, jnp.zeros((heads // 2, 4, nb), bf)], axis=1)

    def cuts_of(width):
        if width % 128 or width < 1024:
            return [(0, width)]
        cut = (width // 128 + 1) // 2 * 128
        return [(0, cut), (cut, width - cut)]

    def gathered(shard, orders, cuts):
        parts = []
        for (offset, width), order in zip(cuts, orders):
            held, came = gather_steps(shard[:, offset : offset + width], order)
            parts.append((held, came, order, offset))
        return parts

    qkv_cuts = cuts_of(w_qkv.shape[1])
    parts = gathered(w_qkv, (order_a, order_b), qkv_cuts)
    wq = assemble(place, parts, n_rows, n_cols)
    gate = parts[0][0]
    wm = assemble(place, gathered(after(w_mem, gate), (order_b,), [(0, w_mem.shape[1])]), n_rows, n_cols)
    wo = assemble(place, gathered(after(w_out, gate), (order_a,), [(0, w_out.shape[1])]), n_rows, n_cols)
    wf = assemble(place, gathered(after(w_fc, gate), (order_a,), [(0, w_fc.shape[1])]), n_rows, n_cols)
    wp = assemble(place, gathered(after(w_proj, gate), (order_b,), [(0, w_proj.shape[1])]), n_rows, n_cols)

    fit = jnp.asarray(fit_constant(nb))
    here = col * span

    def basis_part(i):
        spots = pick(sticky, i) - here
        resident = (spots >= 0) & (spots < span)
        picked = jnp.take(pick(past, i), jnp.clip(spots, 0, span - 1), axis=0)
        parts = jnp.dot(fit * resident.astype(bf)[None, :], picked, preferred_element_type=f32)
        return parts[:nb] + parts[nb:]

    if n_cols == 2:
        basis = basis_part(own) + trade(basis_part(other).astype(bf)).astype(f32)
    else:
        both = lax.psum(jnp.stack([basis_part(i).astype(bf) for i in range(2)]), "col")
        basis = pick(both, own)
    basis = basis.astype(bf)

    normed1, qkv = project_qkv(x, gain1, bias1, wq, VMEM_BYTES)
    halo = 0 if n_cols == 2 else WINDOW
    pairs = heads // 2
    route = [(i, i + 2) for i in range(n_cols - 2)]
    back = [(i + 2, i) for i in range(n_cols - 2)]
    if halo:
        before = lax.ppermute(qkv[-halo:, feat:], "col", route)
        kvx = jnp.concatenate([before, qkv[:, feat:]], axis=0)
        kv = (kvx, 0, kvx, pairs)
    else:
        kv = (qkv, pairs, qkv, 2 * pairs)
    mem_kv = jnp.dot(basis, wm, preferred_element_type=f32).astype(bf)
    context, lse = attention_forward(info, qkv, kv, halo, mem_kv, wls, heads, VMEM_BYTES)

    gate = qkv
    g_chunk = to_chunk(pick(d_out, own), trade(after(pick(d_out, other), gate)))
    vec = jnp.concatenate([bo, gain2, bias2, bp, jnp.zeros((4, feat), f32)], axis=0)
    output, d_middle, d_context, g_out, g_fc, g_proj, g_vec, g_bfc = mlp_block(
        info, context, x, g_chunk, wo, wf, wp, vec, bfc, VMEM_BYTES, fb=min(512, hidden // n_cols)
    )

    def summed(grad, orders, cuts):
        parts = [(o, w, order) for (o, w), order in zip(cuts, orders)]
        cut = disperse(place, grad, n_rows, n_cols, parts)
        done = [scatter_steps(cut[2 * i], cut[2 * i + 1], p[2]) for i, p in enumerate(parts)]
        return jnp.concatenate(done, axis=1) if len(done) > 1 else done[0]

    grad_proj = summed(g_proj, (order_b,), [(0, w_proj.shape[1])])
    grad_fc = summed(g_fc, (order_a,), [(0, w_fc.shape[1])])
    grad_out = summed(g_out, (order_b,), [(0, w_out.shape[1])])

    def from_chunk(chunk):
        halves = chunk.reshape(2, span, feat)
        return pick(halves, own), pick(halves, other)

    def paired(kept, came):
        two = jnp.stack([kept, came])
        return jnp.where(side == 0, two, two[::-1])[:, None]

    kept, sent = from_chunk(output)
    outputs = paired(kept, trade(sent))

    d_q, d_k, d_v, d_mk, d_mv, g_ls = attention_backward(
        info, qkv, kv, halo, mem_kv, wls, lse, d_context, heads, VMEM_BYTES
    )
    if halo:
        d_kv = jnp.concatenate([d_k, d_v], axis=1)
        ret = lax.ppermute(d_kv[:halo], "col", back)
        d_kv = d_kv[halo:].astype(f32) + jnp.pad(ret.astype(f32), ((2 * span - halo, 0), (0, 0)))
        d_kv = d_kv.astype(bf)
        d_k, d_v = d_kv[:, :feat], d_kv[:, feat:]
    d3 = jnp.stack([d_q, d_k, d_v])
    g_qkv = qkv_weight_grad(normed1, d3, VMEM_BYTES)
    d_mem_kv = jnp.concatenate([d_mk, d_mv], axis=1)
    g_mem = lax.dot_general(basis, d_mem_kv, TN, preferred_element_type=f32).astype(bf)
    grad_qkv = summed(g_qkv, (order_a, order_b), qkv_cuts)
    grad_mem = summed(g_mem, (order_b,), [(0, w_mem.shape[1])])
    d_tok, g_vec1 = token_grad(d3, wq, x, d_middle, gain1, VMEM_BYTES)
    kept, sent = from_chunk(d_tok)
    grad_x = paired(kept, trade(sent.astype(bf)).astype(f32))

    devices = n_rows * n_cols
    pieces = [g_vec1[0], g_vec1[1], g_vec[1], g_vec[2], g_vec[0], g_vec[3], g_bfc[0]]
    pieces = [p.reshape(devices, -1) for p in pieces]
    for part in (g_ls[:, 0:2], g_ls[:, 2:4]):
        pieces.append(part.reshape(heads, devices, -1).transpose(1, 0, 2).reshape(devices, -1))
    pieces.append(jnp.zeros((devices, padded - used), f32))
    table = jnp.concatenate(pieces, axis=1).astype(bf).reshape(devices, padded // 128, 128)
    table = by_slot(flipped(table, row, col), order_a)
    mine = scatter_steps(table[: devices // 2], table[devices // 2 :], order_a).reshape(-1)
    small_grads, at = [], 0
    for size in sizes:
        small_grads.append(mine[at : at + size])
        at += size
    g_loc, g_spread = [g.reshape(heads, -1) for g in small_grads[7:]]
    g_gain1, g_bias1, g_gain2, g_bias2, g_bo, g_bp, g_bf = small_grads[:7]
    return (
        outputs, grad_x, grad_qkv, grad_out, grad_mem, grad_fc, grad_proj,
        g_gain1, g_bias1, g_gain2, g_bias2, g_bo, g_bf, g_bp, g_loc, g_spread,
    )


def solution(mesh):
    grid, both, tail = P("row", "col"), P(("row", "col")), P(None, ("row", "col"))
    act, rows = P(None, "row", "col", None), P(None, "row")
    return jax.shard_map(
        shards,
        mesh=mesh,
        in_specs=(act,) + (grid,) * 5 + (both,) * 7 + (tail,) * 2 + (act, P(None, "row", None), rows, act),
        out_specs=(act, act) + (grid,) * 5 + (both,) * 7 + (tail,) * 2,
        check_vma=False,
    )
```

```python
import functools
import math

import jax
import jax.numpy as jnp
import numpy as np
from jax import lax
from jax.experimental import pallas as pl
from jax.experimental.pallas import tpu as pltpu
from jax.sharding import PartitionSpec as P

WINDOW=512; TILE=256; masked=-1e30
var_scale=0.01
NT=(((1,),(1,)),((),()))
NN=(((1,),(0,)),((),()))

def dot_nt(a,b): return lax.dot_general(a,b,NT,preferred_element_type=jnp.float32)
def dot_nn(a,b): return lax.dot_general(a,b,NN,preferred_element_type=jnp.float32)

def split3(v):
    hi=v.astype(jnp.bfloat16); r=v-hi.astype(jnp.float32)
    mid=r.astype(jnp.bfloat16); lo=(r-mid.astype(jnp.float32)).astype(jnp.bfloat16)
    return hi,mid,lo

def lane_is_first(shape,half):
    return lax.broadcasted_iota(jnp.int32,shape,1)<half

def tile_biases(info_ref,first_key,has_far,has_mid):
    key=lax.broadcasted_iota(jnp.int32,(TILE,TILE),0)
    qry=lax.broadcasted_iota(jnp.int32,(TILE,TILE),1)
    tri=key<=qry
    length=info_ref[0]
    diag_pos=first_key+key
    far_pos=diag_pos-WINDOW
    near=jnp.where((diag_pos<length)|(key==qry),0.0,masked)
    far=jnp.where((far_pos>=0)&(far_pos<length),0.0,masked) if has_far else masked
    comb=jnp.where(tri,near,far)
    mid_pos=diag_pos-TILE
    mid=jnp.where((mid_pos>=0)&(mid_pos<length),0.0,masked)
    return comb,mid

def density_rows(wls,mk,half):
    vec=dot_nn(wls,mk)
    row=lax.broadcasted_iota(jnp.int32,vec.shape,0)
    lane=lax.broadcasted_iota(jnp.int32,vec.shape,1)
    return jnp.where((row%2==0)==(lane<half),vec,0.0)

def logits_of(vec,qb):
    hi,mid,lo=split3(vec)
    parts=dot_nt(jnp.concatenate([hi,mid,lo,lo],axis=0),qb)
    return (parts[16:24]+parts[8:16])+parts[0:8]

def spreads(logits,nb):
    location=1.0/(1.0+jnp.exp(-logits))
    soft=jnp.maximum(logits,0.0)+jnp.log1p(jnp.exp(-jnp.abs(logits)))
    spread=var_scale*soft+1.0/(nb*nb)
    return location,spread

def fwd_kernel(halo,half,info_ref,q_ref,k_ref,v_ref,mk_ref,mv_ref,wls_ref,ctx_ref,lse_ref,bias_ref):
    S=q_ref.shape[0]; nblk=S//TILE; nb=mk_ref.shape[0]; ht=halo//TILE
    @pl.when(pl.program_id(0)==0)
    def _():
        for i in range(nblk):
            comb,mid=tile_biases(info_ref,info_ref[1]+i*TILE,ht+i>=2,ht+i>=1)
            bias_ref[2*i]=comb; bias_ref[2*i+1]=mid
    tri=lax.broadcasted_iota(jnp.int32,(TILE,TILE),0)<=lax.broadcasted_iota(jnp.int32,(TILE,TILE),1)
    trib=jnp.where(tri,1.0,0.0).astype(jnp.bfloat16)
    lane=lax.broadcasted_iota(jnp.int32,(16,2*half),1)
    sides=[jnp.where(lane<half,1.0,0.0)[0:1].astype(jnp.bfloat16),jnp.where(lane<half,0.0,1.0)[0:1].astype(jnp.bfloat16)]
    centers=(lax.broadcasted_iota(jnp.int32,(nb,TILE),0).astype(jnp.float32)+0.5)/nb
    vec=density_rows(wls_ref[0],mk_ref[...],half)
    vT=v_ref[...].T
    mvT=mv_ref[...].T
    lse_ref[...]=jnp.zeros_like(lse_ref)
    for i in range(nblk):
        rows=slice(i*TILE,(i+1)*TILE)
        qb=q_ref[rows,:]*jnp.bfloat16(half**-0.5)
        d0=halo+i*TILE
        has_mid=ht+i>=1; has_far=ht+i>=2
        kd=k_ref[d0:d0+TILE,:]
        logits=logits_of(vec,qb)
        location,spread=spreads(logits,nb)
        nis=-0.5/spread
        norm=lax.rsqrt(2.0*math.pi*spread)*(1.0/nb)
        outs=[]
        for x in range(2):
            qx=qb*sides[x]
            vx=vT[x*half:(x+1)*half,:]
            sd=dot_nt(kd,qx)
            if has_far:
                sf=dot_nt(k_ref[d0-2*TILE:d0-TILE,:],qx)
                sc=jnp.where(tri,sd,sf)+bias_ref[2*i]
            else:
                sc=sd+bias_ref[2*i]
            top=jnp.max(sc,axis=0,keepdims=True)
            if has_mid:
                sm=dot_nt(k_ref[d0-TILE:d0,:],qx)+bias_ref[2*i+1]
                top=jnp.maximum(top,jnp.max(sm,axis=0,keepdims=True))
            ec=jnp.exp(sc-top)
            tot=jnp.sum(ec,axis=0,keepdims=True)
            ecl=ec.astype(jnp.bfloat16)
            if has_far:
                near=ecl*trib
                o=dot_nn(vx[:,d0:d0+TILE],near)+dot_nn(vx[:,d0-2*TILE:d0-TILE],ecl-near)
            else:
                o=dot_nn(vx[:,d0:d0+TILE],ecl)
            if has_mid:
                em=jnp.exp(sm-top)
                tot=tot+jnp.sum(em,axis=0,keepdims=True)
                o=o+dot_nn(vx[:,d0-TILE:d0],em.astype(jnp.bfloat16))
            lse_ref[0,x:x+1,rows]=top+jnp.log(tot)
            o=o*(1.0/tot)
            z=location[x:x+1]-centers
            e=jnp.exp(nis[2+x:3+x]*(z*z))
            r=dot_nn(mvT[x*half:(x+1)*half,:],e.astype(jnp.bfloat16))*norm[2+x:3+x]
            outs.append(o+r)
        ctx_ref[rows,:]=jnp.concatenate(outs,axis=0).T.astype(jnp.bfloat16)

def bwd_kernel(halo,half,info_ref,q_ref,k_ref,v_ref,mk_ref,mv_ref,wls_ref,lse_ref,do_ref,
               dq_ref,dk_ref,dv_ref,dmk_ref,dmv_ref,gls_ref,bias_ref,dk_acc,dv_acc):
    S=q_ref.shape[0]; nblk=S//TILE; nb=mk_ref.shape[0]; ht=halo//TILE
    @pl.when(pl.program_id(0)==0)
    def _():
        for i in range(nblk):
            comb,mid=tile_biases(info_ref,info_ref[1]+i*TILE,ht+i>=2,ht+i>=1)
            bias_ref[2*i]=comb; bias_ref[2*i+1]=mid
    tri=lax.broadcasted_iota(jnp.int32,(TILE,TILE),0)<=lax.broadcasted_iota(jnp.int32,(TILE,TILE),1)
    trib=jnp.where(tri,1.0,0.0).astype(jnp.bfloat16)
    lane=lax.broadcasted_iota(jnp.int32,(16,2*half),1)
    sides=[jnp.where(lane<half,1.0,0.0)[0:1].astype(jnp.bfloat16),jnp.where(lane<half,0.0,1.0)[0:1].astype(jnp.bfloat16)]
    centers=(lax.broadcasted_iota(jnp.int32,(nb,TILE),0).astype(jnp.float32)+0.5)/nb
    mk=mk_ref[...]; mv=mv_ref[...]
    vec=density_rows(wls_ref[0],mk,half)
    vecT=vec.T
    kT=k_ref[...].T
    dk_acc[...]=jnp.zeros_like(dk_acc); dv_acc[...]=jnp.zeros_like(dv_acc)
    dmv=jnp.zeros((nb,2*half),jnp.float32)
    dvec=jnp.zeros((8,2*half),jnp.float32)
    for i in range(nblk):
        rows=slice(i*TILE,(i+1)*TILE)
        qb=q_ref[rows,:]*jnp.bfloat16(half**-0.5)
        dob=do_ref[rows,:]
        d0=halo+i*TILE
        has_mid=ht+i>=1; has_far=ht+i>=2
        dg=slice(d0,d0+TILE); md=slice(d0-TILE,d0); fr=slice(d0-2*TILE,d0-TILE)
        logits=logits_of(vec,qb)
        location,spread=spreads(logits,nb)
        inv=1.0/spread
        nis=-0.5*inv
        norm=lax.rsqrt(2.0*math.pi*spread)*(1.0/nb)
        outs=[]; s0s=[]; s1s=[]; s2s=[]
        for x in range(2):
            qx=qb*sides[x]
            dox=dob*sides[x]
            kx=kT[x*half:(x+1)*half,:]
            lse=lse_ref[0,x:x+1,rows]
            sc=dot_nt(k_ref[dg,:],qx)
            dpc=dot_nt(v_ref[dg,:],dox)
            if has_far:
                sc=jnp.where(tri,sc,dot_nt(k_ref[fr,:],qx))
                dpc=jnp.where(tri,dpc,dot_nt(v_ref[fr,:],dox))
            pc=jnp.exp(sc+bias_ref[2*i]-lse)
            delta=jnp.sum(pc*dpc,axis=0,keepdims=True)
            if has_mid:
                sm=dot_nt(k_ref[md,:],qx)
                dpm=dot_nt(v_ref[md,:],dox)
                pm=jnp.exp(sm+bias_ref[2*i+1]-lse)
                delta=delta+jnp.sum(pm*dpm,axis=0,keepdims=True)
                dsm=(pm*(dpm-delta)).astype(jnp.bfloat16)
                dv_acc[md,:]+=dot_nn(pm.astype(jnp.bfloat16),dox)
                dk_acc[md,:]+=dot_nn(dsm,qx)
            dsc=(pc*(dpc-delta)).astype(jnp.bfloat16)
            pcl=pc.astype(jnp.bfloat16)
            if has_far:
                dsd=dsc*trib; dsf=dsc-dsd
                near=pcl*trib
                dv_acc[dg,:]+=dot_nn(near,dox)
                dv_acc[fr,:]+=dot_nn(pcl-near,dox)
                dk_acc[dg,:]+=dot_nn(dsd,qx)
                dk_acc[fr,:]+=dot_nn(dsf,qx)
                dq=dot_nn(kx[:,dg],dsd)+dot_nn(kx[:,fr],dsf)
            else:
                dv_acc[dg,:]+=dot_nn(pcl,dox)
                dk_acc[dg,:]+=dot_nn(dsc,qx)
                dq=dot_nn(kx[:,dg],dsc)
            if has_mid:
                dq=dq+dot_nn(kx[:,md],dsm)
            outs.append(dq)
            z=location[x:x+1]-centers
            e=jnp.exp(nis[2+x:3+x]*(z*z))
            g=dot_nt(mv,dox)*e
            gz=g*z
            s0s.append(jnp.sum(g,axis=0,keepdims=True))
            s1s.append(jnp.sum(gz,axis=0,keepdims=True))
            s2s.append(jnp.sum(gz*z,axis=0,keepdims=True))
            dmv=dmv+dot_nn((e*norm[2+x:3+x]).astype(jnp.bfloat16),dox)
        n2=norm[2:4]; i2=inv[2:4]
        s0=jnp.concatenate(s0s,axis=0); s1=jnp.concatenate(s1s,axis=0); s2=jnp.concatenate(s2s,axis=0)
        dloc=-(n2*i2)*s1
        dspr=n2*(0.5*i2)*(s2*i2-s0)
        l2=location[0:2]
        dll=dloc*l2*(1.0-l2)
        dsl=dspr*var_scale*location[2:4]
        dl=jnp.concatenate([dll,dsl,jnp.zeros((4,TILE),jnp.float32)],axis=0)
        hi=dl.astype(jnp.bfloat16); lo=(dl-hi.astype(jnp.float32)).astype(jnp.bfloat16)
        both=dot_nn(jnp.concatenate([hi,lo],axis=0),qb)
        dvec=dvec+(both[0:8]+both[8:16])
        for x in range(2):
            seg=slice(x*half,(x+1)*half)
            outs[x]=outs[x]+vecT[seg,x:x+1]*dl[x:x+1]+vecT[seg,2+x:3+x]*dl[2+x:3+x]
        dq_ref[rows,:]=(jnp.concatenate(outs,axis=0)*(half**-0.5)).T.astype(jnp.bfloat16)
    dk_ref[...]=dk_acc[...].astype(jnp.bfloat16)
    dv_ref[...]=dv_acc[...].astype(jnp.bfloat16)
    dmv_ref[...]=dmv.astype(jnp.bfloat16)
    row=lax.broadcasted_iota(jnp.int32,dvec.shape,0)
    lane=lax.broadcasted_iota(jnp.int32,dvec.shape,1)
    dvec=jnp.where((row%2==0)==(lane<half),dvec,0.0)
    hi=dvec.astype(jnp.bfloat16); lo=(dvec-hi.astype(jnp.float32)).astype(jnp.bfloat16)
    stack=jnp.concatenate([hi,lo],axis=0)
    gl=dot_nt(stack,mk)
    gls_ref[0]=gl[0:8]+gl[8:16]
    wT=wls_ref[0].astype(jnp.float32).T.astype(jnp.bfloat16)
    dmk_ref[...]=dot_nn(jnp.concatenate([wT,wT],axis=1),stack).astype(jnp.bfloat16)

def col_block(rows,width,first,stride=1):
    return pl.BlockSpec((rows,width),lambda p,info: (0,first+stride*p))

def attention_forward(info,qkv,kv,halo,mem_kv,wls,heads,vmem):
    S=qkv.shape[0]; pairs=heads//2; width=kv[0].shape[1]
    nb=mem_kv.shape[0]; feat=mem_kv.shape[1]//2; w=feat//pairs; half=w//2
    karr,koff,varr,voff=kv[0],kv[1],kv[2],kv[3]
    nblk=S//TILE
    spec=pltpu.PrefetchScalarGridSpec(num_scalar_prefetch=1,grid=(pairs,),
        in_specs=[col_block(S,w,0),col_block(halo+S,w,koff),col_block(halo+S,w,voff),col_block(nb,w,0),col_block(nb,w,pairs),
                  pl.BlockSpec((1,8,nb),lambda p,info:(p,0,0))],
        out_specs=[col_block(S,w,0),pl.BlockSpec((1,8,S),lambda p,info:(p,0,0))],
        scratch_shapes=[pltpu.VMEM((2*nblk,TILE,TILE),jnp.float32)])
    return pl.pallas_call(functools.partial(fwd_kernel,halo,half),grid_spec=spec,
        out_shape=[jax.ShapeDtypeStruct((S,feat),jnp.bfloat16),jax.ShapeDtypeStruct((pairs,8,S),jnp.float32)],
        compiler_params=pltpu.CompilerParams(vmem_limit_bytes=vmem,dimension_semantics=("arbitrary",)),
        cost_estimate=pl.CostEstimate(flops=24*S*S*feat//4,bytes_accessed=10*S*feat,transcendentals=heads*S*768),
        name="mix_forward")(info,qkv,karr,varr,mem_kv,mem_kv,wls)

def attention_backward(info,qkv,kv,halo,mem_kv,wls,lse,d_context,heads,vmem,begin,count,stride):
    S=qkv.shape[0]; pairs=heads//2
    nb=mem_kv.shape[0]; feat=mem_kv.shape[1]//2; w=feat//pairs; half=w//2
    karr,koff,varr,voff=kv
    nblk=S//TILE; bf=jnp.bfloat16
    spec=pltpu.PrefetchScalarGridSpec(num_scalar_prefetch=1,grid=(count,),
        in_specs=[col_block(S,w,begin,stride),col_block(halo+S,w,koff+begin,stride),col_block(halo+S,w,voff+begin,stride),
                  col_block(nb,w,begin,stride),col_block(nb,w,pairs+begin,stride),pl.BlockSpec((1,8,nb),lambda p,info:(begin+stride*p,0,0)),
                  pl.BlockSpec((1,8,S),lambda p,info:(begin+stride*p,0,0)),col_block(S,w,begin,stride)],
        out_specs=[col_block(S,w,0),col_block(halo+S,w,0),col_block(halo+S,w,0),col_block(nb,w,0),col_block(nb,w,0),
                   pl.BlockSpec((1,8,nb),lambda p,info:(p,0,0))],
        scratch_shapes=[pltpu.VMEM((2*nblk,TILE,TILE),jnp.float32),pltpu.VMEM((halo+S,w),jnp.float32),pltpu.VMEM((halo+S,w),jnp.float32)])
    part=count*w
    return pl.pallas_call(functools.partial(bwd_kernel,halo,half),grid_spec=spec,
        out_shape=[jax.ShapeDtypeStruct((S,part),bf),jax.ShapeDtypeStruct((halo+S,part),bf),jax.ShapeDtypeStruct((halo+S,part),bf),
                   jax.ShapeDtypeStruct((nb,part),bf),jax.ShapeDtypeStruct((nb,part),bf),jax.ShapeDtypeStruct((count,8,nb),jnp.float32)],
        compiler_params=pltpu.CompilerParams(vmem_limit_bytes=vmem,dimension_semantics=("arbitrary",)),
        cost_estimate=pl.CostEstimate(flops=30*S*S*part,bytes_accessed=20*S*part,transcendentals=2*count*S*768),
        name="mix_backward")(info,qkv,karr,varr,mem_kv,mem_kv,wls,lse,d_context)


eps=1e-5
TN=(((0,),(0,)),((),()))
def dot_tn(a,b): return lax.dot_general(a,b,TN,preferred_element_type=jnp.float32)

def norm_parts(v):
    center=jnp.mean(v,axis=-1,keepdims=True)
    off=v-center
    rstd=lax.rsqrt(jnp.mean(off*off,axis=-1,keepdims=True)+eps)
    return off*rstd,rstd

def norm_back(gd,xhat,rstd):
    return rstd*(gd-jnp.mean(gd,axis=-1,keepdims=True)-xhat*jnp.mean(gd*xhat,axis=-1,keepdims=True))

def whole(shape): return pl.BlockSpec(shape,lambda *a: (0,)*len(shape),pipeline_mode=pl.Buffered(1))

def shard_copies(loads, pieces, targets, sem, row, col, which):
    for n, (src, dst, fr, fc, rows, cols, slot, at, column, width) in enumerate(loads):
        if dst not in which:
            continue
        if rows is None:
            yield pltpu.make_async_copy(pieces[src], targets[dst], sem.at[n])
            continue
        r0 = pl.multiple_of((row ^ fr) * rows, 16)
        c0 = pl.multiple_of((col ^ fc) * cols + column, 128)
        yield pltpu.make_async_copy(
            pieces[src].at[slot, :, pl.ds(at, width)], targets[dst].at[pl.ds(r0, rows), pl.ds(c0, width)], sem.at[n]
        )


def qkv_kernel(loads, pairs, info_ref, x_ref, vec_ref, own_ref, came_ref, *refs):
    count = max(load[0] for load in loads) + 1
    pieces, refs = refs[:count], refs[count:]
    nT_ref, o_ref, mem_ref, bT_ref, wq_ref, wq_s, wm_s, in_sem, out_sem = refs
    i = pl.program_id(0)
    D = wq_s.shape[0]
    w, half = D // pairs, pairs // 2
    outs = []
    for n in range(3 * pairs):
        kind, p, j = n // pairs, n % pairs // 2, n % 2
        at = kind * D + (j * half + p) * w
        copy = pltpu.make_async_copy(wq_s.at[:, at : at + w], wq_ref.at[:, n * w : (n + 1) * w], out_sem.at[n])
        outs.append(copy)

    @pl.when(i == 0)
    def _():
        for begin in (True, False):
            for copy in shard_copies(loads, pieces, (wq_s, wm_s), in_sem, info_ref[2], info_ref[3], (0, 1)):
                copy.start() if begin else copy.wait()
        for out in outs:
            out.start()
        basis = (own_ref[...] + came_ref[...].astype(jnp.float32)).astype(jnp.bfloat16)
        bT_ref[...] = basis.T
        mem_ref[...] = dot_nn(basis, wm_s[...]).astype(jnp.bfloat16)

    xhat, _ = norm_parts(x_ref[...].astype(jnp.float32))
    n = (xhat * vec_ref[0:1] + vec_ref[1:2]).astype(jnp.bfloat16)
    nT_ref[...] = n.T
    o_ref[...] = dot_nn(n, wq_s[...]).astype(jnp.bfloat16)

    @pl.when(i == pl.num_programs(0) - 1)
    def _():
        for out in outs:
            out.wait()


def project_qkv(info, x, vec, own_basis, came_basis, pieces, loads, pairs, vmem, rows=256):
    S, D = x.shape
    nb = own_basis.shape[0]
    bf, sd = jnp.bfloat16, jax.ShapeDtypeStruct
    hbm = pl.BlockSpec(memory_space=pl.ANY)
    return pl.pallas_call(
        functools.partial(qkv_kernel, loads, pairs),
        grid_spec=pltpu.PrefetchScalarGridSpec(
            num_scalar_prefetch=1,
            grid=(S // rows,),
            in_specs=[pl.BlockSpec((rows, D), lambda i, info: (i, 0)), whole((8, D)), whole((nb, D)), whole((nb, D))]
            + [hbm] * len(pieces),
            out_specs=[
                pl.BlockSpec((D, rows), lambda i, info: (0, i)), pl.BlockSpec((rows, 3 * D), lambda i, info: (i, 0)),
                whole((nb, 2 * D)), whole((D, nb)), hbm,
            ],
            scratch_shapes=[
                pltpu.VMEM((D, 3 * D), bf), pltpu.VMEM((D, 2 * D), bf),
                pltpu.SemaphoreType.DMA((len(loads),)), pltpu.SemaphoreType.DMA((3 * pairs,)),
            ],
        ),
        out_shape=[sd((D, S), bf), sd((S, 3 * D), bf), sd((nb, 2 * D), bf), sd((D, nb), bf), sd((D, 3 * D), bf)],
        compiler_params=pltpu.CompilerParams(vmem_limit_bytes=vmem),
        cost_estimate=pl.CostEstimate(
            flops=6 * S * D * D + 4 * nb * D * D, bytes_accessed=10 * S * D + 16 * D * D, transcendentals=0
        ),
        name="project_qkv",
    )(info, x, vec, own_basis, came_basis, *pieces)


def row_slot(fr, order):
    return sum(((fr >> bit) & 1) << i for i, (axis, bit) in enumerate(order[:-1]) if axis == "row")


def col_slot(fc, order):
    return sum(((fc >> bit) & 1) << i for i, (axis, bit) in enumerate(order[:-1]) if axis == "col")


def mlp_kernel(steps, chunk, loads, cut, info_ref, c_ref, x_ref, g_ref, vec_ref, bf_ref, *refs):
    count = max(load[0] for load in loads) + 1
    pieces, refs = refs[:count], refs[count:]
    out_ref, dmid_ref, dctx_ref, gv_ref, gb_ref = refs[:5]
    made = 3 if cut is None else 4
    grads, refs = refs[5 : 5 + made], refs[5 + made :]
    n_s, nT_s, dm_s, mid_s, acc_s, dn_s, hid_s, dp_s, wf_s, wo_s, wp_s, go_s, gf_s, gp_s, in_sem, out_sem, go_sem = refs
    f = pl.program_id(0)
    S, D = x_ref.shape
    fb = gf_s.shape[2]
    length, base, row, col = info_ref[0], info_ref[1], info_ref[2], info_ref[3]
    nchunk = S // chunk
    buf = f % 2

    def valid_of(i):
        pos = base + i * chunk + lax.broadcasted_iota(jnp.int32, (chunk, 1), 0)
        return jnp.where(pos < length, 1.0, 0.0)

    def load_copies(which):
        return shard_copies(loads, pieces, (wf_s, wo_s, wp_s), in_sem, row, col, which)

    def block_copies(begin, buf=buf):
        if cut is None:
            copies = [
                pltpu.make_async_copy(gf_s.at[buf], grads[0].at[:, pl.ds(pl.multiple_of(f * fb, 128), fb)], out_sem.at[buf, 0]),
                pltpu.make_async_copy(gp_s.at[buf], grads[2].at[pl.ds(pl.multiple_of(f * fb, 16), fb), :], out_sem.at[buf, 1]),
            ]
            for copy in copies:
                copy.start() if begin else copy.wait()
            return
        n_rows, n_cols, order2, order3 = cut
        rows2, rows3 = D // n_rows, fb * steps // n_rows
        cols2, cols3 = fb * steps // n_cols, D // n_cols
        per = cols2 // fb
        c = f // per
        at = pl.multiple_of((f % per) * fb, 128)
        for fr in range(n_rows):
            slot = row_slot(fr, order2) + col_slot(c ^ col, order2)
            src = gf_s.at[buf, pl.ds(pl.multiple_of((row ^ fr) * rows2, 16), rows2), :]
            copy = pltpu.make_async_copy(src, grads[fr & 1].at[slot, :, pl.ds(at, fb)], out_sem.at[buf, fr])
            copy.start() if begin else copy.wait()
        n = n_rows
        for i in range(fb // rows3):
            rel = (f * (fb // rows3) + i) ^ row
            for c in range(n_cols):
                slot = row_slot(rel, order3) + col_slot(c ^ col, order3)
                src = gp_s.at[buf, i * rows3 : (i + 1) * rows3, c * cols3 : (c + 1) * cols3]
                if begin:
                    for side in range(2):

                        @pl.when(rel & 1 == side)
                        def _():
                            pltpu.make_async_copy(src, grads[2 + side].at[slot], out_sem.at[buf, n]).start()
                else:
                    pltpu.make_async_copy(src, grads[2].at[0], out_sem.at[buf, n]).wait()
                n += 1

    @pl.when(f == 0)
    def _():
        for copy in load_copies((1, 0, 2)):
            copy.start()
        for i in range(nchunk):
            rs = slice(i * chunk, (i + 1) * chunk)
            dm_s[rs, :] = (g_ref[rs, :].astype(jnp.float32) * valid_of(i)).astype(jnp.bfloat16)
        acc_s[...] = jnp.zeros_like(acc_s)
        dn_s[...] = jnp.zeros_like(dn_s)
        for copy in load_copies((1,)):
            copy.wait()
        for i in range(nchunk):
            rs = slice(i * chunk, (i + 1) * chunk)
            branch = dot_nn(c_ref[rs, :], wo_s[...]) + vec_ref[0:1]
            mid = x_ref[rs, :].astype(jnp.float32) + valid_of(i) * branch
            mid_s[rs, :] = mid
            xhat, _ = norm_parts(mid)
            n = (xhat * vec_ref[1:2] + vec_ref[2:3]).astype(jnp.bfloat16)
            n_s[rs, :] = n
            nT_s[:, rs] = n.T
        for copy in load_copies((0, 2)):
            copy.wait()

    @pl.when(f >= 2)
    def _():
        block_copies(False)

    cs = pl.ds(pl.multiple_of(f * fb, 128), fb)
    wf = wf_s[:, cs]
    wp = wp_s[cs, :]
    c0 = math.sqrt(2.0 / math.pi)
    gb = jnp.zeros((1, fb), jnp.float32)
    for i in range(nchunk):
        rs = slice(i * chunk, (i + 1) * chunk)
        pre = dot_nn(n_s[rs, :], wf) + bf_ref[...]
        sq = pre * pre
        t = jnp.tanh(c0 * pre * (1.0 + 0.044715 * sq))
        hp = 0.5 * pre
        hid = hp + hp * t
        dgel = 0.5 + 0.5 * t + hp * (1.0 - t * t) * (c0 * (1.0 + (3 * 0.044715) * sq))
        hidb = hid.astype(jnp.bfloat16)
        hid_s[rs, :] = hidb
        acc_s[rs, :] += dot_nn(hidb, wp)
        dpb = (dot_nt(dm_s[rs, :], wp) * dgel).astype(jnp.bfloat16)
        dp_s[rs, :] = dpb
        gb = gb + jnp.sum(dpb.astype(jnp.float32), axis=0, keepdims=True)
        dn_s[rs, :] += dot_nt(dpb, wf)
    gb_ref[...] = jnp.broadcast_to(gb, gb_ref.shape)
    gf_s[buf] = dot_nn(nT_s[...], dp_s[...]).astype(jnp.bfloat16)
    gp_s[buf] = dot_tn(hid_s[...], dm_s[...]).astype(jnp.bfloat16)
    block_copies(True)

    @pl.when(f == steps - 1)
    def _():
        gg = jnp.zeros((1, D), jnp.float32)
        gbi, gbo, gbp = gg, gg, gg
        for i in range(nchunk):
            rs = slice(i * chunk, (i + 1) * chunk)
            valid = valid_of(i)
            mid = mid_s[rs, :]
            out_ref[rs, :] = (mid + valid * (acc_s[rs, :] + vec_ref[3:4])).astype(jnp.bfloat16)
            xhat, rstd = norm_parts(mid)
            dn = dn_s[rs, :]
            cot = dm_s[rs, :].astype(jnp.float32)
            dmid = cot + norm_back(dn * vec_ref[1:2], xhat, rstd)
            dmid_ref[rs, :] = dmid
            db = (valid * dmid).astype(jnp.bfloat16)
            gg = gg + jnp.sum(dn * xhat, axis=0, keepdims=True)
            gbi = gbi + jnp.sum(dn, axis=0, keepdims=True)
            gbo = gbo + jnp.sum(db.astype(jnp.float32), axis=0, keepdims=True)
            gbp = gbp + jnp.sum(cot, axis=0, keepdims=True)
            n_s[rs, :] = db
        go_s[...] = dot_tn(c_ref[...], n_s[...]).astype(jnp.bfloat16)
        copies = []
        if cut is None:
            copies.append(pltpu.make_async_copy(go_s, grads[1], go_sem.at[0]))
        else:
            n_rows, n_cols, order2, _ = cut
            rows, cols = D // n_rows, D // n_cols
            at = fb * steps // n_cols
            for fr in range(n_rows):
                for c in range(n_cols):
                    slot = row_slot(fr, order2) + col_slot(c ^ col, order2)
                    src = go_s.at[pl.ds(pl.multiple_of((row ^ fr) * rows, 16), rows), c * cols : (c + 1) * cols]
                    dst = grads[fr & 1].at[slot, :, at : at + cols]
                    copies.append(pltpu.make_async_copy(src, dst, go_sem.at[len(copies)]))
        for copy in copies:
            copy.start()
        for i in range(nchunk):
            rs = slice(i * chunk, (i + 1) * chunk)
            dctx_ref[rs, :] = dot_nt(n_s[rs, :], wo_s[...]).astype(jnp.bfloat16)
        gv_ref[...] = jnp.concatenate([gbo, gg, gbi, gbp, jnp.zeros((4, D), jnp.float32)], axis=0)
        for copy in copies:
            copy.wait()
        for slot in range(min(2, steps)):
            block_copies(False, slot)


def mlp_block(info, context, x, d_out, pieces, loads, vec, b_fc, cut, widths, vmem, fb=768, chunk=256):
    S, D = x.shape
    FF = b_fc.shape[1]
    steps = FF // fb
    bf, f32, sd = jnp.bfloat16, jnp.float32, jax.ShapeDtypeStruct
    hbm = pl.BlockSpec(memory_space=pl.ANY)
    if cut is None:
        grads = [sd((D, FF), bf), sd((D, D), bf), sd((FF, D), bf)]
        n_out, n_go = 2, 1
    else:
        n_rows, n_cols = cut[:2]
        half = n_rows * n_cols // 2
        grads = [sd((half, D // n_rows, sum(widths)), bf)] * 2 + [sd((half, FF // n_rows, D // n_cols), bf)] * 2
        n_out, n_go = n_rows + fb * n_rows // FF * n_cols, n_rows * n_cols
    spec = pltpu.PrefetchScalarGridSpec(
        num_scalar_prefetch=1,
        grid=(steps,),
        in_specs=[whole((S, D))] * 3 + [whole((8, D)), pl.BlockSpec((1, fb), lambda f, i: (0, f))] + [hbm] * len(pieces),
        out_specs=[whole((S, D))] * 3 + [whole((8, D)), pl.BlockSpec((8, fb), lambda f, i: (0, f))] + [hbm] * len(grads),
        scratch_shapes=[
            pltpu.VMEM((S, D), bf), pltpu.VMEM((D, S), bf), pltpu.VMEM((S, D), bf),
            pltpu.VMEM((S, D), f32), pltpu.VMEM((S, D), f32), pltpu.VMEM((S, D), f32),
            pltpu.VMEM((S, fb), bf), pltpu.VMEM((S, fb), bf),
            pltpu.VMEM((D, FF), bf), pltpu.VMEM((D, D), bf), pltpu.VMEM((FF, D), bf), pltpu.VMEM((D, D), bf),
            pltpu.VMEM((2, D, fb), bf), pltpu.VMEM((2, fb, D), bf),
            pltpu.SemaphoreType.DMA((len(loads),)), pltpu.SemaphoreType.DMA((2, n_out)), pltpu.SemaphoreType.DMA((n_go,)),
        ],
    )
    return pl.pallas_call(
        functools.partial(mlp_kernel, steps, chunk, loads, cut),
        grid_spec=spec,
        out_shape=[sd((S, D), bf), sd((S, D), f32), sd((S, D), bf), sd((8, D), f32), sd((8, FF), f32)] + grads,
        compiler_params=pltpu.CompilerParams(vmem_limit_bytes=vmem, dimension_semantics=("arbitrary",)),
        cost_estimate=pl.CostEstimate(
            flops=12 * S * D * FF + 6 * S * D * D, bytes_accessed=8 * D * FF + 20 * S * D, transcendentals=S * FF
        ),
        name="mlp_block",
    )(info, context, x, d_out, vec, b_fc, *pieces)


def wgrad_kernel(cut, count, split, info_ref, nT_ref, bT_ref, *refs):
    n_rows, n_cols = cut
    parts, outs, (g_s, sem) = refs[: 5 * count], refs[5 * count : -2], refs[-2:]
    D = nT_ref.shape[0]
    rows, w = D // n_rows, parts[0].shape[1] // 2
    row, col = info_ref[2], info_ref[3]
    copies = []
    nT, bT = nT_ref[...], bT_ref[...]
    for c in range(n_cols):
        at = 0
        for p in range(count):
            q_ref, k_ref, v_ref, mk_ref, mv_ref = parts[5 * p : 5 * p + 5]
            if c == 0:
                terms = [(nT, q_ref[...]), (nT, k_ref[:, :w]), (bT, mk_ref[...])]
            else:
                terms = [(nT, k_ref[:, w:]), (nT, v_ref[...]), (bT, mv_ref[...])]
            for left, right in terms:
                g_s[c, :, at : at + right.shape[1]] = dot_nn(left, right).astype(jnp.bfloat16)
                at += right.shape[1]
        at = 0
        for i, (width, order) in enumerate(split):
            for fr in range(n_rows):
                slot = row_slot(fr, order) + col_slot(c ^ col, order)
                block = g_s.at[c, pl.ds(pl.multiple_of((row ^ fr) * rows, 16), rows), at : at + width]
                copies.append(pltpu.make_async_copy(block, outs[2 * i + (fr & 1)].at[slot], sem.at[len(copies)]))
                copies[-1].start()
            at += width
    for copy in copies:
        copy.wait()


def weight_grads(info, nT, bT, parts, n_rows, split, vmem):
    D, S = nT.shape
    nb, w, n_cols, count = bT.shape[1], parts[0][0].shape[1] // 2, 2, len(parts)
    rows = D // n_rows
    flat = [d for part in parts for d in part]
    bf, hbm = jnp.bfloat16, pl.BlockSpec(memory_space=pl.ANY)
    outs = []
    for width, _ in split:
        outs += [jax.ShapeDtypeStruct((n_rows * n_cols // 2, rows, width), bf)] * 2
    outs = pl.pallas_call(
        functools.partial(wgrad_kernel, (n_rows, n_cols), count, split),
        grid_spec=pltpu.PrefetchScalarGridSpec(
            num_scalar_prefetch=1,
            grid=(1,),
            in_specs=[whole(a.shape) for a in [nT, bT] + flat],
            out_specs=[hbm] * len(outs),
            scratch_shapes=[
                pltpu.VMEM((n_cols, D, 5 * w * count), bf), pltpu.SemaphoreType.DMA((n_rows * n_cols * len(split),)),
            ],
        ),
        out_shape=outs,
        compiler_params=pltpu.CompilerParams(vmem_limit_bytes=vmem),
        cost_estimate=pl.CostEstimate(
            flops=12 * S * D * w * count, bytes_accessed=14 * S * w * count + 2 * S * D + 20 * D * w * count, transcendentals=0
        ),
        name="weight_grads",
    )(info, nT, bT, *flat)
    return [Scatter(outs[2 * i], outs[2 * i + 1], order) for i, (_, order) in enumerate(split)]


def tokens_kernel(count,w_ref,x_ref,dm_ref,gain_ref,*refs):
    o_ref,gv_ref=refs[-2:]
    i=pl.program_id(0); D=x_ref.shape[1]; width=D//(2*count)
    dn=None
    for kind in range(3):
        for p in range(count):
            at=kind*D+2*p*width
            term=dot_nt(refs[3*p+kind][...],w_ref[:,at:at+2*width])
            dn=term if dn is None else dn+term
    xhat,rstd=norm_parts(x_ref[...].astype(jnp.float32))
    o_ref[...]=dm_ref[...]+norm_back(dn*gain_ref[...],xhat,rstd)
    @pl.when(i==0)
    def _(): gv_ref[...]=jnp.zeros_like(gv_ref)
    gv_ref[0:1]+=jnp.sum(dn*xhat,axis=0,keepdims=True)
    gv_ref[1:2]+=jnp.sum(dn,axis=0,keepdims=True)

def token_grad(parts,w,x,d_middle,gain,vmem,rows=256):
    S,D=x.shape; count=len(parts); width=D//count
    by_row=lambda width: pl.BlockSpec((rows,width),lambda i:(i,0))
    return pl.pallas_call(functools.partial(tokens_kernel,count),grid=(S//rows,),
        in_specs=[whole((D,3*D)),by_row(D),by_row(D),whole((1,D))]+[by_row(width)]*(3*count),
        out_specs=[by_row(D),pl.BlockSpec((8,D),lambda i:(0,0))],
        out_shape=[jax.ShapeDtypeStruct((S,D),jnp.float32),jax.ShapeDtypeStruct((8,D),jnp.float32)],
        compiler_params=pltpu.CompilerParams(vmem_limit_bytes=vmem),
        cost_estimate=pl.CostEstimate(flops=6*S*D*D,bytes_accessed=16*S*D+6*D*D,transcendentals=0),name="token_grad")(w,x,d_middle,gain,*[d for part in parts for d in part])


VMEM_BYTES = 58 << 20
FIT_NODE_COUNT = 512
ridge = 0.5


def fit_constant(nb):
    centers = (np.arange(nb, dtype=np.float64) + 0.5) / nb
    times = (np.arange(FIT_NODE_COUNT, dtype=np.float64) + 0.5) / FIT_NODE_COUNT
    design = np.exp(-0.5 * (times[None, :] - centers[:, None]) ** 2 * (nb * nb))
    table = np.linalg.solve(design @ design.T + ridge * np.eye(nb), design).astype(np.float32)
    hi = table.astype(jnp.bfloat16)
    lo = (table - hi.astype(np.float32)).astype(jnp.bfloat16)
    return np.concatenate([hi, lo], axis=0)


def bits_of(n):
    count = n.bit_length() - 1
    assert 1 << count == n
    return count


def swap(block, stage):
    axis, bit = stage
    n = lax.axis_size(axis)
    return lax.ppermute(block, axis, [(i, i ^ (1 << bit)) for i in range(n)])


class Chain:
    def __init__(self):
        self.last = ()

    def wait(self, *values):
        got = lax.optimization_barrier(values + self.last)
        self.last = got[:1]
        return got[0] if len(values) == 1 else got[: len(values)]


def stage_lists():
    rows = bits_of(lax.axis_size("row"))
    cols = bits_of(lax.axis_size("col"))
    far = [("row", b) for b in range(rows - 1, 1, -1)]
    col = [("col", b) for b in range(cols - 1, -1, -1)]
    near = [("row", 1)] if rows > 1 else []
    return far, col, near, [("row", 0)]


def slot_offsets(order):
    table = []
    for slot in range(1 << len(order)):
        flips = {"row": 0, "col": 0}
        for i, (axis, bit) in enumerate(order):
            if slot >> i & 1:
                flips[axis] ^= 1 << bit
        table.append((flips["row"], flips["col"]))
    return table


def place_bits():
    rows, cols = bits_of(lax.axis_size("row")), bits_of(lax.axis_size("col"))
    return [("row", b) for b in range(rows - 1, -1, -1)] + [("col", b) for b in range(cols - 1, -1, -1)]


def by_place(slots, order):
    seen = order[::-1]
    dims = [seen.index(p) for p in place_bits()]
    split = slots.reshape((2,) * len(order) + slots.shape[1:])
    tail = range(len(order), split.ndim)
    return split.transpose(dims + list(tail)).reshape(slots.shape)


def by_slot(blocks, order):
    places = place_bits()
    dims = [places.index(p) for p in order[::-1]]
    split = blocks.reshape((2,) * len(order) + blocks.shape[1:])
    tail = range(len(order), split.ndim)
    return split.transpose(dims + list(tail)).reshape(blocks.shape)


def flipped(blocks, row, col):
    places = place_bits()
    split = blocks.reshape((2,) * len(places) + blocks.shape[1:])
    for dim, (axis, bit) in enumerate(places):
        mine = (row if axis == "row" else col) >> bit & 1
        split = jnp.where(mine == 1, jnp.flip(split, dim), split)
    return split.reshape(blocks.shape)


class Gather:
    def __init__(self, block, order, done=0):
        self.held, self.order, self.done = (block if done else block[None]), order, done

    def send(self):
        self.came = swap(self.held, self.order[self.done])
        return self

    def take(self, came):
        self.done += 1
        if self.done == len(self.order):
            self.came = came
        else:
            self.held = jnp.concatenate([self.held, came], axis=0)
        return self

    def halves(self, cut, orders):
        return [
            Gather(self.held[:, :, :cut], orders[0], self.done),
            Gather(self.held[:, :, cut:], orders[1], self.done),
        ]


def advance(chain, *gathers):
    got = chain.wait(*[g.came for g in gathers])
    got = got if len(gathers) > 1 else (got,)
    for g, came in zip(gathers, got):
        g.take(came)
        if g.done < len(g.order):
            g.send()


def copy_kernel(plans, place_ref, *refs):
    sem = refs[-1]
    copies = []
    for src, dst, fr, fc, rows, cols, slot, at, column, width, outward in plans:
        r = place_ref[0] ^ fr
        c = place_ref[1] ^ fc
        matrix, slots = (refs[dst], refs[src]) if outward else (refs[src], refs[dst])
        block = matrix.at[
            pl.ds(pl.multiple_of(r * rows, 8), rows), pl.ds(pl.multiple_of(c * cols + column, 128), width)
        ]
        piece = slots.at[slot, :, pl.ds(at, width)]
        pair = (piece, block) if outward else (block, piece)
        copies.append(pltpu.make_async_copy(*pair, sem.at[len(copies)]))
    for copy in copies:
        copy.start()
    for copy in copies:
        copy.wait()


def copy_call(plans, place, ins, out_shapes, resident, name):
    hbm = pl.BlockSpec(memory_space=pl.ANY)
    size = sum(math.prod(o.shape) for o in out_shapes)
    return pl.pallas_call(
        functools.partial(copy_kernel, plans),
        grid_spec=pltpu.PrefetchScalarGridSpec(
            num_scalar_prefetch=1,
            grid=(1,),
            in_specs=[hbm] * len(ins),
            out_specs=[whole(o.shape) if resident else hbm for o in out_shapes],
            scratch_shapes=[pltpu.SemaphoreType.DMA((len(plans),))],
        ),
        out_shape=out_shapes,
        compiler_params=pltpu.CompilerParams(vmem_limit_bytes=24 << 20),
        cost_estimate=pl.CostEstimate(flops=0, bytes_accessed=4 * size, transcendentals=0),
        name=name,
    )(place, *ins)


def ranges_of(layout, offset, width):
    found, at = [], 0
    for i, size in enumerate(layout):
        low, high = max(at, offset), min(at + size, offset + width)
        if low < high:
            found.append((i, low - offset, low - at, high - low))
        at += size
    return found


def assemble(place, gathers, layout, n_rows, n_cols):
    rows = gathers[0].held.shape[1]
    shapes = [jax.ShapeDtypeStruct((rows * n_rows, w * n_cols), jnp.bfloat16) for w in layout]
    pieces, plans, offset = [], [], 0
    aligned = rows % 8 == 0 and all(w % 128 == 0 for w in layout)
    if not aligned:
        full = []
        for g in gathers:
            slots = jnp.concatenate([g.held, g.came], axis=0)
            full.append(flipped(by_place(slots, g.order), place[0], place[1]))
        full = jnp.concatenate(full, axis=2)
        res, at = [], 0
        for w in layout:
            block = full[:, :, at : at + w].reshape(n_rows, n_cols, rows, w)
            res.append(block.transpose(0, 2, 1, 3).reshape(rows * n_rows, w * n_cols))
            at += w
        return res
    for g in gathers:
        table = slot_offsets(g.order)
        width = g.held.shape[2]
        for slot, (fr, fc) in enumerate(table):
            src = len(pieces) + slot // (len(table) // 2)
            for i, at, column, w in ranges_of(layout, offset, width):
                plans.append((src, i, fr, fc, rows, layout[i], slot % (len(table) // 2), at, column, w, True))
        pieces += [g.held, g.came]
        offset += width
    plans = [(p[0], len(pieces) + p[1]) + p[2:] for p in plans]
    return copy_call(plans, place, pieces, shapes, True, "assemble")


class Scatter:
    def __init__(self, keep, send, order):
        self.order, self.left = order, len(order)
        self.terms, self.out = [keep], send
        self.total = None

    def send(self):
        self.left -= 1
        self.came = swap(self.out, self.order[self.left])
        return self

    def take(self, came):
        self.terms.append(came)
        if self.left == 0:
            self.total = sum(t.astype(jnp.float32) for t in self.terms)[0]
            return self
        half = self.terms[0].shape[0] // 2
        self.out = sum(t[half:].astype(jnp.float32) for t in self.terms).astype(jnp.bfloat16)
        self.terms = [t[:half] for t in self.terms]
        return self


def joint(*scatters):
    one = Scatter(None, jnp.concatenate([s.out for s in scatters], axis=2), scatters[0].order)
    kept = [sum(t.astype(jnp.float32) for t in s.terms) for s in scatters]
    one.terms, one.left = [jnp.concatenate(kept, axis=2)], scatters[0].left
    return one


def onward(chain, *scatters):
    got = chain.wait(*[s.came for s in scatters])
    got = got if len(scatters) > 1 else (got,)
    for s, came in zip(scatters, got):
        s.take(came)
        if s.left:
            s.send()


def disperse(place, grads, cuts, n_rows, n_cols):
    rows = grads[0].shape[0] // n_rows
    blocks = [g.reshape(n_rows, rows, n_cols, -1).transpose(0, 2, 1, 3) for g in grads]
    joined = jnp.concatenate(blocks, axis=3).reshape(n_rows * n_cols, rows, -1)
    joined = flipped(joined, place[0], place[1])
    res, offset = [], 0
    for width, order in cuts:
        slots = by_slot(joined[:, :, offset : offset + width], order)
        res.append(Scatter(slots[: len(slots) // 2], slots[len(slots) // 2 :], order))
        offset += width
    return res


def shards(
    tokens, w_qkv, w_out, w_mem, w_fc, w_proj, gain_attn, bias_attn, gain_mlp, bias_mlp, b_out, b_fc, b_proj,
    w_loc, w_spread, past_states, sticky_pos, seq_lengths, d_out,
):
    bf, f32 = jnp.bfloat16, jnp.float32
    n_rows, n_cols = lax.axis_size("row"), lax.axis_size("col")
    row, col = lax.axis_index("row"), lax.axis_index("col")
    place = jnp.stack([row, col]).astype(jnp.int32)
    batches, _, span, feat = tokens.shape
    heads, nb = w_loc.shape[0], w_loc.shape[1] * n_rows * n_cols
    hidden = w_fc.shape[1] * n_cols
    assert batches == 2 and n_cols % 2 == 0
    side = col % 2
    own, other = side, 1 - side
    first = (col - side) * span
    far, along, near, core = stage_lists()
    zyx, zxy, yzx = far + along + near + core, far + near + along + core, along + far + near + core
    devices = n_rows * n_cols

    def pick(a, i):
        return lax.dynamic_index_in_dim(a, i, 0, keepdims=False)

    def to_chunk(mine, came):
        two = jnp.stack([mine, came])
        return jnp.where(side == 0, two, two[::-1]).reshape((2 * span,) + mine.shape[1:])

    def trade(a):
        return swap(a, ("col", 0))

    tokens, past, d_out = tokens[:, 0], past_states[:, 0], d_out[:, 0]
    sticky, lengths = sticky_pos[:, 0], seq_lengths[:, 0]
    length = pick(lengths, own)
    info = jnp.stack([length, first, row, col]).astype(jnp.int32)

    singles = [gain_attn, bias_attn, gain_mlp, bias_mlp, b_out, b_proj, b_fc]
    n_single, n_small = len(singles), len(singles) + heads
    rows_small = -(-n_small // 8) * 8
    both_w = jnp.concatenate([w_loc, w_spread], axis=1)

    def wide(v):
        v = v.reshape(-1, v.shape[-1])
        return jnp.pad(v, ((0, 0), (0, 128 - v.shape[1])))

    layout1 = [w_qkv.shape[1], w_mem.shape[1]]
    layout2 = [w_fc.shape[1], w_out.shape[1]]
    layout3 = [w_proj.shape[1]]
    width1 = sum(layout1)
    cut1 = (width1 // 128 + 1) // 2 * 128
    rows1 = w_qkv.shape[0]
    fb = 768
    direct = n_cols == 2 and all(w % 128 == 0 for w in layout1 + layout2 + layout3) and rows1 % 16 == 0
    direct = direct and layout2[0] % fb == 0 and fb % w_proj.shape[0] == 0

    def loads_of(gathers, layout, base, first):
        loads, pieces, offset = [], [], 0
        for g in gathers:
            table = slot_offsets(g.order)
            half, width = len(table) // 2, g.held.shape[2]
            for slot, (fr, fc) in enumerate(table):
                for i, at, column, w in ranges_of(layout, offset, width):
                    src = first + len(pieces) + slot // half
                    loads.append((src, base + i, fr, fc, g.held.shape[1], layout[i], slot % half, at, column, w))
            pieces += [g.held, g.came]
            offset += width
        return loads, pieces

    chain = Chain()
    g1 = Gather(jnp.concatenate([w_qkv, w_mem], axis=1), zyx).send()
    tokens_out, block2 = chain.wait(tokens, jnp.concatenate([w_fc, w_out], axis=1))
    came_tokens = trade(pick(tokens_out, other))
    g2 = Gather(block2, yzx).send()
    g3 = Gather(w_proj, zxy)
    flat = jnp.concatenate([wide(v) for v in singles + [both_w]])
    flat = jnp.pad(flat, ((0, rows_small - n_small), (0, 0)))
    g0 = None
    for _ in far[1:]:
        advance(chain, g1)
        if g0 is None:
            g0 = Gather(chain.wait(flat), zyx).send()
    g1.take(chain.wait(g1.came))
    g1a, g1b = g1.halves(cut1, (zyx, zxy))
    g1a.send()
    g1b.send()
    advance(chain, g0)
    g3.held = chain.wait(g3.held)
    g3.send()
    for _ in far[1:]:
        advance(chain, g3)
    advance(chain, g0)

    fit = jnp.asarray(fit_constant(nb))
    here = col * span
    past, sticky = chain.wait(past, sticky)

    def basis_part(i):
        spots = pick(sticky, i) - here
        resident = (spots >= 0) & (spots < span)
        picked = jnp.take(past.reshape(-1, feat), jnp.clip(spots, 0, span - 1) + i * span, axis=0)
        parts = jnp.dot(fit * resident.astype(bf)[None, :], picked, preferred_element_type=f32)
        return parts[:nb] + parts[nb:]

    advance(chain, g1b, g1a, g0)
    for _ in along[:-1]:
        advance(chain, g2)
    came_g3 = chain.wait(g3.came)
    advance(chain, g2)
    x = to_chunk(pick(tokens, own), chain.wait(came_tokens))
    if n_cols == 2:
        own_basis, basis_out = chain.wait(basis_part(own), basis_part(other).astype(bf))
    else:
        both = lax.psum(jnp.stack([basis_part(i).astype(bf) for i in range(2)]), "col")
        own_basis, came_basis = pick(both, own).astype(f32), jnp.zeros((nb, feat), bf)
    while g1b.done < len(g1b.order) - 1:
        advance(chain, g1b, g1a, g0)
    if n_cols == 2:
        came_basis = trade(chain.wait(basis_out))
    g3.take(chain.wait(came_g3)).send()
    came_out = trade(chain.wait(pick(d_out, other)))
    while g0.done < len(g0.order) - 1:
        advance(chain, g0)
    g0.came = chain.wait(g0.came)
    every = flipped(by_place(jnp.concatenate([g0.held, g0.came], axis=0), zyx), row, col)
    vectors = [every[:, i, : v.shape[0]].astype(f32).reshape(1, -1) for i, v in enumerate(singles)]
    gain1, bias1, gain2, bias2, bo, bp, bfc = vectors
    share = w_loc.shape[1]
    loc, spr = [
        every[:, n_single:n_small, at : at + share].transpose(1, 0, 2).reshape(heads // 2, 2, nb) for at in (0, share)
    ]
    wls = jnp.concatenate([loc, spr, jnp.zeros((heads // 2, 4, nb), bf)], axis=1)
    vec1 = jnp.concatenate([gain1, bias1, jnp.zeros((6, feat), f32)], axis=0)
    vec2 = jnp.concatenate([bo, gain2, bias2, bp, jnp.zeros((4, feat), f32)], axis=0)
    for _ in far[1:]:
        advance(chain, g2)
    x, vec1, vec2, wls = chain.wait(x, vec1, vec2, wls)
    g1b.came, g1a.came, came_basis = chain.wait(g1b.came, g1a.came, came_basis)

    if direct:
        loads, pieces = loads_of([g1a, g1b], layout1, 0, 0)
    else:
        pieces = assemble(place, [g1a, g1b], layout1, n_rows, n_cols)
        loads = [(i, i) + (None,) * 8 for i in range(2)]
    nT, qkv, mem_kv, basisT, wq = project_qkv(info, x, vec1, own_basis, came_basis, pieces, loads, heads // 2, VMEM_BYTES)
    qkv = chain.wait(qkv)
    advance(chain, g2)
    for _ in along[:1]:
        advance(chain, g3)
    g_other = chain.wait(came_out)
    halo = 0 if n_cols == 2 else WINDOW
    pairs = heads // 2
    route = [(i, i + 2) for i in range(n_cols - 2)]
    back = [(i + 2, i) for i in range(n_cols - 2)]
    if halo:
        before = lax.ppermute(qkv[-halo:, feat:], "col", route)
        kvx = jnp.concatenate([before, qkv[:, feat:]], axis=0)
        kv = (kvx, 0, kvx, pairs)
    else:
        kv = (qkv, pairs, qkv, 2 * pairs)
    mem_kv, g2.held, g3.held = chain.wait(mem_kv, g2.held, g3.held)
    context, lse = attention_forward(info, qkv, kv, halo, mem_kv, wls, heads, VMEM_BYTES)
    context = chain.wait(context)
    while g3.done < len(g3.order) - 1:
        advance(chain, g3)
    while g2.done < len(g2.order) - 1:
        advance(chain, g2)
    g_chunk = to_chunk(pick(d_out, own), g_other)
    g3.came, g2.came = chain.wait(g3.came, g2.came)

    if direct:
        loads, pieces = loads_of([g2], layout2, 0, 0)
        loads3, pieces3 = loads_of([g3], layout3, 2, len(pieces))
        loads, pieces = loads + loads3, pieces + pieces3
    else:
        wf, wo = assemble(place, [g2], layout2, n_rows, n_cols)
        wp = assemble(place, [g3], layout3, n_rows, n_cols)[0]
        pieces = [wf, wo, wp]
        loads = [(i, i) + (None,) * 8 for i in range(3)]
    output, d_middle, d_context, g_vec, g_bfc, *cut_grads = mlp_block(
        info, context, x, g_chunk, pieces, loads, vec2, bfc,
        (n_rows, n_cols, yzx, zxy) if direct else None, layout2, VMEM_BYTES, fb,
    )

    def from_chunk(chunk):
        halves = chunk.reshape(2, span, feat)
        return pick(halves, own), pick(halves, other)

    def paired(kept, came):
        two = jnp.stack([kept, came])
        return jnp.where(side == 0, two, two[::-1])[:, None]

    if direct:
        s2, s3 = Scatter(*cut_grads[:2], yzx), Scatter(*cut_grads[2:], zxy)
    else:
        s2 = disperse(place, cut_grads[:2], [(sum(layout2), yzx)], n_rows, n_cols)[0]
        s3 = disperse(place, cut_grads[2:], [(sum(layout3), zxy)], n_rows, n_cols)[0]
    s2.send()
    s3.send()
    d_context, s2.terms[0], s3.terms[0] = chain.wait(d_context, s2.terms[0], s3.terms[0])

    def taken(*scatters):
        got = chain.wait(*[s.came for s in scatters])
        for s, came in zip(scatters, got if len(scatters) > 1 else (got,)):
            s.take(came)
        outs = chain.wait(*[s.out for s in scatters])
        for s, out in zip(scatters, outs if len(scatters) > 1 else (outs,)):
            s.out = out
            s.send()

    count = pairs // 2
    mixed, parts = [], []
    kept_out, sent = from_chunk(output)
    d_context, sent = chain.wait(d_context, sent)
    came_output = trade(sent)
    for i in range(count):
        d_context = chain.wait(d_context)
        got = list(
            attention_backward(info, qkv, kv, halo, mem_kv, wls, lse, d_context, heads, VMEM_BYTES, i, 2, count)
        )
        got[0] = chain.wait(got[0])
        mixed.append(got)
        d_q, d_k, d_v, d_mk, d_mv, _ = got
        if halo:
            d_kv = jnp.concatenate([d_k, d_v], axis=1)
            ret = lax.ppermute(d_kv[:halo], "col", back)
            d_kv = d_kv[halo:].astype(f32) + jnp.pad(ret.astype(f32), ((2 * span - halo, 0), (0, 0)))
            d_kv = d_kv.astype(bf)
            d_k, d_v = jnp.split(d_kv, 2, axis=1)
        parts.append((d_q, d_k, d_v, d_mk, d_mv))
        if i == 0:
            came_output = chain.wait(came_output)
            taken(s2, s3)
    taken(s3)
    taken(s2)
    d_middle = chain.wait(d_middle)
    d_tok, g_vec1 = token_grad([p[:3] for p in parts], wq, x, d_middle, gain1, VMEM_BYTES)
    d_tok, g_vec1 = chain.wait(d_tok, g_vec1)
    taken(s3)
    taken(s2)
    kept_x, sent_x = from_chunk(d_tok)
    came_x = trade(chain.wait(sent_x.astype(bf)))
    nT = chain.wait(nT)
    if direct:
        s1 = weight_grads(info, nT, basisT, parts, n_rows, [(cut1, zyx), (width1 - cut1, zxy)], VMEM_BYTES)
    else:
        ordered = [jnp.stack([p[k].reshape(p[k].shape[0], 2, -1) for p in parts], axis=2) for k in range(5)]
        ordered = [a.reshape(a.shape[0], feat) for a in ordered]
        g_qkv = jnp.dot(nT, jnp.concatenate(ordered[:3], axis=1), preferred_element_type=f32).astype(bf)
        g_mem = jnp.dot(basisT, jnp.concatenate(ordered[3:], axis=1), preferred_element_type=f32).astype(bf)
        s1 = disperse(place, [g_qkv, g_mem], [(cut1, zyx), (width1 - cut1, zxy)], n_rows, n_cols)
    for s_ in s1:
        s_.send()
    s1[0].terms[0] = chain.wait(s1[0].terms[0])
    came_x = chain.wait(came_x)
    by_pair = [m[5][j] for j in range(2) for m in mixed]
    total = jnp.concatenate([g_vec, g_vec1, g_bfc] + by_pair, axis=1)
    stages = zyx[::-1]
    came = swap(total.astype(bf), stages.pop(0))
    while any(s_.left for s_ in s1 + [s2, s3]) or came is not None:
        live = [s_ for s_ in s1 if s_.left]
        if live and len(s1) == 2 and live[0].left == len(far):
            for s_, got in zip(s1, chain.wait(*[s_.came for s_ in s1])):
                s_.take(got)
            s1 = [joint(*s1).send()]
        elif live:
            onward(chain, *live)
        if came is not None:
            total = total + chain.wait(came).astype(f32)
            came = swap(total.astype(bf), stages.pop(0)) if stages else None
        for s_ in (s3, s2):
            if s_.left:
                onward(chain, s_)
    for s_ in [s3, s2]:
        if s_.total is None:
            s_.take(chain.wait(s_.came))
    index = row * n_cols + col

    def mine(block, first, width):
        return lax.dynamic_slice_in_dim(block, first + index * width, width, axis=1)

    g_bo, g_gain2, g_bias2, g_bp = mine(total, 0, gain_mlp.shape[0])[:4]
    g_gain1, g_bias1 = mine(total, feat, gain_attn.shape[0])[:2]
    g_bf = mine(total, 2 * feat, b_fc.shape[0])[0]
    per_pair = total[:, 2 * feat + hidden :].reshape(8, pairs, nb).transpose(1, 0, 2)
    g_loc = lax.dynamic_slice_in_dim(per_pair[:, 0:2].reshape(heads, nb), index * share, share, axis=1)
    g_spread = lax.dynamic_slice_in_dim(per_pair[:, 2:4].reshape(heads, nb), index * share, share, axis=1)
    outputs = paired(kept_out, came_output)
    grad_x = paired(kept_x, came_x.astype(f32))
    for s_ in s1:
        s_.take(chain.wait(s_.came))
    joined = jnp.concatenate([s_.total for s_ in s1], axis=1)
    if direct:
        w = feat // pairs
        n_qkv = layout1[0] // (count * w)
        blocks = joined.reshape(rows1, count, 5, w)
        grad_qkv = blocks[:, :, :n_qkv].transpose(0, 2, 1, 3).reshape(rows1, layout1[0])
        grad_mem = blocks[:, :, n_qkv:].transpose(0, 2, 1, 3).reshape(rows1, layout1[1])
    else:
        grad_qkv, grad_mem = joined[:, : layout1[0]], joined[:, layout1[0] :]
    grad_fc, grad_out = s2.total[:, : layout2[0]], s2.total[:, layout2[0] :]
    grad_proj = s3.total
    return (
        outputs, grad_x, grad_qkv, grad_out, grad_mem, grad_fc, grad_proj,
        g_gain1, g_bias1, g_gain2, g_bias2, g_bo, g_bf, g_bp, g_loc, g_spread,
    )


def solution(mesh):
    grid, both, tail = P("row", "col"), P(("row", "col")), P(None, ("row", "col"))
    act, rows = P(None, "row", "col", None), P(None, "row")
    return jax.shard_map(
        shards,
        mesh=mesh,
        in_specs=(act,) + (grid,) * 5 + (both,) * 7 + (tail,) * 2 + (act, P(None, "row", None), rows, act),
        out_specs=(act, act) + (grid,) * 5 + (both,) * 7 + (tail,) * 2,
        check_vma=False,
    )
```

```python
import functools
import math

import jax
import jax.numpy as jnp
import numpy as np
from jax import lax
from jax.experimental import pallas as pl
from jax.experimental.pallas import tpu as pltpu
from jax.sharding import PartitionSpec as P

WINDOW=512; TILE=256; masked=-1e30
var_scale=0.01
NT=(((1,),(1,)),((),()))
NN=(((1,),(0,)),((),()))

def dot_nt(a,b): return lax.dot_general(a,b,NT,preferred_element_type=jnp.float32)
def dot_nn(a,b): return lax.dot_general(a,b,NN,preferred_element_type=jnp.float32)

def split3(v):
    hi=v.astype(jnp.bfloat16); r=v-hi.astype(jnp.float32)
    mid=r.astype(jnp.bfloat16); lo=(r-mid.astype(jnp.float32)).astype(jnp.bfloat16)
    return hi,mid,lo

def lane_is_first(shape,half):
    return lax.broadcasted_iota(jnp.int32,shape,1)<half

def tile_biases(info_ref,first_key,has_far,has_mid):
    key=lax.broadcasted_iota(jnp.int32,(TILE,TILE),0)
    qry=lax.broadcasted_iota(jnp.int32,(TILE,TILE),1)
    tri=key<=qry
    length=info_ref[0]
    diag_pos=first_key+key
    far_pos=diag_pos-WINDOW
    near=jnp.where((diag_pos<length)|(key==qry),0.0,masked)
    far=jnp.where((far_pos>=0)&(far_pos<length),0.0,masked) if has_far else masked
    comb=jnp.where(tri,near,far)
    mid_pos=diag_pos-TILE
    mid=jnp.where((mid_pos>=0)&(mid_pos<length),0.0,masked)
    return comb,mid

def density_rows(wls,mk,half):
    vec=dot_nn(wls,mk)
    row=lax.broadcasted_iota(jnp.int32,vec.shape,0)
    lane=lax.broadcasted_iota(jnp.int32,vec.shape,1)
    return jnp.where((row%2==0)==(lane<half),vec,0.0)

def logits_of(vec,qb):
    hi,mid,lo=split3(vec)
    parts=dot_nt(jnp.concatenate([hi,mid,lo,lo],axis=0),qb)
    return (parts[16:24]+parts[8:16])+parts[0:8]

def spreads(logits,nb):
    location=1.0/(1.0+jnp.exp(-logits))
    soft=jnp.maximum(logits,0.0)+jnp.log1p(jnp.exp(-jnp.abs(logits)))
    spread=var_scale*soft+1.0/(nb*nb)
    return location,spread

def fwd_kernel(halo,half,info_ref,q_ref,k_ref,v_ref,mk_ref,mv_ref,wls_ref,ctx_ref,lse_ref,bias_ref):
    S=q_ref.shape[0]; nblk=S//TILE; nb=mk_ref.shape[0]; ht=halo//TILE
    @pl.when(pl.program_id(0)==0)
    def _():
        for i in range(nblk):
            comb,mid=tile_biases(info_ref,info_ref[1]+i*TILE,ht+i>=2,ht+i>=1)
            bias_ref[2*i]=comb; bias_ref[2*i+1]=mid
    tri=lax.broadcasted_iota(jnp.int32,(TILE,TILE),0)<=lax.broadcasted_iota(jnp.int32,(TILE,TILE),1)
    trib=jnp.where(tri,1.0,0.0).astype(jnp.bfloat16)
    lane=lax.broadcasted_iota(jnp.int32,(16,2*half),1)
    sides=[jnp.where(lane<half,1.0,0.0)[0:1].astype(jnp.bfloat16),jnp.where(lane<half,0.0,1.0)[0:1].astype(jnp.bfloat16)]
    centers=(lax.broadcasted_iota(jnp.int32,(nb,TILE),0).astype(jnp.float32)+0.5)/nb
    vec=density_rows(wls_ref[0],mk_ref[...],half)
    vT=v_ref[...].T
    mvT=mv_ref[...].T
    lse_ref[...]=jnp.zeros_like(lse_ref)
    for i in range(nblk):
        rows=slice(i*TILE,(i+1)*TILE)
        qb=q_ref[rows,:]*jnp.bfloat16(half**-0.5)
        d0=halo+i*TILE
        has_mid=ht+i>=1; has_far=ht+i>=2
        kd=k_ref[d0:d0+TILE,:]
        logits=logits_of(vec,qb)
        location,spread=spreads(logits,nb)
        nis=-0.5/spread
        norm=lax.rsqrt(2.0*math.pi*spread)*(1.0/nb)
        outs=[]
        for x in range(2):
            qx=qb*sides[x]
            vx=vT[x*half:(x+1)*half,:]
            sd=dot_nt(kd,qx)
            if has_far:
                sf=dot_nt(k_ref[d0-2*TILE:d0-TILE,:],qx)
                sc=jnp.where(tri,sd,sf)+bias_ref[2*i]
            else:
                sc=sd+bias_ref[2*i]
            top=jnp.max(sc,axis=0,keepdims=True)
            if has_mid:
                sm=dot_nt(k_ref[d0-TILE:d0,:],qx)+bias_ref[2*i+1]
                top=jnp.maximum(top,jnp.max(sm,axis=0,keepdims=True))
            ec=jnp.exp(sc-top)
            tot=jnp.sum(ec,axis=0,keepdims=True)
            ecl=ec.astype(jnp.bfloat16)
            if has_far:
                near=ecl*trib
                o=dot_nn(vx[:,d0:d0+TILE],near)+dot_nn(vx[:,d0-2*TILE:d0-TILE],ecl-near)
            else:
                o=dot_nn(vx[:,d0:d0+TILE],ecl)
            if has_mid:
                em=jnp.exp(sm-top)
                tot=tot+jnp.sum(em,axis=0,keepdims=True)
                o=o+dot_nn(vx[:,d0-TILE:d0],em.astype(jnp.bfloat16))
            lse_ref[0,x:x+1,rows]=top+jnp.log(tot)
            o=o*(1.0/tot)
            z=location[x:x+1]-centers
            e=jnp.exp(nis[2+x:3+x]*(z*z))
            r=dot_nn(mvT[x*half:(x+1)*half,:],e.astype(jnp.bfloat16))*norm[2+x:3+x]
            outs.append(o+r)
        ctx_ref[rows,:]=jnp.concatenate(outs,axis=0).T.astype(jnp.bfloat16)

def bwd_kernel(halo,half,info_ref,q_ref,k_ref,v_ref,mk_ref,mv_ref,wls_ref,lse_ref,do_ref,
               dq_ref,dk_ref,dv_ref,dmk_ref,dmv_ref,gls_ref,bias_ref,dk_acc,dv_acc):
    S=q_ref.shape[0]; nblk=S//TILE; nb=mk_ref.shape[0]; ht=halo//TILE
    @pl.when(pl.program_id(0)==0)
    def _():
        for i in range(nblk):
            comb,mid=tile_biases(info_ref,info_ref[1]+i*TILE,ht+i>=2,ht+i>=1)
            bias_ref[2*i]=comb; bias_ref[2*i+1]=mid
    tri=lax.broadcasted_iota(jnp.int32,(TILE,TILE),0)<=lax.broadcasted_iota(jnp.int32,(TILE,TILE),1)
    trib=jnp.where(tri,1.0,0.0).astype(jnp.bfloat16)
    lane=lax.broadcasted_iota(jnp.int32,(16,2*half),1)
    sides=[jnp.where(lane<half,1.0,0.0)[0:1].astype(jnp.bfloat16),jnp.where(lane<half,0.0,1.0)[0:1].astype(jnp.bfloat16)]
    centers=(lax.broadcasted_iota(jnp.int32,(nb,TILE),0).astype(jnp.float32)+0.5)/nb
    mk=mk_ref[...]; mv=mv_ref[...]
    vec=density_rows(wls_ref[0],mk,half)
    vecT=vec.T
    kT=k_ref[...].T
    dk_acc[...]=jnp.zeros_like(dk_acc); dv_acc[...]=jnp.zeros_like(dv_acc)
    dmv=jnp.zeros((nb,2*half),jnp.float32)
    dvec=jnp.zeros((8,2*half),jnp.float32)
    for i in range(nblk):
        rows=slice(i*TILE,(i+1)*TILE)
        qb=q_ref[rows,:]*jnp.bfloat16(half**-0.5)
        dob=do_ref[rows,:]
        d0=halo+i*TILE
        has_mid=ht+i>=1; has_far=ht+i>=2
        dg=slice(d0,d0+TILE); md=slice(d0-TILE,d0); fr=slice(d0-2*TILE,d0-TILE)
        logits=logits_of(vec,qb)
        location,spread=spreads(logits,nb)
        inv=1.0/spread
        nis=-0.5*inv
        norm=lax.rsqrt(2.0*math.pi*spread)*(1.0/nb)
        outs=[]; s0s=[]; s1s=[]; s2s=[]
        for x in range(2):
            qx=qb*sides[x]
            dox=dob*sides[x]
            kx=kT[x*half:(x+1)*half,:]
            lse=lse_ref[0,x:x+1,rows]
            sc=dot_nt(k_ref[dg,:],qx)
            dpc=dot_nt(v_ref[dg,:],dox)
            if has_far:
                sc=jnp.where(tri,sc,dot_nt(k_ref[fr,:],qx))
                dpc=jnp.where(tri,dpc,dot_nt(v_ref[fr,:],dox))
            pc=jnp.exp(sc+bias_ref[2*i]-lse)
            delta=jnp.sum(pc*dpc,axis=0,keepdims=True)
            if has_mid:
                sm=dot_nt(k_ref[md,:],qx)
                dpm=dot_nt(v_ref[md,:],dox)
                pm=jnp.exp(sm+bias_ref[2*i+1]-lse)
                delta=delta+jnp.sum(pm*dpm,axis=0,keepdims=True)
                dsm=(pm*(dpm-delta)).astype(jnp.bfloat16)
                dv_acc[md,:]+=dot_nn(pm.astype(jnp.bfloat16),dox)
                dk_acc[md,:]+=dot_nn(dsm,qx)
            dsc=(pc*(dpc-delta)).astype(jnp.bfloat16)
            pcl=pc.astype(jnp.bfloat16)
            if has_far:
                dsd=dsc*trib; dsf=dsc-dsd
                near=pcl*trib
                dv_acc[dg,:]+=dot_nn(near,dox)
                dv_acc[fr,:]+=dot_nn(pcl-near,dox)
                dk_acc[dg,:]+=dot_nn(dsd,qx)
                dk_acc[fr,:]+=dot_nn(dsf,qx)
                dq=dot_nn(kx[:,dg],dsd)+dot_nn(kx[:,fr],dsf)
            else:
                dv_acc[dg,:]+=dot_nn(pcl,dox)
                dk_acc[dg,:]+=dot_nn(dsc,qx)
                dq=dot_nn(kx[:,dg],dsc)
            if has_mid:
                dq=dq+dot_nn(kx[:,md],dsm)
            outs.append(dq)
            z=location[x:x+1]-centers
            e=jnp.exp(nis[2+x:3+x]*(z*z))
            g=dot_nt(mv,dox)*e
            gz=g*z
            s0s.append(jnp.sum(g,axis=0,keepdims=True))
            s1s.append(jnp.sum(gz,axis=0,keepdims=True))
            s2s.append(jnp.sum(gz*z,axis=0,keepdims=True))
            dmv=dmv+dot_nn((e*norm[2+x:3+x]).astype(jnp.bfloat16),dox)
        n2=norm[2:4]; i2=inv[2:4]
        s0=jnp.concatenate(s0s,axis=0); s1=jnp.concatenate(s1s,axis=0); s2=jnp.concatenate(s2s,axis=0)
        dloc=-(n2*i2)*s1
        dspr=n2*(0.5*i2)*(s2*i2-s0)
        l2=location[0:2]
        dll=dloc*l2*(1.0-l2)
        dsl=dspr*var_scale*location[2:4]
        dl=jnp.concatenate([dll,dsl,jnp.zeros((4,TILE),jnp.float32)],axis=0)
        hi=dl.astype(jnp.bfloat16); lo=(dl-hi.astype(jnp.float32)).astype(jnp.bfloat16)
        both=dot_nn(jnp.concatenate([hi,lo],axis=0),qb)
        dvec=dvec+(both[0:8]+both[8:16])
        for x in range(2):
            seg=slice(x*half,(x+1)*half)
            outs[x]=outs[x]+vecT[seg,x:x+1]*dl[x:x+1]+vecT[seg,2+x:3+x]*dl[2+x:3+x]
        dq_ref[rows,:]=(jnp.concatenate(outs,axis=0)*(half**-0.5)).T.astype(jnp.bfloat16)
    dk_ref[...]=dk_acc[...].astype(jnp.bfloat16)
    dv_ref[...]=dv_acc[...].astype(jnp.bfloat16)
    dmv_ref[...]=dmv.astype(jnp.bfloat16)
    row=lax.broadcasted_iota(jnp.int32,dvec.shape,0)
    lane=lax.broadcasted_iota(jnp.int32,dvec.shape,1)
    dvec=jnp.where((row%2==0)==(lane<half),dvec,0.0)
    hi=dvec.astype(jnp.bfloat16); lo=(dvec-hi.astype(jnp.float32)).astype(jnp.bfloat16)
    stack=jnp.concatenate([hi,lo],axis=0)
    gl=dot_nt(stack,mk)
    gls_ref[0]=gl[0:8]+gl[8:16]
    wT=wls_ref[0].astype(jnp.float32).T.astype(jnp.bfloat16)
    dmk_ref[...]=dot_nn(jnp.concatenate([wT,wT],axis=1),stack).astype(jnp.bfloat16)

def col_block(rows,width,first,stride=1):
    return pl.BlockSpec((rows,width),lambda p,info: (0,first+stride*p))

def attention_forward(info,qkv,kv,halo,mem_kv,wls,heads,vmem):
    S=qkv.shape[0]; pairs=heads//2; width=kv[0].shape[1]
    nb=mem_kv.shape[0]; feat=mem_kv.shape[1]//2; w=feat//pairs; half=w//2
    karr,koff,varr,voff=kv[0],kv[1],kv[2],kv[3]
    nblk=S//TILE
    spec=pltpu.PrefetchScalarGridSpec(num_scalar_prefetch=1,grid=(pairs,),
        in_specs=[col_block(S,w,0),col_block(halo+S,w,koff),col_block(halo+S,w,voff),col_block(nb,w,0),col_block(nb,w,pairs),
                  pl.BlockSpec((1,8,nb),lambda p,info:(p,0,0))],
        out_specs=[col_block(S,w,0),pl.BlockSpec((1,8,S),lambda p,info:(p,0,0))],
        scratch_shapes=[pltpu.VMEM((2*nblk,TILE,TILE),jnp.float32)])
    return pl.pallas_call(functools.partial(fwd_kernel,halo,half),grid_spec=spec,
        out_shape=[jax.ShapeDtypeStruct((S,feat),jnp.bfloat16),jax.ShapeDtypeStruct((pairs,8,S),jnp.float32)],
        compiler_params=pltpu.CompilerParams(vmem_limit_bytes=vmem,dimension_semantics=("arbitrary",)),
        cost_estimate=pl.CostEstimate(flops=24*S*S*feat//4,bytes_accessed=10*S*feat,transcendentals=heads*S*768),
        name="mix_forward")(info,qkv,karr,varr,mem_kv,mem_kv,wls)

def attention_backward(info,qkv,kv,halo,mem_kv,wls,lse,d_context,heads,vmem,begin,count,stride):
    S=qkv.shape[0]; pairs=heads//2
    nb=mem_kv.shape[0]; feat=mem_kv.shape[1]//2; w=feat//pairs; half=w//2
    karr,koff,varr,voff=kv
    nblk=S//TILE; bf=jnp.bfloat16
    spec=pltpu.PrefetchScalarGridSpec(num_scalar_prefetch=1,grid=(count,),
        in_specs=[col_block(S,w,begin,stride),col_block(halo+S,w,koff+begin,stride),col_block(halo+S,w,voff+begin,stride),
                  col_block(nb,w,begin,stride),col_block(nb,w,pairs+begin,stride),pl.BlockSpec((1,8,nb),lambda p,info:(begin+stride*p,0,0)),
                  pl.BlockSpec((1,8,S),lambda p,info:(begin+stride*p,0,0)),col_block(S,w,begin,stride)],
        out_specs=[col_block(S,w,0),col_block(halo+S,w,0),col_block(halo+S,w,0),col_block(nb,w,0),col_block(nb,w,0),
                   pl.BlockSpec((1,8,nb),lambda p,info:(p,0,0))],
        scratch_shapes=[pltpu.VMEM((2*nblk,TILE,TILE),jnp.float32),pltpu.VMEM((halo+S,w),jnp.float32),pltpu.VMEM((halo+S,w),jnp.float32)])
    part=count*w
    return pl.pallas_call(functools.partial(bwd_kernel,halo,half),grid_spec=spec,
        out_shape=[jax.ShapeDtypeStruct((S,part),bf),jax.ShapeDtypeStruct((halo+S,part),bf),jax.ShapeDtypeStruct((halo+S,part),bf),
                   jax.ShapeDtypeStruct((nb,part),bf),jax.ShapeDtypeStruct((nb,part),bf),jax.ShapeDtypeStruct((count,8,nb),jnp.float32)],
        compiler_params=pltpu.CompilerParams(vmem_limit_bytes=vmem,dimension_semantics=("arbitrary",)),
        cost_estimate=pl.CostEstimate(flops=30*S*S*part,bytes_accessed=20*S*part,transcendentals=2*count*S*768),
        name="mix_backward")(info,qkv,karr,varr,mem_kv,mem_kv,wls,lse,d_context)


eps=1e-5
TN=(((0,),(0,)),((),()))
def dot_tn(a,b): return lax.dot_general(a,b,TN,preferred_element_type=jnp.float32)

def norm_parts(v):
    center=jnp.mean(v,axis=-1,keepdims=True)
    off=v-center
    rstd=lax.rsqrt(jnp.mean(off*off,axis=-1,keepdims=True)+eps)
    return off*rstd,rstd

def norm_back(gd,xhat,rstd):
    return rstd*(gd-jnp.mean(gd,axis=-1,keepdims=True)-xhat*jnp.mean(gd*xhat,axis=-1,keepdims=True))

def whole(shape): return pl.BlockSpec(shape,lambda *a: (0,)*len(shape),pipeline_mode=pl.Buffered(1))

def shard_copies(loads, pieces, targets, sem, row, col, which):
    for n, (src, dst, fr, fc, rows, cols, slot, at, column, width) in enumerate(loads):
        if dst not in which:
            continue
        if rows is None:
            yield pltpu.make_async_copy(pieces[src], targets[dst], sem.at[n])
            continue
        r0 = pl.multiple_of((row ^ fr) * rows, 16)
        c0 = pl.multiple_of((col ^ fc) * cols + column, 128)
        yield pltpu.make_async_copy(
            pieces[src].at[slot, :, pl.ds(at, width)], targets[dst].at[pl.ds(r0, rows), pl.ds(c0, width)], sem.at[n]
        )


def qkv_kernel(loads, pairs, info_ref, x_ref, vec_ref, own_ref, came_ref, *refs):
    count = max(load[0] for load in loads) + 1
    pieces, refs = refs[:count], refs[count:]
    nT_ref, o_ref, mem_ref, bT_ref, wq_ref, wq_s, wm_s, in_sem, out_sem = refs
    i = pl.program_id(0)
    D = wq_s.shape[0]
    w, half = D // pairs, pairs // 2
    outs = []
    for n in range(3 * pairs):
        kind, p, j = n // pairs, n % pairs // 2, n % 2
        at = kind * D + (j * half + p) * w
        copy = pltpu.make_async_copy(wq_s.at[:, at : at + w], wq_ref.at[:, n * w : (n + 1) * w], out_sem.at[n])
        outs.append(copy)

    @pl.when(i == 0)
    def _():
        for begin in (True, False):
            for copy in shard_copies(loads, pieces, (wq_s, wm_s), in_sem, info_ref[2], info_ref[3], (0, 1)):
                copy.start() if begin else copy.wait()
        for out in outs:
            out.start()
        basis = (own_ref[...] + came_ref[...].astype(jnp.float32)).astype(jnp.bfloat16)
        bT_ref[...] = basis.T
        mem_ref[...] = dot_nn(basis, wm_s[...]).astype(jnp.bfloat16)

    xhat, _ = norm_parts(x_ref[...].astype(jnp.float32))
    n = (xhat * vec_ref[0:1] + vec_ref[1:2]).astype(jnp.bfloat16)
    nT_ref[...] = n.T
    o_ref[...] = dot_nn(n, wq_s[...]).astype(jnp.bfloat16)

    @pl.when(i == pl.num_programs(0) - 1)
    def _():
        for out in outs:
            out.wait()


def project_qkv(info, x, vec, own_basis, came_basis, pieces, loads, pairs, vmem, rows=256):
    S, D = x.shape
    nb = own_basis.shape[0]
    bf, sd = jnp.bfloat16, jax.ShapeDtypeStruct
    hbm = pl.BlockSpec(memory_space=pl.ANY)
    return pl.pallas_call(
        functools.partial(qkv_kernel, loads, pairs),
        grid_spec=pltpu.PrefetchScalarGridSpec(
            num_scalar_prefetch=1,
            grid=(S // rows,),
            in_specs=[pl.BlockSpec((rows, D), lambda i, info: (i, 0)), whole((8, D)), whole((nb, D)), whole((nb, D))]
            + [hbm] * len(pieces),
            out_specs=[
                pl.BlockSpec((D, rows), lambda i, info: (0, i)), pl.BlockSpec((rows, 3 * D), lambda i, info: (i, 0)),
                whole((nb, 2 * D)), whole((D, nb)), hbm,
            ],
            scratch_shapes=[
                pltpu.VMEM((D, 3 * D), bf), pltpu.VMEM((D, 2 * D), bf),
                pltpu.SemaphoreType.DMA((len(loads),)), pltpu.SemaphoreType.DMA((3 * pairs,)),
            ],
        ),
        out_shape=[sd((D, S), bf), sd((S, 3 * D), bf), sd((nb, 2 * D), bf), sd((D, nb), bf), sd((D, 3 * D), bf)],
        compiler_params=pltpu.CompilerParams(vmem_limit_bytes=vmem),
        cost_estimate=pl.CostEstimate(
            flops=6 * S * D * D + 4 * nb * D * D, bytes_accessed=10 * S * D + 16 * D * D, transcendentals=0
        ),
        name="project_qkv",
    )(info, x, vec, own_basis, came_basis, *pieces)


def row_slot(fr, order):
    return sum(((fr >> bit) & 1) << i for i, (axis, bit) in enumerate(order[:-1]) if axis == "row")


def col_slot(fc, order):
    return sum(((fc >> bit) & 1) << i for i, (axis, bit) in enumerate(order[:-1]) if axis == "col")


class _Fixed:
    def __init__(self, sem):
        self.at = self
        self.sem = sem

    def __getitem__(self, index):
        return self.sem


def mlp_kernel(steps, chunk, loads, cut, info_ref, c_ref, x_ref, g_ref, vec_ref, bf_ref, *refs):
    count = max(load[0] for load in loads) + 1
    pieces, refs = refs[:count], refs[count:]
    out_ref, dmid_ref, dctx_ref, gv_ref, gb_ref = refs[:5]
    made = 3 if cut is None else 4
    grads, refs = refs[5 : 5 + made], refs[5 + made :]
    n_s, nT_s, dm_s, mid_s, acc_s, dn_s, hid_s, dp_s, wf_s, wo_s, wp_s, go_s, gf_s, gp_s, in_sem, out_sem, go_sem = refs
    f = pl.program_id(0)
    S, D = x_ref.shape
    fb = gf_s.shape[2]
    length, base, row, col = info_ref[0], info_ref[1], info_ref[2], info_ref[3]
    nchunk = S // chunk
    buf = f % 2
    fe, per_col = f, steps
    if cut is not None:
        fe, per_col = f ^ (row // (cut[0] // steps)), steps // cut[1]

    def valid_of(i):
        pos = base + i * chunk + lax.broadcasted_iota(jnp.int32, (chunk, 1), 0)
        return jnp.where(pos < length, 1.0, 0.0)

    targets = (wf_s, wo_s, wp_s)

    def arrive(which, rows=None, cols=None):
        if cut is None:
            for copy in shard_copies(loads, pieces, targets, in_sem, row, col, which):
                copy.wait()
            return
        n_rows, n_cols = cut[:2]
        seen = set()
        for src, dst, _, _, height, across, slot, at, _, width in loads:
            if dst not in which or dst in seen:
                continue
            seen.add(dst)
            for r in range(n_rows) if rows is None else rows:
                for c in range(n_cols) if cols is None else cols:
                    n = (dst * n_rows + r) * n_cols + c
                    pltpu.make_async_copy(
                        pieces[src].at[slot, :, pl.ds(at, width)], targets[dst].at[:height, :width], in_sem.at[n]
                    ).wait()

    def depart(which, only=None):
        for n, load in enumerate(loads):
            if load[1] in which:
                place = n
                if cut is not None:
                    place = (load[1] * cut[0] + (row ^ load[2])) * cut[1] + (col ^ load[3])
                copy = next(shard_copies([load], pieces, targets, _Fixed(in_sem.at[place]), row, col, which))
                if only is None:
                    copy.start()
                else:
                    pl.when((col ^ load[3]) == only)(copy.start)

    def block_copies(begin, buf=buf):
        if cut is None:
            copies = [
                pltpu.make_async_copy(gf_s.at[buf], grads[0].at[:, pl.ds(pl.multiple_of(fe * fb, 128), fb)], out_sem.at[buf, 0]),
                pltpu.make_async_copy(gp_s.at[buf], grads[2].at[pl.ds(pl.multiple_of(fe * fb, 16), fb), :], out_sem.at[buf, 1]),
            ]
            for copy in copies:
                copy.start() if begin else copy.wait()
            return
        n_rows, n_cols, order2, order3 = cut
        rows2, rows3 = D // n_rows, fb * steps // n_rows
        cols2, cols3 = fb * steps // n_cols, D // n_cols
        per = cols2 // fb
        c = fe // per
        at = pl.multiple_of((fe % per) * fb, 128)
        for fr in range(n_rows):
            slot = row_slot(fr, order2) + col_slot(c ^ col, order2)
            src = gf_s.at[buf, pl.ds(pl.multiple_of((row ^ fr) * rows2, 16), rows2), :]
            copy = pltpu.make_async_copy(src, grads[fr & 1].at[slot, :, pl.ds(at, fb)], out_sem.at[buf, fr])
            copy.start() if begin else copy.wait()
        n = n_rows
        for i in range(fb // rows3):
            rel = (fe * (fb // rows3) + i) ^ row
            for c in range(n_cols):
                slot = row_slot(rel, order3) + col_slot(c ^ col, order3)
                src = gp_s.at[buf, i * rows3 : (i + 1) * rows3, c * cols3 : (c + 1) * cols3]
                if begin:
                    for side in range(2):

                        @pl.when(rel & 1 == side)
                        def _():
                            pltpu.make_async_copy(src, grads[2 + side].at[slot], out_sem.at[buf, n]).start()
                else:
                    pltpu.make_async_copy(src, grads[2].at[0], out_sem.at[buf, n]).wait()
                n += 1

    @pl.when(f == 0)
    def _():
        depart((1,))
        if cut is None:
            depart((0, 2))
        else:
            depart((0,), fe // per_col)
        for i in range(nchunk):
            rs = slice(i * chunk, (i + 1) * chunk)
            dm_s[rs, :] = (g_ref[rs, :].astype(jnp.float32) * valid_of(i)).astype(jnp.bfloat16)
        acc_s[...] = jnp.zeros_like(acc_s)
        dn_s[...] = jnp.zeros_like(dn_s)
        if cut is not None:
            depart((2,))
            for c in range(1, cut[1]):
                depart((0,), fe // per_col ^ c)
        arrive((1,))
        for i in range(nchunk):
            rs = slice(i * chunk, (i + 1) * chunk)
            branch = dot_nn(c_ref[rs, :], wo_s[...]) + vec_ref[2:3]
            mid = x_ref[rs, :].astype(jnp.float32) + valid_of(i) * branch
            mid_s[rs, :] = mid
            xhat, _ = norm_parts(mid)
            n = (xhat * vec_ref[0:1] + vec_ref[1:2]).astype(jnp.bfloat16)
            n_s[rs, :] = n
            nT_s[:, rs] = n.T
        if cut is None:
            arrive((0, 2))

    if cut is not None:

        @pl.when(f % per_col == 0)
        def _():
            arrive((0,), None, [fe // per_col])

        each = cut[0] // steps
        arrive((2,), [fe * each + i for i in range(each)])

    @pl.when(f >= 2)
    def _():
        block_copies(False)

    cs = pl.ds(pl.multiple_of(fe * fb, 128), fb)
    wf = wf_s[:, cs]
    wp = wp_s[cs, :]
    c0 = math.sqrt(2.0 / math.pi)
    gb = jnp.zeros((1, fb), jnp.float32)
    for i in range(nchunk):
        rs = slice(i * chunk, (i + 1) * chunk)
        pre = dot_nn(n_s[rs, :], wf) + bf_ref[...]
        sq = pre * pre
        t = jnp.tanh(c0 * pre * (1.0 + 0.044715 * sq))
        hp = 0.5 * pre
        hid = hp + hp * t
        dgel = 0.5 + 0.5 * t + hp * (1.0 - t * t) * (c0 * (1.0 + (3 * 0.044715) * sq))
        hidb = hid.astype(jnp.bfloat16)
        hid_s[rs, :] = hidb
        acc_s[rs, :] += dot_nn(hidb, wp)
        dpb = (dot_nt(dm_s[rs, :], wp) * dgel).astype(jnp.bfloat16)
        dp_s[rs, :] = dpb
        gb = gb + jnp.sum(dpb.astype(jnp.float32), axis=0, keepdims=True)
        dn_s[rs, :] += dot_nt(dpb, wf)
    gb_ref[...] = jnp.broadcast_to(gb, gb_ref.shape)
    gf_s[buf] = dot_nn(nT_s[...], dp_s[...]).astype(jnp.bfloat16)
    gp_s[buf] = dot_tn(hid_s[...], dm_s[...]).astype(jnp.bfloat16)
    block_copies(True)

    @pl.when(f == steps - 1)
    def _():
        gg = jnp.zeros((1, D), jnp.float32)
        gbi, gbo, gbp = gg, gg, gg
        for i in range(nchunk):
            rs = slice(i * chunk, (i + 1) * chunk)
            valid = valid_of(i)
            mid = mid_s[rs, :]
            out_ref[rs, :] = (mid + valid * (acc_s[rs, :] + vec_ref[3:4])).astype(jnp.bfloat16)
            xhat, rstd = norm_parts(mid)
            dn = dn_s[rs, :]
            cot = dm_s[rs, :].astype(jnp.float32)
            dmid = cot + norm_back(dn * vec_ref[0:1], xhat, rstd)
            dmid_ref[rs, :] = dmid
            db = (valid * dmid).astype(jnp.bfloat16)
            gg = gg + jnp.sum(dn * xhat, axis=0, keepdims=True)
            gbi = gbi + jnp.sum(dn, axis=0, keepdims=True)
            gbo = gbo + jnp.sum(db.astype(jnp.float32), axis=0, keepdims=True)
            gbp = gbp + jnp.sum(cot, axis=0, keepdims=True)
            n_s[rs, :] = db
        go_s[...] = dot_tn(c_ref[...], n_s[...]).astype(jnp.bfloat16)
        copies = []
        if cut is None:
            copies.append(pltpu.make_async_copy(go_s, grads[1], go_sem.at[0]))
        else:
            n_rows, n_cols, order2, _ = cut
            rows, cols = D // n_rows, D // n_cols
            at = fb * steps // n_cols
            for fr in range(n_rows):
                for c in range(n_cols):
                    slot = row_slot(fr, order2) + col_slot(c ^ col, order2)
                    src = go_s.at[pl.ds(pl.multiple_of((row ^ fr) * rows, 16), rows), c * cols : (c + 1) * cols]
                    dst = grads[fr & 1].at[slot, :, at : at + cols]
                    copies.append(pltpu.make_async_copy(src, dst, go_sem.at[len(copies)]))
        for copy in copies:
            copy.start()
        for i in range(nchunk):
            rs = slice(i * chunk, (i + 1) * chunk)
            dctx_ref[rs, :] = dot_nt(n_s[rs, :], wo_s[...]).astype(jnp.bfloat16)
        gv_ref[...] = jnp.concatenate([gbo, gg, gbi, gbp, jnp.zeros((4, D), jnp.float32)], axis=0)
        for copy in copies:
            copy.wait()
        for slot in range(min(2, steps)):
            block_copies(False, slot)


def mlp_block(info, context, x, d_out, pieces, loads, vec, b_fc, cut, widths, vmem, fb=768, chunk=256):
    S, D = x.shape
    FF = b_fc.shape[1]
    steps = FF // fb
    bf, f32, sd = jnp.bfloat16, jnp.float32, jax.ShapeDtypeStruct
    hbm = pl.BlockSpec(memory_space=pl.ANY)
    if cut is None:
        grads = [sd((D, FF), bf), sd((D, D), bf), sd((FF, D), bf)]
        n_in, n_out, n_go = len(loads), 2, 1
    else:
        n_rows, n_cols = cut[:2]
        half = n_rows * n_cols // 2
        grads = [sd((half, D // n_rows, sum(widths)), bf)] * 2 + [sd((half, FF // n_rows, D // n_cols), bf)] * 2
        n_in = 3 * n_rows * n_cols
        n_out, n_go = n_rows + fb * n_rows // FF * n_cols, n_rows * n_cols
    if cut is None:
        at = lambda f, info: (0, f)
    else:
        at = lambda f, info: (0, f ^ (info[2] // (n_rows // steps)))
    spec = pltpu.PrefetchScalarGridSpec(
        num_scalar_prefetch=1,
        grid=(steps,),
        in_specs=[whole((S, D))] * 3 + [whole((8, D)), pl.BlockSpec((1, fb), at)] + [hbm] * len(pieces),
        out_specs=[whole((S, D))] * 3 + [whole((8, D)), pl.BlockSpec((8, fb), at)] + [hbm] * len(grads),
        scratch_shapes=[
            pltpu.VMEM((S, D), bf), pltpu.VMEM((D, S), bf), pltpu.VMEM((S, D), bf),
            pltpu.VMEM((S, D), f32), pltpu.VMEM((S, D), f32), pltpu.VMEM((S, D), f32),
            pltpu.VMEM((S, fb), bf), pltpu.VMEM((S, fb), bf),
            pltpu.VMEM((D, FF), bf), pltpu.VMEM((D, D), bf), pltpu.VMEM((FF, D), bf), pltpu.VMEM((D, D), bf),
            pltpu.VMEM((2, D, fb), bf), pltpu.VMEM((2, fb, D), bf),
            pltpu.SemaphoreType.DMA((n_in,)), pltpu.SemaphoreType.DMA((2, n_out)), pltpu.SemaphoreType.DMA((n_go,)),
        ],
    )
    return pl.pallas_call(
        functools.partial(mlp_kernel, steps, chunk, loads, cut),
        grid_spec=spec,
        out_shape=[sd((S, D), bf), sd((S, D), f32), sd((S, D), bf), sd((8, D), f32), sd((8, FF), f32)] + grads,
        compiler_params=pltpu.CompilerParams(vmem_limit_bytes=vmem, dimension_semantics=("arbitrary",)),
        cost_estimate=pl.CostEstimate(
            flops=12 * S * D * FF + 6 * S * D * D, bytes_accessed=8 * D * FF + 20 * S * D, transcendentals=S * FF
        ),
        name="mlp_block",
    )(info, context, x, d_out, vec, b_fc, *pieces)


def wgrad_kernel(cut, count, split, info_ref, nT_ref, bT_ref, *refs):
    n_rows, n_cols = cut
    parts, outs, (g_s, sem) = refs[: 5 * count], refs[5 * count : -2], refs[-2:]
    D = nT_ref.shape[0]
    rows, w = D // n_rows, parts[0].shape[1] // 2
    row, col = info_ref[2], info_ref[3]
    copies = []
    nT, bT = nT_ref[...], bT_ref[...]
    for c in range(n_cols):
        at = 0
        for p in range(count):
            q_ref, k_ref, v_ref, mk_ref, mv_ref = parts[5 * p : 5 * p + 5]
            if c == 0:
                terms = [(nT, q_ref[...]), (nT, k_ref[:, :w]), (bT, mk_ref[...])]
            else:
                terms = [(nT, k_ref[:, w:]), (nT, v_ref[...]), (bT, mv_ref[...])]
            for left, right in terms:
                g_s[c, :, at : at + right.shape[1]] = dot_nn(left, right).astype(jnp.bfloat16)
                at += right.shape[1]
        at = 0
        for i, (width, order) in enumerate(split):
            for fr in range(n_rows):
                slot = row_slot(fr, order) + col_slot(c ^ col, order)
                block = g_s.at[c, pl.ds(pl.multiple_of((row ^ fr) * rows, 16), rows), at : at + width]
                copies.append(pltpu.make_async_copy(block, outs[2 * i + (fr & 1)].at[slot], sem.at[len(copies)]))
                copies[-1].start()
            at += width
    for copy in copies:
        copy.wait()


def weight_grads(info, nT, bT, parts, n_rows, split, vmem):
    D, S = nT.shape
    nb, w, n_cols, count = bT.shape[1], parts[0][0].shape[1] // 2, 2, len(parts)
    rows = D // n_rows
    flat = [d for part in parts for d in part]
    bf, hbm = jnp.bfloat16, pl.BlockSpec(memory_space=pl.ANY)
    outs = []
    for width, _ in split:
        outs += [jax.ShapeDtypeStruct((n_rows * n_cols // 2, rows, width), bf)] * 2
    outs = pl.pallas_call(
        functools.partial(wgrad_kernel, (n_rows, n_cols), count, split),
        grid_spec=pltpu.PrefetchScalarGridSpec(
            num_scalar_prefetch=1,
            grid=(1,),
            in_specs=[whole(a.shape) for a in [nT, bT] + flat],
            out_specs=[hbm] * len(outs),
            scratch_shapes=[
                pltpu.VMEM((n_cols, D, 5 * w * count), bf), pltpu.SemaphoreType.DMA((n_rows * n_cols * len(split),)),
            ],
        ),
        out_shape=outs,
        compiler_params=pltpu.CompilerParams(vmem_limit_bytes=vmem),
        cost_estimate=pl.CostEstimate(
            flops=12 * S * D * w * count, bytes_accessed=14 * S * w * count + 2 * S * D + 20 * D * w * count, transcendentals=0
        ),
        name="weight_grads",
    )(info, nT, bT, *flat)
    return [Scatter(outs[2 * i], outs[2 * i + 1], order) for i, (_, order) in enumerate(split)]


def tokens_kernel(count,w_ref,x_ref,dm_ref,gain_ref,*refs):
    o_ref,gv_ref=refs[-2:]
    i=pl.program_id(0); D=x_ref.shape[1]; width=D//(2*count)
    dn=None
    for kind in range(3):
        for p in range(count):
            at=kind*D+2*p*width
            term=dot_nt(refs[3*p+kind][...],w_ref[:,at:at+2*width])
            dn=term if dn is None else dn+term
    xhat,rstd=norm_parts(x_ref[...].astype(jnp.float32))
    o_ref[...]=dm_ref[...]+norm_back(dn*gain_ref[...],xhat,rstd)
    @pl.when(i==0)
    def _(): gv_ref[...]=jnp.zeros_like(gv_ref)
    gv_ref[0:1]+=jnp.sum(dn*xhat,axis=0,keepdims=True)
    gv_ref[1:2]+=jnp.sum(dn,axis=0,keepdims=True)

def token_grad(parts,w,x,d_middle,gain,vmem,rows=256):
    S,D=x.shape; count=len(parts); width=D//count
    by_row=lambda width: pl.BlockSpec((rows,width),lambda i:(i,0))
    return pl.pallas_call(functools.partial(tokens_kernel,count),grid=(S//rows,),
        in_specs=[whole((D,3*D)),by_row(D),by_row(D),whole((1,D))]+[by_row(width)]*(3*count),
        out_specs=[by_row(D),pl.BlockSpec((8,D),lambda i:(0,0))],
        out_shape=[jax.ShapeDtypeStruct((S,D),jnp.float32),jax.ShapeDtypeStruct((8,D),jnp.float32)],
        compiler_params=pltpu.CompilerParams(vmem_limit_bytes=vmem),
        cost_estimate=pl.CostEstimate(flops=6*S*D*D,bytes_accessed=16*S*D+6*D*D,transcendentals=0),name="token_grad")(w,x,d_middle,gain,*[d for part in parts for d in part])


VMEM_BYTES = 58 << 20
MLP_VMEM_BYTES = 50 << 20
FIT_NODE_COUNT = 512
ridge = 0.5


def fit_constant(nb):
    centers = (np.arange(nb, dtype=np.float64) + 0.5) / nb
    times = (np.arange(FIT_NODE_COUNT, dtype=np.float64) + 0.5) / FIT_NODE_COUNT
    design = np.exp(-0.5 * (times[None, :] - centers[:, None]) ** 2 * (nb * nb))
    table = np.linalg.solve(design @ design.T + ridge * np.eye(nb), design).astype(np.float32)
    hi = table.astype(jnp.bfloat16)
    lo = (table - hi.astype(np.float32)).astype(jnp.bfloat16)
    return np.concatenate([hi, lo], axis=0)


def bits_of(n):
    count = n.bit_length() - 1
    assert 1 << count == n
    return count


def swap(block, stage):
    axis, bit = stage
    n = lax.axis_size(axis)
    return lax.ppermute(block, axis, [(i, i ^ (1 << bit)) for i in range(n)])


class Chain:
    def __init__(self):
        self.last = ()

    def wait(self, *values):
        got = lax.optimization_barrier(values + self.last)
        self.last = got[:1]
        return got[0] if len(values) == 1 else got[: len(values)]


def stage_lists():
    rows = bits_of(lax.axis_size("row"))
    cols = bits_of(lax.axis_size("col"))
    far = [("row", b) for b in range(rows - 1, 1, -1)]
    col = [("col", b) for b in range(cols - 1, -1, -1)]
    near = [("row", 1)] if rows > 1 else []
    return far, col, near, [("row", 0)]


def slot_offsets(order):
    table = []
    for slot in range(1 << len(order)):
        flips = {"row": 0, "col": 0}
        for i, (axis, bit) in enumerate(order):
            if slot >> i & 1:
                flips[axis] ^= 1 << bit
        table.append((flips["row"], flips["col"]))
    return table


def place_bits():
    rows, cols = bits_of(lax.axis_size("row")), bits_of(lax.axis_size("col"))
    return [("row", b) for b in range(rows - 1, -1, -1)] + [("col", b) for b in range(cols - 1, -1, -1)]


def by_place(slots, order):
    seen = order[::-1]
    dims = [seen.index(p) for p in place_bits()]
    split = slots.reshape((2,) * len(order) + slots.shape[1:])
    tail = range(len(order), split.ndim)
    return split.transpose(dims + list(tail)).reshape(slots.shape)


def by_slot(blocks, order):
    places = place_bits()
    dims = [places.index(p) for p in order[::-1]]
    split = blocks.reshape((2,) * len(order) + blocks.shape[1:])
    tail = range(len(order), split.ndim)
    return split.transpose(dims + list(tail)).reshape(blocks.shape)


def flipped(blocks, row, col):
    places = place_bits()
    split = blocks.reshape((2,) * len(places) + blocks.shape[1:])
    for dim, (axis, bit) in enumerate(places):
        mine = (row if axis == "row" else col) >> bit & 1
        split = jnp.where(mine == 1, jnp.flip(split, dim), split)
    return split.reshape(blocks.shape)


class Gather:
    def __init__(self, block, order, done=0):
        self.held, self.order, self.done = (block if done else block[None]), order, done

    def send(self):
        self.came = swap(self.held, self.order[self.done])
        return self

    def take(self, came):
        self.done += 1
        if self.done == len(self.order):
            self.came = came
        else:
            self.held = jnp.concatenate([self.held, came], axis=0)
        return self

    def halves(self, cut, orders):
        return [
            Gather(self.held[:, :, :cut], orders[0], self.done),
            Gather(self.held[:, :, cut:], orders[1], self.done),
        ]


def advance(chain, *gathers):
    got = chain.wait(*[g.came for g in gathers])
    got = got if len(gathers) > 1 else (got,)
    for g, came in zip(gathers, got):
        g.take(came)
        if g.done < len(g.order):
            g.send()


def copy_kernel(plans, place_ref, *refs):
    sem = refs[-1]
    copies = []
    for src, dst, fr, fc, rows, cols, slot, at, column, width, outward in plans:
        r = place_ref[0] ^ fr
        c = place_ref[1] ^ fc
        matrix, slots = (refs[dst], refs[src]) if outward else (refs[src], refs[dst])
        block = matrix.at[
            pl.ds(pl.multiple_of(r * rows, 8), rows), pl.ds(pl.multiple_of(c * cols + column, 128), width)
        ]
        piece = slots.at[slot, :, pl.ds(at, width)]
        pair = (piece, block) if outward else (block, piece)
        copies.append(pltpu.make_async_copy(*pair, sem.at[len(copies)]))
    for copy in copies:
        copy.start()
    for copy in copies:
        copy.wait()


def copy_call(plans, place, ins, out_shapes, resident, name):
    hbm = pl.BlockSpec(memory_space=pl.ANY)
    size = sum(math.prod(o.shape) for o in out_shapes)
    return pl.pallas_call(
        functools.partial(copy_kernel, plans),
        grid_spec=pltpu.PrefetchScalarGridSpec(
            num_scalar_prefetch=1,
            grid=(1,),
            in_specs=[hbm] * len(ins),
            out_specs=[whole(o.shape) if resident else hbm for o in out_shapes],
            scratch_shapes=[pltpu.SemaphoreType.DMA((len(plans),))],
        ),
        out_shape=out_shapes,
        compiler_params=pltpu.CompilerParams(vmem_limit_bytes=24 << 20),
        cost_estimate=pl.CostEstimate(flops=0, bytes_accessed=4 * size, transcendentals=0),
        name=name,
    )(place, *ins)


def ranges_of(layout, offset, width):
    found, at = [], 0
    for i, size in enumerate(layout):
        low, high = max(at, offset), min(at + size, offset + width)
        if low < high:
            found.append((i, low - offset, low - at, high - low))
        at += size
    return found


def assemble(place, gathers, layout, n_rows, n_cols):
    rows = gathers[0].held.shape[1]
    shapes = [jax.ShapeDtypeStruct((rows * n_rows, w * n_cols), jnp.bfloat16) for w in layout]
    pieces, plans, offset = [], [], 0
    aligned = rows % 8 == 0 and all(w % 128 == 0 for w in layout)
    if not aligned:
        full = []
        for g in gathers:
            slots = jnp.concatenate([g.held, g.came], axis=0)
            full.append(flipped(by_place(slots, g.order), place[0], place[1]))
        full = jnp.concatenate(full, axis=2)
        res, at = [], 0
        for w in layout:
            block = full[:, :, at : at + w].reshape(n_rows, n_cols, rows, w)
            res.append(block.transpose(0, 2, 1, 3).reshape(rows * n_rows, w * n_cols))
            at += w
        return res
    for g in gathers:
        table = slot_offsets(g.order)
        width = g.held.shape[2]
        for slot, (fr, fc) in enumerate(table):
            src = len(pieces) + slot // (len(table) // 2)
            for i, at, column, w in ranges_of(layout, offset, width):
                plans.append((src, i, fr, fc, rows, layout[i], slot % (len(table) // 2), at, column, w, True))
        pieces += [g.held, g.came]
        offset += width
    plans = [(p[0], len(pieces) + p[1]) + p[2:] for p in plans]
    return copy_call(plans, place, pieces, shapes, True, "assemble")


class Scatter:
    def __init__(self, keep, send, order):
        self.order, self.left = order, len(order)
        self.terms, self.out = [keep], send
        self.total = None

    def send(self):
        self.left -= 1
        self.came = swap(self.out, self.order[self.left])
        return self

    def take(self, came):
        self.terms.append(came)
        if self.left == 0:
            self.total = sum(t.astype(jnp.float32) for t in self.terms)[0]
            return self
        half = self.terms[0].shape[0] // 2
        self.out = sum(t[half:].astype(jnp.float32) for t in self.terms).astype(jnp.bfloat16)
        self.terms = [t[:half] for t in self.terms]
        return self


def onward(chain, *scatters):
    got = chain.wait(*[s.came for s in scatters])
    got = got if len(scatters) > 1 else (got,)
    for s, came in zip(scatters, got):
        s.take(came)
        if s.left:
            s.send()


def disperse(place, grads, cuts, n_rows, n_cols):
    rows = grads[0].shape[0] // n_rows
    blocks = [g.reshape(n_rows, rows, n_cols, -1).transpose(0, 2, 1, 3) for g in grads]
    joined = jnp.concatenate(blocks, axis=3).reshape(n_rows * n_cols, rows, -1)
    joined = flipped(joined, place[0], place[1])
    res, offset = [], 0
    for width, order in cuts:
        slots = by_slot(joined[:, :, offset : offset + width], order)
        res.append(Scatter(slots[: len(slots) // 2], slots[len(slots) // 2 :], order))
        offset += width
    return res


def shards(
    tokens, w_qkv, w_out, w_mem, w_fc, w_proj, gain_attn, bias_attn, gain_mlp, bias_mlp, b_out, b_fc, b_proj,
    w_loc, w_spread, past_states, sticky_pos, seq_lengths, d_out,
):
    bf, f32 = jnp.bfloat16, jnp.float32
    n_rows, n_cols = lax.axis_size("row"), lax.axis_size("col")
    row, col = lax.axis_index("row"), lax.axis_index("col")
    place = jnp.stack([row, col]).astype(jnp.int32)
    batches, _, span, feat = tokens.shape
    heads, nb = w_loc.shape[0], w_loc.shape[1] * n_rows * n_cols
    hidden = w_fc.shape[1] * n_cols
    assert batches == 2 and n_cols % 2 == 0
    side = col % 2
    own, other = side, 1 - side
    first = (col - side) * span
    far, along, near, core = stage_lists()
    zyx, zxy, yzx = far + along + near + core, far + near + along + core, along + far + near + core
    devices = n_rows * n_cols

    def pick(a, i):
        return lax.dynamic_index_in_dim(a, i, 0, keepdims=False)

    def to_chunk(mine, came):
        two = jnp.stack([mine, came])
        return jnp.where(side == 0, two, two[::-1]).reshape((2 * span,) + mine.shape[1:])

    def trade(a):
        return swap(a, ("col", 0))

    tokens, past, d_out = tokens[:, 0], past_states[:, 0], d_out[:, 0]
    sticky, lengths = sticky_pos[:, 0], seq_lengths[:, 0]
    length = pick(lengths, own)
    info = jnp.stack([length, first, row, col]).astype(jnp.int32)

    singles = [gain_attn, bias_attn, gain_mlp, bias_mlp, b_out, b_proj, b_fc]
    n_single, n_small = len(singles), len(singles) + heads
    rows_small = -(-n_small // 8) * 8
    both_w = jnp.concatenate([w_loc, w_spread], axis=1)

    def wide(v):
        v = v.reshape(-1, v.shape[-1])
        return jnp.pad(v, ((0, 0), (0, 128 - v.shape[1])))

    layout1 = [w_qkv.shape[1], w_mem.shape[1]]
    layout2 = [w_fc.shape[1], w_out.shape[1]]
    layout3 = [w_proj.shape[1]]
    width1 = sum(layout1)
    cut1 = (width1 // 128 + 1) // 2 * 128
    rows1 = w_qkv.shape[0]
    fb = 768
    direct = n_cols == 2 and all(w % 128 == 0 for w in layout1 + layout2 + layout3) and rows1 % 16 == 0
    steps = hidden // fb
    direct = direct and layout2[0] % fb == 0 and fb % w_proj.shape[0] == 0 and steps & (steps - 1) == 0

    def loads_of(gathers, layout, base, first):
        loads, pieces, offset = [], [], 0
        for g in gathers:
            table = slot_offsets(g.order)
            half, width = len(table) // 2, g.held.shape[2]
            for slot, (fr, fc) in enumerate(table):
                for i, at, column, w in ranges_of(layout, offset, width):
                    src = first + len(pieces) + slot // half
                    loads.append((src, base + i, fr, fc, g.held.shape[1], layout[i], slot % half, at, column, w))
            pieces += [g.held, g.came]
            offset += width
        return loads, pieces

    chain = Chain()
    g1 = Gather(jnp.concatenate([w_qkv, w_mem], axis=1), zyx).send()
    tokens_out, block2 = chain.wait(tokens, jnp.concatenate([w_fc, w_out], axis=1))
    came_tokens = trade(pick(tokens_out, other))
    g2 = Gather(block2, yzx).send()
    g3 = Gather(w_proj, zxy)
    flat = jnp.concatenate([wide(v) for v in singles + [both_w]])
    flat = jnp.pad(flat, ((0, rows_small - n_small), (0, 0)))
    g0 = None
    for _ in far[1:]:
        advance(chain, g1)
        if g0 is None:
            g0 = Gather(chain.wait(flat), zyx).send()
    g1.take(chain.wait(g1.came))
    g1a, g1b = g1.halves(cut1, (zyx, zxy))
    g1a.send()
    g1b.send()
    advance(chain, g0)
    g3.held = chain.wait(g3.held)
    g3.send()
    for _ in far[1:]:
        advance(chain, g3)
    for _ in along:
        advance(chain, g2)
    advance(chain, g0)
    advance(chain, g1b, g1a)

    fit = jnp.asarray(fit_constant(nb))
    here = col * span
    past, sticky = chain.wait(past, sticky)

    def basis_part(i):
        spots = pick(sticky, i) - here
        resident = (spots >= 0) & (spots < span)
        picked = jnp.take(past.reshape(-1, feat), jnp.clip(spots, 0, span - 1) + i * span, axis=0)
        parts = jnp.dot(fit * resident.astype(bf)[None, :], picked, preferred_element_type=f32)
        return parts[:nb] + parts[nb:]

    came_g3 = chain.wait(g3.came)
    if n_cols == 2:
        own_basis, basis_out = chain.wait(basis_part(own), basis_part(other).astype(bf))
    else:
        both = lax.psum(jnp.stack([basis_part(i).astype(bf) for i in range(2)]), "col")
        own_basis, came_basis = pick(both, own).astype(f32), jnp.zeros((nb, feat), bf)
    advance(chain, g0)
    for _ in far[1:]:
        advance(chain, g2)
    x = to_chunk(pick(tokens, own), chain.wait(came_tokens))
    while g1b.done < len(g1b.order) - 1:
        advance(chain, g1b, g1a)
    if n_cols == 2:
        came_basis = trade(chain.wait(basis_out))
    g3.take(chain.wait(came_g3)).send()
    came_out = trade(chain.wait(pick(d_out, other)))
    while g0.done < len(g0.order) - 1:
        advance(chain, g0)
    g0.came = chain.wait(g0.came)
    every = flipped(by_place(jnp.concatenate([g0.held, g0.came], axis=0), zyx), row, col)
    share, width = w_loc.shape[1], gain_attn.shape[0]

    def rows_of(first, count):
        return every[:, first : first + count, :width].transpose(1, 0, 2).reshape(count, feat).astype(f32)

    vec1 = jnp.pad(rows_of(0, 2), ((0, 6), (0, 0)))
    advance(chain, g2)
    x, vec1 = chain.wait(x, vec1)
    g1b.came, g1a.came, came_basis = chain.wait(g1b.came, g1a.came, came_basis)

    if direct:
        loads, pieces = loads_of([g1a, g1b], layout1, 0, 0)
    else:
        pieces = assemble(place, [g1a, g1b], layout1, n_rows, n_cols)
        loads = [(i, i) + (None,) * 8 for i in range(2)]
    nT, qkv, mem_kv, basisT, wq = project_qkv(info, x, vec1, own_basis, came_basis, pieces, loads, heads // 2, VMEM_BYTES)
    qkv, every = chain.wait(qkv, every)
    vec2 = jnp.pad(rows_of(2, 4), ((0, 4), (0, 0)))
    bfc = every[:, n_single - 1, : b_fc.shape[0]].astype(f32).reshape(1, -1)
    loc, spr = [
        every[:, n_single:n_small, at : at + share].transpose(1, 0, 2).reshape(heads // 2, 2, nb) for at in (0, share)
    ]
    wls = jnp.concatenate([loc, spr, jnp.zeros((heads // 2, 4, nb), bf)], axis=1)
    for _ in along[:1]:
        advance(chain, g3)
    g_other = chain.wait(came_out)
    halo = 0 if n_cols == 2 else WINDOW
    pairs = heads // 2
    route = [(i, i + 2) for i in range(n_cols - 2)]
    back = [(i + 2, i) for i in range(n_cols - 2)]
    if halo:
        before = lax.ppermute(qkv[-halo:, feat:], "col", route)
        kvx = jnp.concatenate([before, qkv[:, feat:]], axis=0)
        kv = (kvx, 0, kvx, pairs)
    else:
        kv = (qkv, pairs, qkv, 2 * pairs)
    mem_kv, g2.held, g3.held = chain.wait(mem_kv, g2.held, g3.held)
    context, lse = attention_forward(info, qkv, kv, halo, mem_kv, wls, heads, VMEM_BYTES)
    context = chain.wait(context)
    while g3.done < len(g3.order) - 1:
        advance(chain, g3)
    while g2.done < len(g2.order) - 1:
        advance(chain, g2)
    g_chunk = to_chunk(pick(d_out, own), g_other)
    g3.came, g2.came = chain.wait(g3.came, g2.came)

    if direct:
        loads, pieces = loads_of([g2], layout2, 0, 0)
        loads3, pieces3 = loads_of([g3], layout3, 2, len(pieces))
        loads = loads + loads3
        pieces = [pltpu.with_memory_space_constraint(piece, pltpu.VMEM) for piece in pieces + pieces3]
    else:
        wf, wo = assemble(place, [g2], layout2, n_rows, n_cols)
        wp = assemble(place, [g3], layout3, n_rows, n_cols)[0]
        pieces = [wf, wo, wp]
        loads = [(i, i) + (None,) * 8 for i in range(3)]
    output, d_middle, d_context, g_vec, g_bfc, *cut_grads = mlp_block(
        info, context, x, g_chunk, pieces, loads, vec2, bfc,
        (n_rows, n_cols, yzx, zxy) if direct else None, layout2, MLP_VMEM_BYTES, fb,
    )

    def from_chunk(chunk):
        halves = chunk.reshape(2, span, feat)
        return pick(halves, own), pick(halves, other)

    def paired(kept, came):
        two = jnp.stack([kept, came])
        return jnp.where(side == 0, two, two[::-1])[:, None]

    if direct:
        s2, s3 = Scatter(*cut_grads[:2], yzx), Scatter(*cut_grads[2:], zxy)
    else:
        s2 = disperse(place, cut_grads[:2], [(sum(layout2), yzx)], n_rows, n_cols)[0]
        s3 = disperse(place, cut_grads[2:], [(sum(layout3), zxy)], n_rows, n_cols)[0]
    s2.send()
    s3.send()
    d_context, s2.terms[0], s3.terms[0] = chain.wait(d_context, s2.terms[0], s3.terms[0])

    def taken(*scatters):
        got = chain.wait(*[s.came for s in scatters])
        for s, came in zip(scatters, got if len(scatters) > 1 else (got,)):
            s.take(came)
        outs = chain.wait(*[s.out for s in scatters])
        for s, out in zip(scatters, outs if len(scatters) > 1 else (outs,)):
            s.out = out
            s.send()

    count = pairs // 2
    mixed, parts = [], []
    kept_out, sent = from_chunk(output)
    d_context, sent = chain.wait(d_context, sent)
    came_output = trade(sent)
    for i in range(count):
        d_context = chain.wait(d_context)
        got = list(
            attention_backward(info, qkv, kv, halo, mem_kv, wls, lse, d_context, heads, VMEM_BYTES, i, 2, count)
        )
        got[0] = chain.wait(got[0])
        mixed.append(got)
        d_q, d_k, d_v, d_mk, d_mv, _ = got
        if halo:
            d_kv = jnp.concatenate([d_k, d_v], axis=1)
            ret = lax.ppermute(d_kv[:halo], "col", back)
            d_kv = d_kv[halo:].astype(f32) + jnp.pad(ret.astype(f32), ((2 * span - halo, 0), (0, 0)))
            d_kv = d_kv.astype(bf)
            d_k, d_v = jnp.split(d_kv, 2, axis=1)
        parts.append((d_q, d_k, d_v, d_mk, d_mv))
        if i == 0:
            came_output = chain.wait(came_output)
            taken(s2, s3)
        if i == count - 2 and direct:
            s1 = weight_grads(info, nT, basisT, parts, n_rows, [(len(parts) * 5 * (feat // pairs), zyx)], VMEM_BYTES)
            s1[0].send()
            s1[0].terms[0] = chain.wait(s1[0].terms[0])
    taken(s3)
    taken(s2)
    if direct:
        taken(s1[0])
    d_middle = chain.wait(d_middle)
    d_tok, g_vec1 = token_grad([p[:3] for p in parts], wq, x, d_middle, vec1[0:1], VMEM_BYTES)
    d_tok, g_vec1 = chain.wait(d_tok, g_vec1)
    taken(s3)
    taken(s2)
    kept_x, sent_x = from_chunk(d_tok)
    came_x = trade(chain.wait(sent_x.astype(bf)))
    nT = chain.wait(nT)
    if direct:
        s1 += weight_grads(info, nT, basisT, parts[-1:], n_rows, [(5 * (feat // pairs), zyx)], VMEM_BYTES)
        s1[1].send()
    else:
        ordered = [jnp.stack([p[k].reshape(p[k].shape[0], 2, -1) for p in parts], axis=2) for k in range(5)]
        ordered = [a.reshape(a.shape[0], feat) for a in ordered]
        g_qkv = jnp.dot(nT, jnp.concatenate(ordered[:3], axis=1), preferred_element_type=f32).astype(bf)
        g_mem = jnp.dot(basisT, jnp.concatenate(ordered[3:], axis=1), preferred_element_type=f32).astype(bf)
        s1 = disperse(place, [g_qkv, g_mem], [(cut1, zyx), (width1 - cut1, zxy)], n_rows, n_cols)
        for s_ in s1:
            s_.send()
    s1[-1].terms[0] = chain.wait(s1[-1].terms[0])
    by_pair = [m[5][j] for j in range(2) for m in mixed]
    total = jnp.concatenate([g_vec, g_vec1, g_bfc] + by_pair, axis=1)
    stages = core + far + along + near
    came = swap(total.astype(bf), stages.pop(0))
    last, early = s1[-1], s1[0]
    everyone = [last, early, s3, s2]
    plan = [last, came_x, early, None, last, s3, early, None, last, s2, early, None, last, s3, None, last, s2, None, early]
    while any(s_.total is None for s_ in everyone) or came is not None:
        s_ = plan.pop(0) if plan else next((s_ for s_ in everyone if s_.total is None), None)
        if s_ is came_x:
            came_x = chain.wait(came_x)
        elif s_ is None:
            if came is not None:
                total = total + chain.wait(came).astype(f32)
                came = swap(total.astype(bf), stages.pop(0)) if stages else None
        elif s_.left:
            onward(chain, s_)
        elif s_.total is None:
            s_.take(chain.wait(s_.came))
    index = row * n_cols + col

    def mine(block, first, width):
        return lax.dynamic_slice_in_dim(block, first + index * width, width, axis=1)

    g_bo, g_gain2, g_bias2, g_bp = mine(total, 0, gain_mlp.shape[0])[:4]
    g_gain1, g_bias1 = mine(total, feat, gain_attn.shape[0])[:2]
    g_bf = mine(total, 2 * feat, b_fc.shape[0])[0]
    per_pair = total[:, 2 * feat + hidden :].reshape(8, pairs, nb).transpose(1, 0, 2)
    g_loc = lax.dynamic_slice_in_dim(per_pair[:, 0:2].reshape(heads, nb), index * share, share, axis=1)
    g_spread = lax.dynamic_slice_in_dim(per_pair[:, 2:4].reshape(heads, nb), index * share, share, axis=1)
    outputs = paired(kept_out, came_output)
    grad_x = paired(kept_x, came_x.astype(f32))
    joined = jnp.concatenate([s_.total for s_ in s1], axis=1)
    if direct:
        w = feat // pairs
        n_qkv = layout1[0] // (count * w)
        blocks = joined.reshape(rows1, count, 5, w)
        grad_qkv = blocks[:, :, :n_qkv].transpose(0, 2, 1, 3).reshape(rows1, layout1[0])
        grad_mem = blocks[:, :, n_qkv:].transpose(0, 2, 1, 3).reshape(rows1, layout1[1])
    else:
        grad_qkv, grad_mem = joined[:, : layout1[0]], joined[:, layout1[0] :]
    grad_fc, grad_out = s2.total[:, : layout2[0]], s2.total[:, layout2[0] :]
    grad_proj = s3.total
    return (
        outputs, grad_x, grad_qkv, grad_out, grad_mem, grad_fc, grad_proj,
        g_gain1, g_bias1, g_gain2, g_bias2, g_bo, g_bf, g_bp, g_loc, g_spread,
    )


def solution(mesh):
    grid, both, tail = P("row", "col"), P(("row", "col")), P(None, ("row", "col"))
    act, rows = P(None, "row", "col", None), P(None, "row")
    return jax.shard_map(
        shards,
        mesh=mesh,
        in_specs=(act,) + (grid,) * 5 + (both,) * 7 + (tail,) * 2 + (act, P(None, "row", None), rows, act),
        out_specs=(act, act) + (grid,) * 5 + (both,) * 7 + (tail,) * 2,
        check_vma=False,
    )
```

```python
import functools
import math

import jax
import jax.numpy as jnp
import numpy as np
from jax import lax
from jax.experimental import pallas as pl
from jax.experimental.pallas import tpu as pltpu
from jax.sharding import PartitionSpec as P

WINDOW=512; TILE=256; masked=-1e30
var_scale=0.01
NT=(((1,),(1,)),((),()))
NN=(((1,),(0,)),((),()))

def dot_nt(a,b): return lax.dot_general(a,b,NT,preferred_element_type=jnp.float32)
def dot_nn(a,b): return lax.dot_general(a,b,NN,preferred_element_type=jnp.float32)

def split3(v):
    hi=v.astype(jnp.bfloat16); r=v-hi.astype(jnp.float32)
    mid=r.astype(jnp.bfloat16); lo=(r-mid.astype(jnp.float32)).astype(jnp.bfloat16)
    return hi,mid,lo

def lane_is_first(shape,half):
    return lax.broadcasted_iota(jnp.int32,shape,1)<half

def tile_biases(info_ref,first_key,has_far,has_mid):
    key=lax.broadcasted_iota(jnp.int32,(TILE,TILE),0)
    qry=lax.broadcasted_iota(jnp.int32,(TILE,TILE),1)
    tri=key<=qry
    length=info_ref[0]
    diag_pos=first_key+key
    far_pos=diag_pos-WINDOW
    near=jnp.where((diag_pos<length)|(key==qry),0.0,masked)
    far=jnp.where((far_pos>=0)&(far_pos<length),0.0,masked) if has_far else masked
    comb=jnp.where(tri,near,far)
    mid_pos=diag_pos-TILE
    mid=jnp.where((mid_pos>=0)&(mid_pos<length),0.0,masked)
    return comb,mid

def density_rows(wls,mk,half):
    vec=dot_nn(wls,mk)
    row=lax.broadcasted_iota(jnp.int32,vec.shape,0)
    lane=lax.broadcasted_iota(jnp.int32,vec.shape,1)
    return jnp.where((row%2==0)==(lane<half),vec,0.0)

def logits_of(vec,qb):
    hi,mid,lo=split3(vec)
    parts=dot_nt(jnp.concatenate([hi,mid,lo,lo],axis=0),qb)
    return (parts[16:24]+parts[8:16])+parts[0:8]

def spreads(logits,nb):
    location=1.0/(1.0+jnp.exp(-logits))
    soft=jnp.maximum(logits,0.0)+jnp.log1p(jnp.exp(-jnp.abs(logits)))
    spread=var_scale*soft+1.0/(nb*nb)
    return location,spread

def fwd_kernel(halo,half,info_ref,q_ref,k_ref,v_ref,mk_ref,mv_ref,wls_ref,ctx_ref,lse_ref,bias_ref):
    S=q_ref.shape[0]; nblk=S//TILE; nb=mk_ref.shape[0]; ht=halo//TILE
    @pl.when(pl.program_id(0)==0)
    def _():
        for i in range(nblk):
            comb,mid=tile_biases(info_ref,info_ref[1]+i*TILE,ht+i>=2,ht+i>=1)
            bias_ref[2*i]=comb; bias_ref[2*i+1]=mid
    tri=lax.broadcasted_iota(jnp.int32,(TILE,TILE),0)<=lax.broadcasted_iota(jnp.int32,(TILE,TILE),1)
    trib=jnp.where(tri,1.0,0.0).astype(jnp.bfloat16)
    lane=lax.broadcasted_iota(jnp.int32,(16,2*half),1)
    sides=[jnp.where(lane<half,1.0,0.0)[0:1].astype(jnp.bfloat16),jnp.where(lane<half,0.0,1.0)[0:1].astype(jnp.bfloat16)]
    centers=(lax.broadcasted_iota(jnp.int32,(nb,TILE),0).astype(jnp.float32)+0.5)/nb
    vec=density_rows(wls_ref[0],mk_ref[...],half)
    vT=v_ref[...].T
    mvT=mv_ref[...].T
    lse_ref[...]=jnp.zeros_like(lse_ref)
    for i in range(nblk):
        rows=slice(i*TILE,(i+1)*TILE)
        qb=q_ref[rows,:]*jnp.bfloat16(half**-0.5)
        d0=halo+i*TILE
        has_mid=ht+i>=1; has_far=ht+i>=2
        kd=k_ref[d0:d0+TILE,:]
        logits=logits_of(vec,qb)
        location,spread=spreads(logits,nb)
        nis=-0.5/spread
        norm=lax.rsqrt(2.0*math.pi*spread)*(1.0/nb)
        outs=[]
        for x in range(2):
            qx=qb*sides[x]
            vx=vT[x*half:(x+1)*half,:]
            sd=dot_nt(kd,qx)
            if has_far:
                sf=dot_nt(k_ref[d0-2*TILE:d0-TILE,:],qx)
                sc=jnp.where(tri,sd,sf)+bias_ref[2*i]
            else:
                sc=sd+bias_ref[2*i]
            top=jnp.max(sc,axis=0,keepdims=True)
            if has_mid:
                sm=dot_nt(k_ref[d0-TILE:d0,:],qx)+bias_ref[2*i+1]
                top=jnp.maximum(top,jnp.max(sm,axis=0,keepdims=True))
            ec=jnp.exp(sc-top)
            tot=jnp.sum(ec,axis=0,keepdims=True)
            ecl=ec.astype(jnp.bfloat16)
            if has_far:
                near=ecl*trib
                o=dot_nn(vx[:,d0:d0+TILE],near)+dot_nn(vx[:,d0-2*TILE:d0-TILE],ecl-near)
            else:
                o=dot_nn(vx[:,d0:d0+TILE],ecl)
            if has_mid:
                em=jnp.exp(sm-top)
                tot=tot+jnp.sum(em,axis=0,keepdims=True)
                o=o+dot_nn(vx[:,d0-TILE:d0],em.astype(jnp.bfloat16))
            lse_ref[0,x:x+1,rows]=top+jnp.log(tot)
            o=o*(1.0/tot)
            z=location[x:x+1]-centers
            e=jnp.exp(nis[2+x:3+x]*(z*z))
            r=dot_nn(mvT[x*half:(x+1)*half,:],e.astype(jnp.bfloat16))*norm[2+x:3+x]
            outs.append(o+r)
        ctx_ref[rows,:]=jnp.concatenate(outs,axis=0).T.astype(jnp.bfloat16)

def bwd_kernel(halo,half,info_ref,q_ref,k_ref,v_ref,mk_ref,mv_ref,wls_ref,lse_ref,do_ref,
               dq_ref,dk_ref,dv_ref,dmk_ref,dmv_ref,gls_ref,bias_ref,dk_acc,dv_acc):
    S=q_ref.shape[0]; nblk=S//TILE; nb=mk_ref.shape[0]; ht=halo//TILE
    @pl.when(pl.program_id(0)==0)
    def _():
        for i in range(nblk):
            comb,mid=tile_biases(info_ref,info_ref[1]+i*TILE,ht+i>=2,ht+i>=1)
            bias_ref[2*i]=comb; bias_ref[2*i+1]=mid
    tri=lax.broadcasted_iota(jnp.int32,(TILE,TILE),0)<=lax.broadcasted_iota(jnp.int32,(TILE,TILE),1)
    trib=jnp.where(tri,1.0,0.0).astype(jnp.bfloat16)
    lane=lax.broadcasted_iota(jnp.int32,(16,2*half),1)
    sides=[jnp.where(lane<half,1.0,0.0)[0:1].astype(jnp.bfloat16),jnp.where(lane<half,0.0,1.0)[0:1].astype(jnp.bfloat16)]
    centers=(lax.broadcasted_iota(jnp.int32,(nb,TILE),0).astype(jnp.float32)+0.5)/nb
    mk=mk_ref[...]; mv=mv_ref[...]
    vec=density_rows(wls_ref[0],mk,half)
    vecT=vec.T
    kT=k_ref[...].T
    dk_acc[...]=jnp.zeros_like(dk_acc); dv_acc[...]=jnp.zeros_like(dv_acc)
    dmv=jnp.zeros((nb,2*half),jnp.float32)
    dvec=jnp.zeros((8,2*half),jnp.float32)
    for i in range(nblk):
        rows=slice(i*TILE,(i+1)*TILE)
        qb=q_ref[rows,:]*jnp.bfloat16(half**-0.5)
        dob=do_ref[rows,:]
        d0=halo+i*TILE
        has_mid=ht+i>=1; has_far=ht+i>=2
        dg=slice(d0,d0+TILE); md=slice(d0-TILE,d0); fr=slice(d0-2*TILE,d0-TILE)
        logits=logits_of(vec,qb)
        location,spread=spreads(logits,nb)
        inv=1.0/spread
        nis=-0.5*inv
        norm=lax.rsqrt(2.0*math.pi*spread)*(1.0/nb)
        outs=[]; s0s=[]; s1s=[]; s2s=[]
        for x in range(2):
            qx=qb*sides[x]
            dox=dob*sides[x]
            kx=kT[x*half:(x+1)*half,:]
            lse=lse_ref[0,x:x+1,rows]
            sc=dot_nt(k_ref[dg,:],qx)
            dpc=dot_nt(v_ref[dg,:],dox)
            if has_far:
                sc=jnp.where(tri,sc,dot_nt(k_ref[fr,:],qx))
                dpc=jnp.where(tri,dpc,dot_nt(v_ref[fr,:],dox))
            pc=jnp.exp(sc+bias_ref[2*i]-lse)
            delta=jnp.sum(pc*dpc,axis=0,keepdims=True)
            if has_mid:
                sm=dot_nt(k_ref[md,:],qx)
                dpm=dot_nt(v_ref[md,:],dox)
                pm=jnp.exp(sm+bias_ref[2*i+1]-lse)
                delta=delta+jnp.sum(pm*dpm,axis=0,keepdims=True)
                dsm=(pm*(dpm-delta)).astype(jnp.bfloat16)
                dv_acc[md,:]+=dot_nn(pm.astype(jnp.bfloat16),dox)
                dk_acc[md,:]+=dot_nn(dsm,qx)
            dsc=(pc*(dpc-delta)).astype(jnp.bfloat16)
            pcl=pc.astype(jnp.bfloat16)
            if has_far:
                dsd=dsc*trib; dsf=dsc-dsd
                near=pcl*trib
                dv_acc[dg,:]+=dot_nn(near,dox)
                dv_acc[fr,:]+=dot_nn(pcl-near,dox)
                dk_acc[dg,:]+=dot_nn(dsd,qx)
                dk_acc[fr,:]+=dot_nn(dsf,qx)
                dq=dot_nn(kx[:,dg],dsd)+dot_nn(kx[:,fr],dsf)
            else:
                dv_acc[dg,:]+=dot_nn(pcl,dox)
                dk_acc[dg,:]+=dot_nn(dsc,qx)
                dq=dot_nn(kx[:,dg],dsc)
            if has_mid:
                dq=dq+dot_nn(kx[:,md],dsm)
            outs.append(dq)
            z=location[x:x+1]-centers
            e=jnp.exp(nis[2+x:3+x]*(z*z))
            g=dot_nt(mv,dox)*e
            gz=g*z
            s0s.append(jnp.sum(g,axis=0,keepdims=True))
            s1s.append(jnp.sum(gz,axis=0,keepdims=True))
            s2s.append(jnp.sum(gz*z,axis=0,keepdims=True))
            dmv=dmv+dot_nn((e*norm[2+x:3+x]).astype(jnp.bfloat16),dox)
        n2=norm[2:4]; i2=inv[2:4]
        s0=jnp.concatenate(s0s,axis=0); s1=jnp.concatenate(s1s,axis=0); s2=jnp.concatenate(s2s,axis=0)
        dloc=-(n2*i2)*s1
        dspr=n2*(0.5*i2)*(s2*i2-s0)
        l2=location[0:2]
        dll=dloc*l2*(1.0-l2)
        dsl=dspr*var_scale*location[2:4]
        dl=jnp.concatenate([dll,dsl,jnp.zeros((4,TILE),jnp.float32)],axis=0)
        hi=dl.astype(jnp.bfloat16); lo=(dl-hi.astype(jnp.float32)).astype(jnp.bfloat16)
        both=dot_nn(jnp.concatenate([hi,lo],axis=0),qb)
        dvec=dvec+(both[0:8]+both[8:16])
        for x in range(2):
            seg=slice(x*half,(x+1)*half)
            outs[x]=outs[x]+vecT[seg,x:x+1]*dl[x:x+1]+vecT[seg,2+x:3+x]*dl[2+x:3+x]
        dq_ref[rows,:]=(jnp.concatenate(outs,axis=0)*(half**-0.5)).T.astype(jnp.bfloat16)
    dk_ref[...]=dk_acc[...].astype(jnp.bfloat16)
    dv_ref[...]=dv_acc[...].astype(jnp.bfloat16)
    dmv_ref[...]=dmv.astype(jnp.bfloat16)
    row=lax.broadcasted_iota(jnp.int32,dvec.shape,0)
    lane=lax.broadcasted_iota(jnp.int32,dvec.shape,1)
    dvec=jnp.where((row%2==0)==(lane<half),dvec,0.0)
    hi=dvec.astype(jnp.bfloat16); lo=(dvec-hi.astype(jnp.float32)).astype(jnp.bfloat16)
    stack=jnp.concatenate([hi,lo],axis=0)
    gl=dot_nt(stack,mk)
    gls_ref[0]=gl[0:8]+gl[8:16]
    wT=wls_ref[0].astype(jnp.float32).T.astype(jnp.bfloat16)
    dmk_ref[...]=dot_nn(jnp.concatenate([wT,wT],axis=1),stack).astype(jnp.bfloat16)

def col_block(rows,width,first,stride=1):
    return pl.BlockSpec((rows,width),lambda p,info: (0,first+stride*p))

def attention_forward(info,qkv,kv,halo,mem_kv,wls,heads,vmem):
    S=qkv.shape[0]; pairs=heads//2; width=kv[0].shape[1]
    nb=mem_kv.shape[0]; feat=mem_kv.shape[1]//2; w=feat//pairs; half=w//2
    karr,koff,varr,voff=kv[0],kv[1],kv[2],kv[3]
    nblk=S//TILE
    spec=pltpu.PrefetchScalarGridSpec(num_scalar_prefetch=1,grid=(pairs,),
        in_specs=[col_block(S,w,0),col_block(halo+S,w,koff),col_block(halo+S,w,voff),col_block(nb,w,0),col_block(nb,w,pairs),
                  pl.BlockSpec((1,8,nb),lambda p,info:(p,0,0))],
        out_specs=[col_block(S,w,0),pl.BlockSpec((1,8,S),lambda p,info:(p,0,0))],
        scratch_shapes=[pltpu.VMEM((2*nblk,TILE,TILE),jnp.float32)])
    return pl.pallas_call(functools.partial(fwd_kernel,halo,half),grid_spec=spec,
        out_shape=[jax.ShapeDtypeStruct((S,feat),jnp.bfloat16),jax.ShapeDtypeStruct((pairs,8,S),jnp.float32)],
        compiler_params=pltpu.CompilerParams(vmem_limit_bytes=vmem,dimension_semantics=("arbitrary",)),
        cost_estimate=pl.CostEstimate(flops=24*S*S*feat//4,bytes_accessed=10*S*feat,transcendentals=heads*S*768),
        name="mix_forward")(info,qkv,karr,varr,mem_kv,mem_kv,wls)

def attention_backward(info,qkv,kv,halo,mem_kv,wls,lse,d_context,heads,vmem,begin,count,stride):
    S=qkv.shape[0]; pairs=heads//2
    nb=mem_kv.shape[0]; feat=mem_kv.shape[1]//2; w=feat//pairs; half=w//2
    karr,koff,varr,voff=kv
    nblk=S//TILE; bf=jnp.bfloat16
    spec=pltpu.PrefetchScalarGridSpec(num_scalar_prefetch=1,grid=(count,),
        in_specs=[col_block(S,w,begin,stride),col_block(halo+S,w,koff+begin,stride),col_block(halo+S,w,voff+begin,stride),
                  col_block(nb,w,begin,stride),col_block(nb,w,pairs+begin,stride),pl.BlockSpec((1,8,nb),lambda p,info:(begin+stride*p,0,0)),
                  pl.BlockSpec((1,8,S),lambda p,info:(begin+stride*p,0,0)),col_block(S,w,begin,stride)],
        out_specs=[col_block(S,w,0),col_block(halo+S,w,0),col_block(halo+S,w,0),col_block(nb,w,0),col_block(nb,w,0),
                   pl.BlockSpec((1,8,nb),lambda p,info:(p,0,0))],
        scratch_shapes=[pltpu.VMEM((2*nblk,TILE,TILE),jnp.float32),pltpu.VMEM((halo+S,w),jnp.float32),pltpu.VMEM((halo+S,w),jnp.float32)])
    part=count*w
    return pl.pallas_call(functools.partial(bwd_kernel,halo,half),grid_spec=spec,
        out_shape=[jax.ShapeDtypeStruct((S,part),bf),jax.ShapeDtypeStruct((halo+S,part),bf),jax.ShapeDtypeStruct((halo+S,part),bf),
                   jax.ShapeDtypeStruct((nb,part),bf),jax.ShapeDtypeStruct((nb,part),bf),jax.ShapeDtypeStruct((count,8,nb),jnp.float32)],
        compiler_params=pltpu.CompilerParams(vmem_limit_bytes=vmem,dimension_semantics=("arbitrary",)),
        cost_estimate=pl.CostEstimate(flops=30*S*S*part,bytes_accessed=20*S*part,transcendentals=2*count*S*768),
        name="mix_backward")(info,qkv,karr,varr,mem_kv,mem_kv,wls,lse,d_context)


eps=1e-5
TN=(((0,),(0,)),((),()))
def dot_tn(a,b): return lax.dot_general(a,b,TN,preferred_element_type=jnp.float32)

def norm_parts(v):
    center=jnp.mean(v,axis=-1,keepdims=True)
    off=v-center
    rstd=lax.rsqrt(jnp.mean(off*off,axis=-1,keepdims=True)+eps)
    return off*rstd,rstd

def norm_back(gd,xhat,rstd):
    return rstd*(gd-jnp.mean(gd,axis=-1,keepdims=True)-xhat*jnp.mean(gd*xhat,axis=-1,keepdims=True))

def whole(shape): return pl.BlockSpec(shape,lambda *a: (0,)*len(shape),pipeline_mode=pl.Buffered(1))

def shard_copies(loads, pieces, targets, sem, row, col, which):
    for n, (src, dst, fr, fc, rows, cols, slot, at, column, width) in enumerate(loads):
        if dst not in which:
            continue
        if rows is None:
            yield pltpu.make_async_copy(pieces[src], targets[dst], sem.at[n])
            continue
        r0 = pl.multiple_of((row ^ fr) * rows, 16)
        c0 = pl.multiple_of((col ^ fc) * cols + column, 128)
        yield pltpu.make_async_copy(
            pieces[src].at[slot, :, pl.ds(at, width)], targets[dst].at[pl.ds(r0, rows), pl.ds(c0, width)], sem.at[n]
        )


def qkv_kernel(loads, pairs, info_ref, x_ref, vec_ref, own_ref, came_ref, *refs):
    count = max(load[0] for load in loads) + 1
    pieces, refs = refs[:count], refs[count:]
    nT_ref, o_ref, mem_ref, bT_ref, wq_ref, wq_s, wm_s, in_sem, out_sem = refs
    i = pl.program_id(0)
    D = wq_s.shape[0]
    w, half = D // pairs, pairs // 2
    outs = []
    for n in range(3 * pairs):
        kind, p, j = n // pairs, n % pairs // 2, n % 2
        at = kind * D + (j * half + p) * w
        copy = pltpu.make_async_copy(wq_s.at[:, at : at + w], wq_ref.at[:, n * w : (n + 1) * w], out_sem.at[n])
        outs.append(copy)

    @pl.when(i == 0)
    def _():
        for begin in (True, False):
            for copy in shard_copies(loads, pieces, (wq_s, wm_s), in_sem, info_ref[2], info_ref[3], (0, 1)):
                copy.start() if begin else copy.wait()
        for out in outs:
            out.start()
        basis = (own_ref[...] + came_ref[...].astype(jnp.float32)).astype(jnp.bfloat16)
        bT_ref[...] = basis.T
        mem_ref[...] = dot_nn(basis, wm_s[...]).astype(jnp.bfloat16)

    xhat, _ = norm_parts(x_ref[...].astype(jnp.float32))
    n = (xhat * vec_ref[0:1] + vec_ref[1:2]).astype(jnp.bfloat16)
    nT_ref[...] = n.T
    o_ref[...] = dot_nn(n, wq_s[...]).astype(jnp.bfloat16)

    @pl.when(i == pl.num_programs(0) - 1)
    def _():
        for out in outs:
            out.wait()


def project_qkv(info, x, vec, own_basis, came_basis, pieces, loads, pairs, vmem, rows=256):
    S, D = x.shape
    nb = own_basis.shape[0]
    bf, sd = jnp.bfloat16, jax.ShapeDtypeStruct
    hbm = pl.BlockSpec(memory_space=pl.ANY)
    return pl.pallas_call(
        functools.partial(qkv_kernel, loads, pairs),
        grid_spec=pltpu.PrefetchScalarGridSpec(
            num_scalar_prefetch=1,
            grid=(S // rows,),
            in_specs=[pl.BlockSpec((rows, D), lambda i, info: (i, 0)), whole((8, D)), whole((nb, D)), whole((nb, D))]
            + [hbm] * len(pieces),
            out_specs=[
                pl.BlockSpec((D, rows), lambda i, info: (0, i)), pl.BlockSpec((rows, 3 * D), lambda i, info: (i, 0)),
                whole((nb, 2 * D)), whole((D, nb)), hbm,
            ],
            scratch_shapes=[
                pltpu.VMEM((D, 3 * D), bf), pltpu.VMEM((D, 2 * D), bf),
                pltpu.SemaphoreType.DMA((len(loads),)), pltpu.SemaphoreType.DMA((3 * pairs,)),
            ],
        ),
        out_shape=[sd((D, S), bf), sd((S, 3 * D), bf), sd((nb, 2 * D), bf), sd((D, nb), bf), sd((D, 3 * D), bf)],
        compiler_params=pltpu.CompilerParams(vmem_limit_bytes=vmem),
        cost_estimate=pl.CostEstimate(
            flops=6 * S * D * D + 4 * nb * D * D, bytes_accessed=10 * S * D + 16 * D * D, transcendentals=0
        ),
        name="project_qkv",
    )(info, x, vec, own_basis, came_basis, *pieces)


def row_slot(fr, order):
    return sum(((fr >> bit) & 1) << i for i, (axis, bit) in enumerate(order[:-1]) if axis == "row")


def col_slot(fc, order):
    return sum(((fc >> bit) & 1) << i for i, (axis, bit) in enumerate(order[:-1]) if axis == "col")


class _Fixed:
    def __init__(self, sem):
        self.at = self
        self.sem = sem

    def __getitem__(self, index):
        return self.sem


def mlp_kernel(steps, chunk, loads, cut, info_ref, c_ref, x_ref, g_ref, vec_ref, bf_ref, *refs):
    count = max(load[0] for load in loads) + 1
    pieces, refs = refs[:count], refs[count:]
    out_ref, dmid_ref, dctx_ref, gv_ref, gb_ref = refs[:5]
    made = 3 if cut is None else 4
    grads, refs = refs[5 : 5 + made], refs[5 + made :]
    n_s, nT_s, dm_s, mid_s, acc_s, dn_s, hid_s, dp_s, wf_s, wo_s, wp_s, go_s, gf_s, gp_s, in_sem, out_sem, go_sem = refs
    f = pl.program_id(0)
    S, D = x_ref.shape
    fb = gf_s.shape[2]
    length, base, row, col = info_ref[0], info_ref[1], info_ref[2], info_ref[3]
    nchunk = S // chunk
    buf = f % 2
    fe, per_col = f, steps
    if cut is not None:
        fe, per_col = f ^ (row // (cut[0] // steps)), steps // cut[1]

    def valid_of(i):
        pos = base + i * chunk + lax.broadcasted_iota(jnp.int32, (chunk, 1), 0)
        return jnp.where(pos < length, 1.0, 0.0)

    targets = (wf_s, wo_s, wp_s)

    def arrive(which, rows=None, cols=None):
        if cut is None:
            for copy in shard_copies(loads, pieces, targets, in_sem, row, col, which):
                copy.wait()
            return
        n_rows, n_cols = cut[:2]
        seen = set()
        for src, dst, _, _, height, across, slot, at, _, width in loads:
            if dst not in which or dst in seen:
                continue
            seen.add(dst)
            for r in range(n_rows) if rows is None else rows:
                for c in range(n_cols) if cols is None else cols:
                    n = (dst * n_rows + r) * n_cols + c
                    pltpu.make_async_copy(
                        pieces[src].at[slot, :, pl.ds(at, width)], targets[dst].at[:height, :width], in_sem.at[n]
                    ).wait()

    def depart(which, only=None):
        for n, load in enumerate(loads):
            if load[1] in which:
                place = n
                if cut is not None:
                    place = (load[1] * cut[0] + (row ^ load[2])) * cut[1] + (col ^ load[3])
                copy = next(shard_copies([load], pieces, targets, _Fixed(in_sem.at[place]), row, col, which))
                if only is None:
                    copy.start()
                else:
                    pl.when((col ^ load[3]) == only)(copy.start)

    def block_copies(begin, buf=buf):
        if cut is None:
            copies = [
                pltpu.make_async_copy(gf_s.at[buf], grads[0].at[:, pl.ds(pl.multiple_of(fe * fb, 128), fb)], out_sem.at[buf, 0]),
                pltpu.make_async_copy(gp_s.at[buf], grads[2].at[pl.ds(pl.multiple_of(fe * fb, 16), fb), :], out_sem.at[buf, 1]),
            ]
            for copy in copies:
                copy.start() if begin else copy.wait()
            return
        n_rows, n_cols, order2, order3 = cut
        rows2, rows3 = D // n_rows, fb * steps // n_rows
        cols2, cols3 = fb * steps // n_cols, D // n_cols
        per = cols2 // fb
        c = fe // per
        at = pl.multiple_of((fe % per) * fb, 128)
        for fr in range(n_rows):
            slot = row_slot(fr, order2) + col_slot(c ^ col, order2)
            src = gf_s.at[buf, pl.ds(pl.multiple_of((row ^ fr) * rows2, 16), rows2), :]
            copy = pltpu.make_async_copy(src, grads[fr & 1].at[slot, :, pl.ds(at, fb)], out_sem.at[buf, fr])
            copy.start() if begin else copy.wait()
        n = n_rows
        for i in range(fb // rows3):
            rel = (fe * (fb // rows3) + i) ^ row
            for c in range(n_cols):
                slot = row_slot(rel, order3) + col_slot(c ^ col, order3)
                src = gp_s.at[buf, i * rows3 : (i + 1) * rows3, c * cols3 : (c + 1) * cols3]
                if begin:
                    for side in range(2):

                        @pl.when(rel & 1 == side)
                        def _():
                            pltpu.make_async_copy(src, grads[2 + side].at[slot], out_sem.at[buf, n]).start()
                else:
                    pltpu.make_async_copy(src, grads[2].at[0], out_sem.at[buf, n]).wait()
                n += 1

    @pl.when(f == 0)
    def _():
        depart((1,))
        if cut is None:
            depart((0, 2))
        else:
            depart((0,), fe // per_col)
        for i in range(nchunk):
            rs = slice(i * chunk, (i + 1) * chunk)
            dm_s[rs, :] = (g_ref[rs, :].astype(jnp.float32) * valid_of(i)).astype(jnp.bfloat16)
        acc_s[...] = jnp.zeros_like(acc_s)
        dn_s[...] = jnp.zeros_like(dn_s)
        if cut is not None:
            depart((2,))
            for c in range(1, cut[1]):
                depart((0,), fe // per_col ^ c)
        arrive((1,))
        for i in range(nchunk):
            rs = slice(i * chunk, (i + 1) * chunk)
            branch = dot_nn(c_ref[rs, :], wo_s[...]) + vec_ref[2:3]
            mid = x_ref[rs, :].astype(jnp.float32) + valid_of(i) * branch
            mid_s[rs, :] = mid
            xhat, _ = norm_parts(mid)
            n = (xhat * vec_ref[0:1] + vec_ref[1:2]).astype(jnp.bfloat16)
            n_s[rs, :] = n
            nT_s[:, rs] = n.T
        if cut is None:
            arrive((0, 2))

    if cut is not None:

        @pl.when(f % per_col == 0)
        def _():
            arrive((0,), None, [fe // per_col])

        each = cut[0] // steps
        arrive((2,), [fe * each + i for i in range(each)])

    @pl.when(f >= 2)
    def _():
        block_copies(False)

    cs = pl.ds(pl.multiple_of(fe * fb, 128), fb)
    wf = wf_s[:, cs]
    wp = wp_s[cs, :]
    c0 = math.sqrt(2.0 / math.pi)
    gb = jnp.zeros((1, fb), jnp.float32)
    for i in range(nchunk):
        rs = slice(i * chunk, (i + 1) * chunk)
        pre = dot_nn(n_s[rs, :], wf) + bf_ref[...]
        sq = pre * pre
        t = jnp.tanh(c0 * pre * (1.0 + 0.044715 * sq))
        hp = 0.5 * pre
        hid = hp + hp * t
        dgel = 0.5 + 0.5 * t + hp * (1.0 - t * t) * (c0 * (1.0 + (3 * 0.044715) * sq))
        hidb = hid.astype(jnp.bfloat16)
        hid_s[rs, :] = hidb
        acc_s[rs, :] += dot_nn(hidb, wp)
        dpb = (dot_nt(dm_s[rs, :], wp) * dgel).astype(jnp.bfloat16)
        dp_s[rs, :] = dpb
        gb = gb + jnp.sum(dpb.astype(jnp.float32), axis=0, keepdims=True)
        dn_s[rs, :] += dot_nt(dpb, wf)
    gb_ref[...] = jnp.broadcast_to(gb, gb_ref.shape)
    gf_s[buf] = dot_nn(nT_s[...], dp_s[...]).astype(jnp.bfloat16)
    gp_s[buf] = dot_tn(hid_s[...], dm_s[...]).astype(jnp.bfloat16)
    block_copies(True)

    @pl.when(f == steps - 1)
    def _():
        gg = jnp.zeros((1, D), jnp.float32)
        gbi, gbo, gbp = gg, gg, gg
        for i in range(nchunk):
            rs = slice(i * chunk, (i + 1) * chunk)
            valid = valid_of(i)
            mid = mid_s[rs, :]
            out_ref[rs, :] = (mid + valid * (acc_s[rs, :] + vec_ref[3:4])).astype(jnp.bfloat16)
            xhat, rstd = norm_parts(mid)
            dn = dn_s[rs, :]
            cot = dm_s[rs, :].astype(jnp.float32)
            dmid = cot + norm_back(dn * vec_ref[0:1], xhat, rstd)
            dmid_ref[rs, :] = dmid
            db = (valid * dmid).astype(jnp.bfloat16)
            gg = gg + jnp.sum(dn * xhat, axis=0, keepdims=True)
            gbi = gbi + jnp.sum(dn, axis=0, keepdims=True)
            gbo = gbo + jnp.sum(db.astype(jnp.float32), axis=0, keepdims=True)
            gbp = gbp + jnp.sum(cot, axis=0, keepdims=True)
            n_s[rs, :] = db
        go_s[...] = dot_tn(c_ref[...], n_s[...]).astype(jnp.bfloat16)
        copies = []
        if cut is None:
            copies.append(pltpu.make_async_copy(go_s, grads[1], go_sem.at[0]))
        else:
            n_rows, n_cols, order2, _ = cut
            rows, cols = D // n_rows, D // n_cols
            at = fb * steps // n_cols
            for fr in range(n_rows):
                for c in range(n_cols):
                    slot = row_slot(fr, order2) + col_slot(c ^ col, order2)
                    src = go_s.at[pl.ds(pl.multiple_of((row ^ fr) * rows, 16), rows), c * cols : (c + 1) * cols]
                    dst = grads[fr & 1].at[slot, :, at : at + cols]
                    copies.append(pltpu.make_async_copy(src, dst, go_sem.at[len(copies)]))
        for copy in copies:
            copy.start()
        for i in range(nchunk):
            rs = slice(i * chunk, (i + 1) * chunk)
            dctx_ref[rs, :] = dot_nt(n_s[rs, :], wo_s[...]).astype(jnp.bfloat16)
        gv_ref[...] = jnp.concatenate([gbo, gg, gbi, gbp, jnp.zeros((4, D), jnp.float32)], axis=0)
        for copy in copies:
            copy.wait()
        for slot in range(min(2, steps)):
            block_copies(False, slot)


def mlp_block(info, context, x, d_out, pieces, loads, vec, b_fc, cut, widths, vmem, fb=768, chunk=256):
    S, D = x.shape
    FF = b_fc.shape[1]
    steps = FF // fb
    bf, f32, sd = jnp.bfloat16, jnp.float32, jax.ShapeDtypeStruct
    hbm = pl.BlockSpec(memory_space=pl.ANY)
    if cut is None:
        grads = [sd((D, FF), bf), sd((D, D), bf), sd((FF, D), bf)]
        n_in, n_out, n_go = len(loads), 2, 1
    else:
        n_rows, n_cols = cut[:2]
        half = n_rows * n_cols // 2
        grads = [sd((half, D // n_rows, sum(widths)), bf)] * 2 + [sd((half, FF // n_rows, D // n_cols), bf)] * 2
        n_in = 3 * n_rows * n_cols
        n_out, n_go = n_rows + fb * n_rows // FF * n_cols, n_rows * n_cols
    if cut is None:
        at = lambda f, info: (0, f)
    else:
        at = lambda f, info: (0, f ^ (info[2] // (n_rows // steps)))
    spec = pltpu.PrefetchScalarGridSpec(
        num_scalar_prefetch=1,
        grid=(steps,),
        in_specs=[whole((S, D))] * 3 + [whole((8, D)), pl.BlockSpec((1, fb), at)] + [hbm] * len(pieces),
        out_specs=[whole((S, D))] * 3 + [whole((8, D)), pl.BlockSpec((8, fb), at)] + [hbm] * len(grads),
        scratch_shapes=[
            pltpu.VMEM((S, D), bf), pltpu.VMEM((D, S), bf), pltpu.VMEM((S, D), bf),
            pltpu.VMEM((S, D), f32), pltpu.VMEM((S, D), f32), pltpu.VMEM((S, D), f32),
            pltpu.VMEM((S, fb), bf), pltpu.VMEM((S, fb), bf),
            pltpu.VMEM((D, FF), bf), pltpu.VMEM((D, D), bf), pltpu.VMEM((FF, D), bf), pltpu.VMEM((D, D), bf),
            pltpu.VMEM((2, D, fb), bf), pltpu.VMEM((2, fb, D), bf),
            pltpu.SemaphoreType.DMA((n_in,)), pltpu.SemaphoreType.DMA((2, n_out)), pltpu.SemaphoreType.DMA((n_go,)),
        ],
    )
    return pl.pallas_call(
        functools.partial(mlp_kernel, steps, chunk, loads, cut),
        grid_spec=spec,
        out_shape=[sd((S, D), bf), sd((S, D), f32), sd((S, D), bf), sd((8, D), f32), sd((8, FF), f32)] + grads,
        compiler_params=pltpu.CompilerParams(vmem_limit_bytes=vmem, dimension_semantics=("arbitrary",)),
        cost_estimate=pl.CostEstimate(
            flops=12 * S * D * FF + 6 * S * D * D, bytes_accessed=8 * D * FF + 20 * S * D, transcendentals=S * FF
        ),
        name="mlp_block",
    )(info, context, x, d_out, vec, b_fc, *pieces)


def wgrad_kernel(cut, count, split, info_ref, nT_ref, bT_ref, *refs):
    n_rows, n_cols = cut
    parts, outs, (g_s, sem) = refs[: 5 * count], refs[5 * count : -2], refs[-2:]
    D = nT_ref.shape[0]
    rows, w = D // n_rows, parts[0].shape[1] // 2
    row, col = info_ref[2], info_ref[3]
    copies = []
    nT, bT = nT_ref[...], bT_ref[...]
    for c in range(n_cols):
        at = 0
        for p in range(count):
            q_ref, k_ref, v_ref, mk_ref, mv_ref = parts[5 * p : 5 * p + 5]
            if c == 0:
                terms = [(nT, q_ref[...]), (nT, k_ref[:, :w]), (bT, mk_ref[...])]
            else:
                terms = [(nT, k_ref[:, w:]), (nT, v_ref[...]), (bT, mv_ref[...])]
            for left, right in terms:
                g_s[c, :, at : at + right.shape[1]] = dot_nn(left, right).astype(jnp.bfloat16)
                at += right.shape[1]
        at = 0
        for i, (width, order) in enumerate(split):
            for fr in range(n_rows):
                slot = row_slot(fr, order) + col_slot(c ^ col, order)
                block = g_s.at[c, pl.ds(pl.multiple_of((row ^ fr) * rows, 16), rows), at : at + width]
                copies.append(pltpu.make_async_copy(block, outs[2 * i + (fr & 1)].at[slot], sem.at[len(copies)]))
                copies[-1].start()
            at += width
    for copy in copies:
        copy.wait()


def weight_grads(info, nT, bT, parts, n_rows, split, vmem):
    D, S = nT.shape
    nb, w, n_cols, count = bT.shape[1], parts[0][0].shape[1] // 2, 2, len(parts)
    rows = D // n_rows
    flat = [d for part in parts for d in part]
    bf, hbm = jnp.bfloat16, pl.BlockSpec(memory_space=pl.ANY)
    outs = []
    for width, _ in split:
        outs += [jax.ShapeDtypeStruct((n_rows * n_cols // 2, rows, width), bf)] * 2
    outs = pl.pallas_call(
        functools.partial(wgrad_kernel, (n_rows, n_cols), count, split),
        grid_spec=pltpu.PrefetchScalarGridSpec(
            num_scalar_prefetch=1,
            grid=(1,),
            in_specs=[whole(a.shape) for a in [nT, bT] + flat],
            out_specs=[hbm] * len(outs),
            scratch_shapes=[
                pltpu.VMEM((n_cols, D, 5 * w * count), bf), pltpu.SemaphoreType.DMA((n_rows * n_cols * len(split),)),
            ],
        ),
        out_shape=outs,
        compiler_params=pltpu.CompilerParams(vmem_limit_bytes=vmem),
        cost_estimate=pl.CostEstimate(
            flops=12 * S * D * w * count, bytes_accessed=14 * S * w * count + 2 * S * D + 20 * D * w * count, transcendentals=0
        ),
        name="weight_grads",
    )(info, nT, bT, *flat)
    return [Scatter(outs[2 * i], outs[2 * i + 1], order) for i, (_, order) in enumerate(split)]


def tokens_kernel(count,w_ref,x_ref,dm_ref,gain_ref,*refs):
    o_ref,gv_ref=refs[-2:]
    i=pl.program_id(0); D=x_ref.shape[1]; width=D//(2*count)
    dn=None
    for kind in range(3):
        for p in range(count):
            at=kind*D+2*p*width
            term=dot_nt(refs[3*p+kind][...],w_ref[:,at:at+2*width])
            dn=term if dn is None else dn+term
    xhat,rstd=norm_parts(x_ref[...].astype(jnp.float32))
    o_ref[...]=dm_ref[...]+norm_back(dn*gain_ref[...],xhat,rstd)
    @pl.when(i==0)
    def _(): gv_ref[...]=jnp.zeros_like(gv_ref)
    gv_ref[0:1]+=jnp.sum(dn*xhat,axis=0,keepdims=True)
    gv_ref[1:2]+=jnp.sum(dn,axis=0,keepdims=True)

def token_grad(parts,w,x,d_middle,gain,vmem,rows=256):
    S,D=x.shape; count=len(parts); width=D//count
    by_row=lambda width: pl.BlockSpec((rows,width),lambda i:(i,0))
    return pl.pallas_call(functools.partial(tokens_kernel,count),grid=(S//rows,),
        in_specs=[whole((D,3*D)),by_row(D),by_row(D),whole((1,D))]+[by_row(width)]*(3*count),
        out_specs=[by_row(D),pl.BlockSpec((8,D),lambda i:(0,0))],
        out_shape=[jax.ShapeDtypeStruct((S,D),jnp.float32),jax.ShapeDtypeStruct((8,D),jnp.float32)],
        compiler_params=pltpu.CompilerParams(vmem_limit_bytes=vmem),
        cost_estimate=pl.CostEstimate(flops=6*S*D*D,bytes_accessed=16*S*D+6*D*D,transcendentals=0),name="token_grad")(w,x,d_middle,gain,*[d for part in parts for d in part])


VMEM_BYTES = 58 << 20
MLP_VMEM_BYTES = 50 << 20
FIT_NODE_COUNT = 512
ridge = 0.5


def fit_constant(nb):
    centers = (np.arange(nb, dtype=np.float64) + 0.5) / nb
    times = (np.arange(FIT_NODE_COUNT, dtype=np.float64) + 0.5) / FIT_NODE_COUNT
    design = np.exp(-0.5 * (times[None, :] - centers[:, None]) ** 2 * (nb * nb))
    table = np.linalg.solve(design @ design.T + ridge * np.eye(nb), design).astype(np.float32)
    hi = table.astype(jnp.bfloat16)
    lo = (table - hi.astype(np.float32)).astype(jnp.bfloat16)
    return np.concatenate([hi, lo], axis=0)


def bits_of(n):
    count = n.bit_length() - 1
    assert 1 << count == n
    return count


def swap(block, stage):
    axis, bit = stage
    n = lax.axis_size(axis)
    return lax.ppermute(block, axis, [(i, i ^ (1 << bit)) for i in range(n)])


class Chain:
    def __init__(self):
        self.last = ()

    def wait(self, *values):
        got = lax.optimization_barrier(values + self.last)
        self.last = got[:1]
        return got[0] if len(values) == 1 else got[: len(values)]


def stage_lists():
    rows = bits_of(lax.axis_size("row"))
    cols = bits_of(lax.axis_size("col"))
    far = [("row", b) for b in range(rows - 1, 1, -1)]
    col = [("col", b) for b in range(cols - 1, -1, -1)]
    near = [("row", 1)] if rows > 1 else []
    return far, col, near, [("row", 0)]


def slot_offsets(order):
    table = []
    for slot in range(1 << len(order)):
        flips = {"row": 0, "col": 0}
        for i, (axis, bit) in enumerate(order):
            if slot >> i & 1:
                flips[axis] ^= 1 << bit
        table.append((flips["row"], flips["col"]))
    return table


def place_bits():
    rows, cols = bits_of(lax.axis_size("row")), bits_of(lax.axis_size("col"))
    return [("row", b) for b in range(rows - 1, -1, -1)] + [("col", b) for b in range(cols - 1, -1, -1)]


def by_place(slots, order):
    seen = order[::-1]
    dims = [seen.index(p) for p in place_bits()]
    split = slots.reshape((2,) * len(order) + slots.shape[1:])
    tail = range(len(order), split.ndim)
    return split.transpose(dims + list(tail)).reshape(slots.shape)


def by_slot(blocks, order):
    places = place_bits()
    dims = [places.index(p) for p in order[::-1]]
    split = blocks.reshape((2,) * len(order) + blocks.shape[1:])
    tail = range(len(order), split.ndim)
    return split.transpose(dims + list(tail)).reshape(blocks.shape)


def flipped(blocks, row, col):
    places = place_bits()
    split = blocks.reshape((2,) * len(places) + blocks.shape[1:])
    for dim, (axis, bit) in enumerate(places):
        mine = (row if axis == "row" else col) >> bit & 1
        split = jnp.where(mine == 1, jnp.flip(split, dim), split)
    return split.reshape(blocks.shape)


class Gather:
    def __init__(self, block, order, done=0):
        self.held, self.order, self.done = (block if done else block[None]), order, done

    def send(self):
        self.came = swap(self.held, self.order[self.done])
        return self

    def take(self, came):
        self.done += 1
        if self.done == len(self.order):
            self.came = came
        else:
            self.held = jnp.concatenate([self.held, came], axis=0)
        return self

    def halves(self, cut, orders):
        return [
            Gather(self.held[:, :, :cut], orders[0], self.done),
            Gather(self.held[:, :, cut:], orders[1], self.done),
        ]


def advance(chain, *gathers):
    got = chain.wait(*[g.came for g in gathers])
    got = got if len(gathers) > 1 else (got,)
    for g, came in zip(gathers, got):
        g.take(came)
        if g.done < len(g.order):
            g.send()


def copy_kernel(plans, place_ref, *refs):
    sem = refs[-1]
    copies = []
    for src, dst, fr, fc, rows, cols, slot, at, column, width, outward in plans:
        r = place_ref[0] ^ fr
        c = place_ref[1] ^ fc
        matrix, slots = (refs[dst], refs[src]) if outward else (refs[src], refs[dst])
        block = matrix.at[
            pl.ds(pl.multiple_of(r * rows, 8), rows), pl.ds(pl.multiple_of(c * cols + column, 128), width)
        ]
        piece = slots.at[slot, :, pl.ds(at, width)]
        pair = (piece, block) if outward else (block, piece)
        copies.append(pltpu.make_async_copy(*pair, sem.at[len(copies)]))
    for copy in copies:
        copy.start()
    for copy in copies:
        copy.wait()


def copy_call(plans, place, ins, out_shapes, resident, name):
    hbm = pl.BlockSpec(memory_space=pl.ANY)
    size = sum(math.prod(o.shape) for o in out_shapes)
    return pl.pallas_call(
        functools.partial(copy_kernel, plans),
        grid_spec=pltpu.PrefetchScalarGridSpec(
            num_scalar_prefetch=1,
            grid=(1,),
            in_specs=[hbm] * len(ins),
            out_specs=[whole(o.shape) if resident else hbm for o in out_shapes],
            scratch_shapes=[pltpu.SemaphoreType.DMA((len(plans),))],
        ),
        out_shape=out_shapes,
        compiler_params=pltpu.CompilerParams(vmem_limit_bytes=24 << 20),
        cost_estimate=pl.CostEstimate(flops=0, bytes_accessed=4 * size, transcendentals=0),
        name=name,
    )(place, *ins)


def ranges_of(layout, offset, width):
    found, at = [], 0
    for i, size in enumerate(layout):
        low, high = max(at, offset), min(at + size, offset + width)
        if low < high:
            found.append((i, low - offset, low - at, high - low))
        at += size
    return found


def assemble(place, gathers, layout, n_rows, n_cols):
    rows = gathers[0].held.shape[1]
    shapes = [jax.ShapeDtypeStruct((rows * n_rows, w * n_cols), jnp.bfloat16) for w in layout]
    pieces, plans, offset = [], [], 0
    aligned = rows % 8 == 0 and all(w % 128 == 0 for w in layout)
    if not aligned:
        full = []
        for g in gathers:
            slots = jnp.concatenate([g.held, g.came], axis=0)
            full.append(flipped(by_place(slots, g.order), place[0], place[1]))
        full = jnp.concatenate(full, axis=2)
        res, at = [], 0
        for w in layout:
            block = full[:, :, at : at + w].reshape(n_rows, n_cols, rows, w)
            res.append(block.transpose(0, 2, 1, 3).reshape(rows * n_rows, w * n_cols))
            at += w
        return res
    for g in gathers:
        table = slot_offsets(g.order)
        width = g.held.shape[2]
        for slot, (fr, fc) in enumerate(table):
            src = len(pieces) + slot // (len(table) // 2)
            for i, at, column, w in ranges_of(layout, offset, width):
                plans.append((src, i, fr, fc, rows, layout[i], slot % (len(table) // 2), at, column, w, True))
        pieces += [g.held, g.came]
        offset += width
    plans = [(p[0], len(pieces) + p[1]) + p[2:] for p in plans]
    return copy_call(plans, place, pieces, shapes, True, "assemble")


class Scatter:
    def __init__(self, keep, send, order):
        self.order, self.left = order, len(order)
        self.terms, self.out = [keep], send
        self.total = None

    def send(self):
        self.left -= 1
        self.came = swap(self.out, self.order[self.left])
        return self

    def take(self, came):
        self.terms.append(came)
        if self.left == 0:
            self.total = sum(t.astype(jnp.float32) for t in self.terms)[0]
            return self
        half = self.terms[0].shape[0] // 2
        self.out = sum(t[half:].astype(jnp.float32) for t in self.terms).astype(jnp.bfloat16)
        self.terms = [t[:half] for t in self.terms]
        return self


def onward(chain, *scatters):
    got = chain.wait(*[s.came for s in scatters])
    got = got if len(scatters) > 1 else (got,)
    for s, came in zip(scatters, got):
        s.take(came)
        if s.left:
            s.send()


def disperse(place, grads, cuts, n_rows, n_cols):
    rows = grads[0].shape[0] // n_rows
    blocks = [g.reshape(n_rows, rows, n_cols, -1).transpose(0, 2, 1, 3) for g in grads]
    joined = jnp.concatenate(blocks, axis=3).reshape(n_rows * n_cols, rows, -1)
    joined = flipped(joined, place[0], place[1])
    res, offset = [], 0
    for width, order in cuts:
        slots = by_slot(joined[:, :, offset : offset + width], order)
        res.append(Scatter(slots[: len(slots) // 2], slots[len(slots) // 2 :], order))
        offset += width
    return res


def shards(
    tokens, w_qkv, w_out, w_mem, w_fc, w_proj, gain_attn, bias_attn, gain_mlp, bias_mlp, b_out, b_fc, b_proj,
    w_loc, w_spread, past_states, sticky_pos, seq_lengths, d_out,
):
    bf, f32 = jnp.bfloat16, jnp.float32
    n_rows, n_cols = lax.axis_size("row"), lax.axis_size("col")
    row, col = lax.axis_index("row"), lax.axis_index("col")
    place = jnp.stack([row, col]).astype(jnp.int32)
    batches, _, span, feat = tokens.shape
    heads, nb = w_loc.shape[0], w_loc.shape[1] * n_rows * n_cols
    hidden = w_fc.shape[1] * n_cols
    assert batches == 2 and n_cols % 2 == 0
    side = col % 2
    own, other = side, 1 - side
    first = (col - side) * span
    far, along, near, core = stage_lists()
    zyx, zxy, yzx = far + along + near + core, far + near + along + core, along + far + near + core
    devices = n_rows * n_cols

    def pick(a, i):
        return lax.dynamic_index_in_dim(a, i, 0, keepdims=False)

    def to_chunk(mine, came):
        two = jnp.stack([mine, came])
        return jnp.where(side == 0, two, two[::-1]).reshape((2 * span,) + mine.shape[1:])

    def trade(a):
        return swap(a, ("col", 0))

    tokens, past, d_out = tokens[:, 0], past_states[:, 0], d_out[:, 0]
    sticky, lengths = sticky_pos[:, 0], seq_lengths[:, 0]
    length = pick(lengths, own)
    info = jnp.stack([length, first, row, col]).astype(jnp.int32)

    singles = [gain_attn, bias_attn, gain_mlp, bias_mlp, b_out, b_proj, b_fc]
    n_single, n_small = len(singles), len(singles) + heads
    rows_small = -(-n_small // 8) * 8
    both_w = jnp.concatenate([w_loc, w_spread], axis=1)

    def wide(v):
        v = v.reshape(-1, v.shape[-1])
        return jnp.pad(v, ((0, 0), (0, 128 - v.shape[1])))

    layout1 = [w_qkv.shape[1], w_mem.shape[1]]
    layout2 = [w_fc.shape[1], w_out.shape[1]]
    layout3 = [w_proj.shape[1]]
    width1 = sum(layout1)
    cut1 = (width1 // 128 + 1) // 2 * 128
    rows1 = w_qkv.shape[0]
    fb = 768
    direct = n_cols == 2 and all(w % 128 == 0 for w in layout1 + layout2 + layout3) and rows1 % 16 == 0
    steps = hidden // fb
    direct = direct and layout2[0] % fb == 0 and fb % w_proj.shape[0] == 0 and steps & (steps - 1) == 0

    def loads_of(gathers, layout, base, first):
        loads, pieces, offset = [], [], 0
        for g in gathers:
            table = slot_offsets(g.order)
            half, width = len(table) // 2, g.held.shape[2]
            for slot, (fr, fc) in enumerate(table):
                for i, at, column, w in ranges_of(layout, offset, width):
                    src = first + len(pieces) + slot // half
                    loads.append((src, base + i, fr, fc, g.held.shape[1], layout[i], slot % half, at, column, w))
            pieces += [g.held, g.came]
            offset += width
        return loads, pieces

    chain = Chain()
    g1 = Gather(jnp.concatenate([w_qkv, w_mem], axis=1), zyx).send()
    tokens_out, block2 = chain.wait(tokens, jnp.concatenate([w_fc, w_out], axis=1))
    came_tokens = trade(pick(tokens_out, other))
    g2 = Gather(block2, yzx).send()
    g3 = Gather(w_proj, zxy)
    flat = jnp.concatenate([wide(v) for v in singles + [both_w]])
    flat = jnp.pad(flat, ((0, rows_small - n_small), (0, 0)))
    g0 = None
    for _ in far[1:]:
        advance(chain, g1)
        if g0 is None:
            g0 = Gather(chain.wait(flat), zyx).send()
    g1.take(chain.wait(g1.came))
    g1a, g1b = g1.halves(cut1, (zyx, zxy))
    g1a.send()
    g1b.send()
    advance(chain, g0)
    g3.held = chain.wait(g3.held)
    g3.send()
    for _ in far[1:]:
        advance(chain, g3)
    for _ in along:
        advance(chain, g2)
    advance(chain, g0)
    advance(chain, g1b, g1a)

    fit = jnp.asarray(fit_constant(nb))
    here = col * span
    past, sticky = chain.wait(past, sticky)

    def basis_part(i):
        spots = pick(sticky, i) - here
        resident = (spots >= 0) & (spots < span)
        picked = jnp.take(past.reshape(-1, feat), jnp.clip(spots, 0, span - 1) + i * span, axis=0)
        parts = jnp.dot(fit * resident.astype(bf)[None, :], picked, preferred_element_type=f32)
        return parts[:nb] + parts[nb:]

    came_g3 = chain.wait(g3.came)
    if n_cols == 2:
        own_basis, basis_out = chain.wait(basis_part(own), basis_part(other).astype(bf))
    else:
        both = lax.psum(jnp.stack([basis_part(i).astype(bf) for i in range(2)]), "col")
        own_basis, came_basis = pick(both, own).astype(f32), jnp.zeros((nb, feat), bf)
    advance(chain, g0)
    for _ in far[1:]:
        advance(chain, g2)
    x = to_chunk(pick(tokens, own), chain.wait(came_tokens))
    while g1b.done < len(g1b.order) - 1:
        advance(chain, g1b, g1a)
    if n_cols == 2:
        came_basis = trade(chain.wait(basis_out))
    g3.take(chain.wait(came_g3)).send()
    came_out = trade(chain.wait(pick(d_out, other)))
    while g0.done < len(g0.order) - 1:
        advance(chain, g0)
    g0.came = chain.wait(g0.came)
    every = flipped(by_place(jnp.concatenate([g0.held, g0.came], axis=0), zyx), row, col)
    share, width = w_loc.shape[1], gain_attn.shape[0]

    def rows_of(first, count):
        return every[:, first : first + count, :width].transpose(1, 0, 2).reshape(count, feat).astype(f32)

    vec1 = jnp.pad(rows_of(0, 2), ((0, 6), (0, 0)))
    advance(chain, g2)
    x, vec1 = chain.wait(x, vec1)
    g1b.came, g1a.came, came_basis = chain.wait(g1b.came, g1a.came, came_basis)

    if direct:
        loads, pieces = loads_of([g1a, g1b], layout1, 0, 0)
    else:
        pieces = assemble(place, [g1a, g1b], layout1, n_rows, n_cols)
        loads = [(i, i) + (None,) * 8 for i in range(2)]
    nT, qkv, mem_kv, basisT, wq = project_qkv(info, x, vec1, own_basis, came_basis, pieces, loads, heads // 2, VMEM_BYTES)
    qkv, every = chain.wait(qkv, every)
    vec2 = jnp.pad(rows_of(2, 4), ((0, 4), (0, 0)))
    bfc = every[:, n_single - 1, : b_fc.shape[0]].astype(f32).reshape(1, -1)
    loc, spr = [
        every[:, n_single:n_small, at : at + share].transpose(1, 0, 2).reshape(heads // 2, 2, nb) for at in (0, share)
    ]
    wls = jnp.concatenate([loc, spr, jnp.zeros((heads // 2, 4, nb), bf)], axis=1)
    for _ in along[:1]:
        advance(chain, g3)
    g_other = chain.wait(came_out)
    halo = 0 if n_cols == 2 else WINDOW
    pairs = heads // 2
    route = [(i, i + 2) for i in range(n_cols - 2)]
    back = [(i + 2, i) for i in range(n_cols - 2)]
    if halo:
        before = lax.ppermute(qkv[-halo:, feat:], "col", route)
        kvx = jnp.concatenate([before, qkv[:, feat:]], axis=0)
        kv = (kvx, 0, kvx, pairs)
    else:
        kv = (qkv, pairs, qkv, 2 * pairs)
    mem_kv, g2.held, g3.held = chain.wait(mem_kv, g2.held, g3.held)
    context, lse = attention_forward(info, qkv, kv, halo, mem_kv, wls, heads, VMEM_BYTES)
    context = chain.wait(context)
    while g3.done < len(g3.order) - 1:
        advance(chain, g3)
    while g2.done < len(g2.order) - 1:
        advance(chain, g2)
    g_chunk = to_chunk(pick(d_out, own), g_other)
    g3.came, g2.came = chain.wait(g3.came, g2.came)

    if direct:
        loads, pieces = loads_of([g2], layout2, 0, 0)
        loads3, pieces3 = loads_of([g3], layout3, 2, len(pieces))
        loads = loads + loads3
        pieces = [pltpu.with_memory_space_constraint(piece, pltpu.VMEM) for piece in pieces + pieces3]
    else:
        wf, wo = assemble(place, [g2], layout2, n_rows, n_cols)
        wp = assemble(place, [g3], layout3, n_rows, n_cols)[0]
        pieces = [wf, wo, wp]
        loads = [(i, i) + (None,) * 8 for i in range(3)]
    output, d_middle, d_context, g_vec, g_bfc, *cut_grads = mlp_block(
        info, context, x, g_chunk, pieces, loads, vec2, bfc,
        (n_rows, n_cols, yzx, zxy) if direct else None, layout2, MLP_VMEM_BYTES, fb,
    )

    def from_chunk(chunk):
        halves = chunk.reshape(2, span, feat)
        return pick(halves, own), pick(halves, other)

    def paired(kept, came):
        two = jnp.stack([kept, came])
        return jnp.where(side == 0, two, two[::-1])[:, None]

    if direct:
        s2, s3 = Scatter(*cut_grads[:2], yzx), Scatter(*cut_grads[2:], zxy)
    else:
        s2 = disperse(place, cut_grads[:2], [(sum(layout2), yzx)], n_rows, n_cols)[0]
        s3 = disperse(place, cut_grads[2:], [(sum(layout3), zxy)], n_rows, n_cols)[0]
    s2.send()
    s3.send()
    d_context, s2.terms[0], s3.terms[0] = chain.wait(d_context, s2.terms[0], s3.terms[0])

    def taken(*scatters):
        got = chain.wait(*[s.came for s in scatters])
        for s, came in zip(scatters, got if len(scatters) > 1 else (got,)):
            s.take(came)
        outs = chain.wait(*[s.out for s in scatters])
        for s, out in zip(scatters, outs if len(scatters) > 1 else (outs,)):
            s.out = out
            s.send()

    count = pairs // 2
    mixed, parts = [], []
    kept_out, sent = from_chunk(output)
    d_context, sent = chain.wait(d_context, sent)
    came_output = trade(sent)
    for i in range(count):
        d_context = chain.wait(d_context)
        got = list(
            attention_backward(info, qkv, kv, halo, mem_kv, wls, lse, d_context, heads, VMEM_BYTES, i, 2, count)
        )
        got[0] = chain.wait(got[0])
        mixed.append(got)
        d_q, d_k, d_v, d_mk, d_mv, _ = got
        if halo:
            d_kv = jnp.concatenate([d_k, d_v], axis=1)
            ret = lax.ppermute(d_kv[:halo], "col", back)
            d_kv = d_kv[halo:].astype(f32) + jnp.pad(ret.astype(f32), ((2 * span - halo, 0), (0, 0)))
            d_kv = d_kv.astype(bf)
            d_k, d_v = jnp.split(d_kv, 2, axis=1)
        parts.append((d_q, d_k, d_v, d_mk, d_mv))
        if i == 0:
            came_output = chain.wait(came_output)
            taken(s2, s3)
        if i == count - 2 and direct:
            s1 = weight_grads(info, nT, basisT, parts, n_rows, [(len(parts) * 5 * (feat // pairs), zxy)], VMEM_BYTES)
            s1[0].send()
            s1[0].terms[0] = chain.wait(s1[0].terms[0])
    taken(s3)
    taken(s2)
    if direct:
        taken(s1[0])
    d_middle = chain.wait(d_middle)
    d_tok, g_vec1 = token_grad([p[:3] for p in parts], wq, x, d_middle, vec1[0:1], VMEM_BYTES)
    d_tok, g_vec1 = chain.wait(d_tok, g_vec1)
    taken(s3)
    taken(s2)
    kept_x, sent_x = from_chunk(d_tok)
    came_x = trade(chain.wait(sent_x.astype(bf)))
    nT = chain.wait(nT)
    if direct:
        s1 += weight_grads(info, nT, basisT, parts[-1:], n_rows, [(5 * (feat // pairs), zyx)], VMEM_BYTES)
        s1[1].send()
    else:
        ordered = [jnp.stack([p[k].reshape(p[k].shape[0], 2, -1) for p in parts], axis=2) for k in range(5)]
        ordered = [a.reshape(a.shape[0], feat) for a in ordered]
        g_qkv = jnp.dot(nT, jnp.concatenate(ordered[:3], axis=1), preferred_element_type=f32).astype(bf)
        g_mem = jnp.dot(basisT, jnp.concatenate(ordered[3:], axis=1), preferred_element_type=f32).astype(bf)
        s1 = disperse(place, [g_qkv, g_mem], [(cut1, zyx), (width1 - cut1, zxy)], n_rows, n_cols)
        for s_ in s1:
            s_.send()
    s1[-1].terms[0] = chain.wait(s1[-1].terms[0])
    by_pair = [m[5][j] for j in range(2) for m in mixed]
    total = jnp.concatenate([g_vec, g_vec1, g_bfc] + by_pair, axis=1)
    stages = core + far + along + near
    came = swap(total.astype(bf), stages.pop(0))
    last, early = s1[-1], s1[0]
    everyone = [last, early, s3, s2]
    plan = [last, early, None, last, early, s3, None, last, came_x, early, s2, None, last, early, s3, None, last, s2, None]
    while any(s_.total is None for s_ in everyone) or came is not None:
        s_ = plan.pop(0) if plan else next((s_ for s_ in everyone if s_.total is None), None)
        if s_ is came_x:
            came_x = chain.wait(came_x)
        elif s_ is None:
            if came is not None:
                total = total + chain.wait(came).astype(f32)
                came = swap(total.astype(bf), stages.pop(0)) if stages else None
        elif s_.left:
            onward(chain, s_)
        elif s_.total is None:
            s_.take(chain.wait(s_.came))
    index = row * n_cols + col

    def mine(block, first, width):
        return lax.dynamic_slice_in_dim(block, first + index * width, width, axis=1)

    g_bo, g_gain2, g_bias2, g_bp = mine(total, 0, gain_mlp.shape[0])[:4]
    g_gain1, g_bias1 = mine(total, feat, gain_attn.shape[0])[:2]
    g_bf = mine(total, 2 * feat, b_fc.shape[0])[0]
    per_pair = total[:, 2 * feat + hidden :].reshape(8, pairs, nb).transpose(1, 0, 2)
    g_loc = lax.dynamic_slice_in_dim(per_pair[:, 0:2].reshape(heads, nb), index * share, share, axis=1)
    g_spread = lax.dynamic_slice_in_dim(per_pair[:, 2:4].reshape(heads, nb), index * share, share, axis=1)
    outputs = paired(kept_out, came_output)
    grad_x = paired(kept_x, came_x.astype(f32))
    joined = jnp.concatenate([s_.total for s_ in s1], axis=1)
    if direct:
        w = feat // pairs
        n_qkv = layout1[0] // (count * w)
        blocks = joined.reshape(rows1, count, 5, w)
        grad_qkv = blocks[:, :, :n_qkv].transpose(0, 2, 1, 3).reshape(rows1, layout1[0])
        grad_mem = blocks[:, :, n_qkv:].transpose(0, 2, 1, 3).reshape(rows1, layout1[1])
    else:
        grad_qkv, grad_mem = joined[:, : layout1[0]], joined[:, layout1[0] :]
    grad_fc, grad_out = s2.total[:, : layout2[0]], s2.total[:, layout2[0] :]
    grad_proj = s3.total
    return (
        outputs, grad_x, grad_qkv, grad_out, grad_mem, grad_fc, grad_proj,
        g_gain1, g_bias1, g_gain2, g_bias2, g_bo, g_bf, g_bp, g_loc, g_spread,
    )


def solution(mesh):
    grid, both, tail = P("row", "col"), P(("row", "col")), P(None, ("row", "col"))
    act, rows = P(None, "row", "col", None), P(None, "row")
    return jax.shard_map(
        shards,
        mesh=mesh,
        in_specs=(act,) + (grid,) * 5 + (both,) * 7 + (tail,) * 2 + (act, P(None, "row", None), rows, act),
        out_specs=(act, act) + (grid,) * 5 + (both,) * 7 + (tail,) * 2,
        check_vma=False,
    )
```

```python
import functools
import math

import jax
import jax.numpy as jnp
import numpy as np
from jax import lax
from jax.experimental import pallas as pl
from jax.experimental.pallas import tpu as pltpu
from jax.sharding import PartitionSpec as P

WINDOW=512; TILE=256; masked=-1e30
var_scale=0.01
NT=(((1,),(1,)),((),()))
NN=(((1,),(0,)),((),()))

def dot_nt(a,b): return lax.dot_general(a,b,NT,preferred_element_type=jnp.float32)
def dot_nn(a,b): return lax.dot_general(a,b,NN,preferred_element_type=jnp.float32)

def split3(v):
    hi=v.astype(jnp.bfloat16); r=v-hi.astype(jnp.float32)
    mid=r.astype(jnp.bfloat16); lo=(r-mid.astype(jnp.float32)).astype(jnp.bfloat16)
    return hi,mid,lo

def lane_is_first(shape,half):
    return lax.broadcasted_iota(jnp.int32,shape,1)<half

def tile_biases(info_ref,first_key,has_far,has_mid):
    key=lax.broadcasted_iota(jnp.int32,(TILE,TILE),0)
    qry=lax.broadcasted_iota(jnp.int32,(TILE,TILE),1)
    tri=key<=qry
    length=info_ref[0]
    diag_pos=first_key+key
    far_pos=diag_pos-WINDOW
    near=jnp.where((diag_pos<length)|(key==qry),0.0,masked)
    far=jnp.where((far_pos>=0)&(far_pos<length),0.0,masked) if has_far else masked
    comb=jnp.where(tri,near,far)
    mid_pos=diag_pos-TILE
    mid=jnp.where((mid_pos>=0)&(mid_pos<length),0.0,masked)
    return comb,mid

def density_rows(wls,mk,half):
    vec=dot_nn(wls,mk)
    row=lax.broadcasted_iota(jnp.int32,vec.shape,0)
    lane=lax.broadcasted_iota(jnp.int32,vec.shape,1)
    return jnp.where((row%2==0)==(lane<half),vec,0.0)

def logits_of(vec,qb):
    hi,mid,lo=split3(vec)
    parts=dot_nt(jnp.concatenate([hi,mid,lo,lo],axis=0),qb)
    return (parts[16:24]+parts[8:16])+parts[0:8]

def spreads(logits,nb):
    location=1.0/(1.0+jnp.exp(-logits))
    soft=jnp.maximum(logits,0.0)+jnp.log1p(jnp.exp(-jnp.abs(logits)))
    spread=var_scale*soft+1.0/(nb*nb)
    return location,spread

def fwd_kernel(halo,half,info_ref,q_ref,k_ref,v_ref,mk_ref,mv_ref,wls_ref,ctx_ref,lse_ref,bias_ref):
    S=q_ref.shape[0]; nblk=S//TILE; nb=mk_ref.shape[0]; ht=halo//TILE
    @pl.when(pl.program_id(0)==0)
    def _():
        for i in range(nblk):
            comb,mid=tile_biases(info_ref,info_ref[1]+i*TILE,ht+i>=2,ht+i>=1)
            bias_ref[2*i]=comb; bias_ref[2*i+1]=mid
    tri=lax.broadcasted_iota(jnp.int32,(TILE,TILE),0)<=lax.broadcasted_iota(jnp.int32,(TILE,TILE),1)
    trib=jnp.where(tri,1.0,0.0).astype(jnp.bfloat16)
    lane=lax.broadcasted_iota(jnp.int32,(16,2*half),1)
    sides=[jnp.where(lane<half,1.0,0.0)[0:1].astype(jnp.bfloat16),jnp.where(lane<half,0.0,1.0)[0:1].astype(jnp.bfloat16)]
    centers=(lax.broadcasted_iota(jnp.int32,(nb,TILE),0).astype(jnp.float32)+0.5)/nb
    vec=density_rows(wls_ref[0],mk_ref[...],half)
    vT=v_ref[...].T
    mvT=mv_ref[...].T
    lse_ref[...]=jnp.zeros_like(lse_ref)
    for i in range(nblk):
        rows=slice(i*TILE,(i+1)*TILE)
        qb=q_ref[rows,:]*jnp.bfloat16(half**-0.5)
        d0=halo+i*TILE
        has_mid=ht+i>=1; has_far=ht+i>=2
        kd=k_ref[d0:d0+TILE,:]
        logits=logits_of(vec,qb)
        location,spread=spreads(logits,nb)
        nis=-0.5/spread
        norm=lax.rsqrt(2.0*math.pi*spread)*(1.0/nb)
        outs=[]
        for x in range(2):
            qx=qb*sides[x]
            vx=vT[x*half:(x+1)*half,:]
            sd=dot_nt(kd,qx)
            if has_far:
                sf=dot_nt(k_ref[d0-2*TILE:d0-TILE,:],qx)
                sc=jnp.where(tri,sd,sf)+bias_ref[2*i]
            else:
                sc=sd+bias_ref[2*i]
            top=jnp.max(sc,axis=0,keepdims=True)
            if has_mid:
                sm=dot_nt(k_ref[d0-TILE:d0,:],qx)+bias_ref[2*i+1]
                top=jnp.maximum(top,jnp.max(sm,axis=0,keepdims=True))
            ec=jnp.exp(sc-top)
            tot=jnp.sum(ec,axis=0,keepdims=True)
            ecl=ec.astype(jnp.bfloat16)
            if has_far:
                near=ecl*trib
                o=dot_nn(vx[:,d0:d0+TILE],near)+dot_nn(vx[:,d0-2*TILE:d0-TILE],ecl-near)
            else:
                o=dot_nn(vx[:,d0:d0+TILE],ecl)
            if has_mid:
                em=jnp.exp(sm-top)
                tot=tot+jnp.sum(em,axis=0,keepdims=True)
                o=o+dot_nn(vx[:,d0-TILE:d0],em.astype(jnp.bfloat16))
            lse_ref[0,x:x+1,rows]=top+jnp.log(tot)
            o=o*(1.0/tot)
            z=location[x:x+1]-centers
            e=jnp.exp(nis[2+x:3+x]*(z*z))
            r=dot_nn(mvT[x*half:(x+1)*half,:],e.astype(jnp.bfloat16))*norm[2+x:3+x]
            outs.append(o+r)
        ctx_ref[rows,:]=jnp.concatenate(outs,axis=0).T.astype(jnp.bfloat16)

def bwd_kernel(halo,half,info_ref,q_ref,k_ref,v_ref,mk_ref,mv_ref,wls_ref,lse_ref,do_ref,
               dq_ref,dk_ref,dv_ref,dmk_ref,dmv_ref,gls_ref,bias_ref,dk_acc,dv_acc):
    S=q_ref.shape[0]; nblk=S//TILE; nb=mk_ref.shape[0]; ht=halo//TILE
    @pl.when(pl.program_id(0)==0)
    def _():
        for i in range(nblk):
            comb,mid=tile_biases(info_ref,info_ref[1]+i*TILE,ht+i>=2,ht+i>=1)
            bias_ref[2*i]=comb; bias_ref[2*i+1]=mid
    tri=lax.broadcasted_iota(jnp.int32,(TILE,TILE),0)<=lax.broadcasted_iota(jnp.int32,(TILE,TILE),1)
    trib=jnp.where(tri,1.0,0.0).astype(jnp.bfloat16)
    lane=lax.broadcasted_iota(jnp.int32,(16,2*half),1)
    sides=[jnp.where(lane<half,1.0,0.0)[0:1].astype(jnp.bfloat16),jnp.where(lane<half,0.0,1.0)[0:1].astype(jnp.bfloat16)]
    centers=(lax.broadcasted_iota(jnp.int32,(nb,TILE),0).astype(jnp.float32)+0.5)/nb
    mk=mk_ref[...]; mv=mv_ref[...]
    vec=density_rows(wls_ref[0],mk,half)
    vecT=vec.T
    kT=k_ref[...].T
    dk_acc[...]=jnp.zeros_like(dk_acc); dv_acc[...]=jnp.zeros_like(dv_acc)
    dmv=jnp.zeros((nb,2*half),jnp.float32)
    dvec=jnp.zeros((8,2*half),jnp.float32)
    for i in range(nblk):
        rows=slice(i*TILE,(i+1)*TILE)
        qb=q_ref[rows,:]*jnp.bfloat16(half**-0.5)
        dob=do_ref[rows,:]
        d0=halo+i*TILE
        has_mid=ht+i>=1; has_far=ht+i>=2
        dg=slice(d0,d0+TILE); md=slice(d0-TILE,d0); fr=slice(d0-2*TILE,d0-TILE)
        logits=logits_of(vec,qb)
        location,spread=spreads(logits,nb)
        inv=1.0/spread
        nis=-0.5*inv
        norm=lax.rsqrt(2.0*math.pi*spread)*(1.0/nb)
        outs=[]; s0s=[]; s1s=[]; s2s=[]
        for x in range(2):
            qx=qb*sides[x]
            dox=dob*sides[x]
            kx=kT[x*half:(x+1)*half,:]
            lse=lse_ref[0,x:x+1,rows]
            sc=dot_nt(k_ref[dg,:],qx)
            dpc=dot_nt(v_ref[dg,:],dox)
            if has_far:
                sc=jnp.where(tri,sc,dot_nt(k_ref[fr,:],qx))
                dpc=jnp.where(tri,dpc,dot_nt(v_ref[fr,:],dox))
            pc=jnp.exp(sc+bias_ref[2*i]-lse)
            delta=jnp.sum(pc*dpc,axis=0,keepdims=True)
            if has_mid:
                sm=dot_nt(k_ref[md,:],qx)
                dpm=dot_nt(v_ref[md,:],dox)
                pm=jnp.exp(sm+bias_ref[2*i+1]-lse)
                delta=delta+jnp.sum(pm*dpm,axis=0,keepdims=True)
                dsm=(pm*(dpm-delta)).astype(jnp.bfloat16)
                dv_acc[md,:]+=dot_nn(pm.astype(jnp.bfloat16),dox)
                dk_acc[md,:]+=dot_nn(dsm,qx)
            dsc=(pc*(dpc-delta)).astype(jnp.bfloat16)
            pcl=pc.astype(jnp.bfloat16)
            if has_far:
                dsd=dsc*trib; dsf=dsc-dsd
                near=pcl*trib
                dv_acc[dg,:]+=dot_nn(near,dox)
                dv_acc[fr,:]+=dot_nn(pcl-near,dox)
                dk_acc[dg,:]+=dot_nn(dsd,qx)
                dk_acc[fr,:]+=dot_nn(dsf,qx)
                dq=dot_nn(kx[:,dg],dsd)+dot_nn(kx[:,fr],dsf)
            else:
                dv_acc[dg,:]+=dot_nn(pcl,dox)
                dk_acc[dg,:]+=dot_nn(dsc,qx)
                dq=dot_nn(kx[:,dg],dsc)
            if has_mid:
                dq=dq+dot_nn(kx[:,md],dsm)
            outs.append(dq)
            z=location[x:x+1]-centers
            e=jnp.exp(nis[2+x:3+x]*(z*z))
            g=dot_nt(mv,dox)*e
            gz=g*z
            s0s.append(jnp.sum(g,axis=0,keepdims=True))
            s1s.append(jnp.sum(gz,axis=0,keepdims=True))
            s2s.append(jnp.sum(gz*z,axis=0,keepdims=True))
            dmv=dmv+dot_nn((e*norm[2+x:3+x]).astype(jnp.bfloat16),dox)
        n2=norm[2:4]; i2=inv[2:4]
        s0=jnp.concatenate(s0s,axis=0); s1=jnp.concatenate(s1s,axis=0); s2=jnp.concatenate(s2s,axis=0)
        dloc=-(n2*i2)*s1
        dspr=n2*(0.5*i2)*(s2*i2-s0)
        l2=location[0:2]
        dll=dloc*l2*(1.0-l2)
        dsl=dspr*var_scale*location[2:4]
        dl=jnp.concatenate([dll,dsl,jnp.zeros((4,TILE),jnp.float32)],axis=0)
        hi=dl.astype(jnp.bfloat16); lo=(dl-hi.astype(jnp.float32)).astype(jnp.bfloat16)
        both=dot_nn(jnp.concatenate([hi,lo],axis=0),qb)
        dvec=dvec+(both[0:8]+both[8:16])
        for x in range(2):
            seg=slice(x*half,(x+1)*half)
            outs[x]=outs[x]+vecT[seg,x:x+1]*dl[x:x+1]+vecT[seg,2+x:3+x]*dl[2+x:3+x]
        dq_ref[rows,:]=(jnp.concatenate(outs,axis=0)*(half**-0.5)).T.astype(jnp.bfloat16)
    dk_ref[...]=dk_acc[...].astype(jnp.bfloat16)
    dv_ref[...]=dv_acc[...].astype(jnp.bfloat16)
    dmv_ref[...]=dmv.astype(jnp.bfloat16)
    row=lax.broadcasted_iota(jnp.int32,dvec.shape,0)
    lane=lax.broadcasted_iota(jnp.int32,dvec.shape,1)
    dvec=jnp.where((row%2==0)==(lane<half),dvec,0.0)
    hi=dvec.astype(jnp.bfloat16); lo=(dvec-hi.astype(jnp.float32)).astype(jnp.bfloat16)
    stack=jnp.concatenate([hi,lo],axis=0)
    gl=dot_nt(stack,mk)
    gls_ref[0]=gl[0:8]+gl[8:16]
    wT=wls_ref[0].astype(jnp.float32).T.astype(jnp.bfloat16)
    dmk_ref[...]=dot_nn(jnp.concatenate([wT,wT],axis=1),stack).astype(jnp.bfloat16)

def col_block(rows,width,first,stride=1):
    return pl.BlockSpec((rows,width),lambda p,info: (0,first+stride*p))

def attention_forward(info,qkv,kv,halo,mem_kv,wls,heads,vmem):
    S=qkv.shape[0]; pairs=heads//2; width=kv[0].shape[1]
    nb=mem_kv.shape[0]; feat=mem_kv.shape[1]//2; w=feat//pairs; half=w//2
    karr,koff,varr,voff=kv[0],kv[1],kv[2],kv[3]
    nblk=S//TILE
    spec=pltpu.PrefetchScalarGridSpec(num_scalar_prefetch=1,grid=(pairs,),
        in_specs=[col_block(S,w,0),col_block(halo+S,w,koff),col_block(halo+S,w,voff),col_block(nb,w,0),col_block(nb,w,pairs),
                  pl.BlockSpec((1,8,nb),lambda p,info:(p,0,0))],
        out_specs=[col_block(S,w,0),pl.BlockSpec((1,8,S),lambda p,info:(p,0,0))],
        scratch_shapes=[pltpu.VMEM((2*nblk,TILE,TILE),jnp.float32)])
    return pl.pallas_call(functools.partial(fwd_kernel,halo,half),grid_spec=spec,
        out_shape=[jax.ShapeDtypeStruct((S,feat),jnp.bfloat16),jax.ShapeDtypeStruct((pairs,8,S),jnp.float32)],
        compiler_params=pltpu.CompilerParams(vmem_limit_bytes=vmem,dimension_semantics=("arbitrary",)),
        cost_estimate=pl.CostEstimate(flops=24*S*S*feat//4,bytes_accessed=10*S*feat,transcendentals=heads*S*768),
        name="mix_forward")(info,qkv,karr,varr,mem_kv,mem_kv,wls)

def attention_backward(info,qkv,kv,halo,mem_kv,wls,lse,d_context,heads,vmem,begin,count,stride):
    S=qkv.shape[0]; pairs=heads//2
    nb=mem_kv.shape[0]; feat=mem_kv.shape[1]//2; w=feat//pairs; half=w//2
    karr,koff,varr,voff=kv
    nblk=S//TILE; bf=jnp.bfloat16
    spec=pltpu.PrefetchScalarGridSpec(num_scalar_prefetch=1,grid=(count,),
        in_specs=[col_block(S,w,begin,stride),col_block(halo+S,w,koff+begin,stride),col_block(halo+S,w,voff+begin,stride),
                  col_block(nb,w,begin,stride),col_block(nb,w,pairs+begin,stride),pl.BlockSpec((1,8,nb),lambda p,info:(begin+stride*p,0,0)),
                  pl.BlockSpec((1,8,S),lambda p,info:(begin+stride*p,0,0)),col_block(S,w,begin,stride)],
        out_specs=[col_block(S,w,0),col_block(halo+S,w,0),col_block(halo+S,w,0),col_block(nb,w,0),col_block(nb,w,0),
                   pl.BlockSpec((1,8,nb),lambda p,info:(p,0,0))],
        scratch_shapes=[pltpu.VMEM((2*nblk,TILE,TILE),jnp.float32),pltpu.VMEM((halo+S,w),jnp.float32),pltpu.VMEM((halo+S,w),jnp.float32)])
    part=count*w
    return pl.pallas_call(functools.partial(bwd_kernel,halo,half),grid_spec=spec,
        out_shape=[jax.ShapeDtypeStruct((S,part),bf),jax.ShapeDtypeStruct((halo+S,part),bf),jax.ShapeDtypeStruct((halo+S,part),bf),
                   jax.ShapeDtypeStruct((nb,part),bf),jax.ShapeDtypeStruct((nb,part),bf),jax.ShapeDtypeStruct((count,8,nb),jnp.float32)],
        compiler_params=pltpu.CompilerParams(vmem_limit_bytes=vmem,dimension_semantics=("arbitrary",)),
        cost_estimate=pl.CostEstimate(flops=30*S*S*part,bytes_accessed=20*S*part,transcendentals=2*count*S*768),
        name="mix_backward")(info,qkv,karr,varr,mem_kv,mem_kv,wls,lse,d_context)


eps=1e-5
TN=(((0,),(0,)),((),()))
def dot_tn(a,b): return lax.dot_general(a,b,TN,preferred_element_type=jnp.float32)

def norm_parts(v):
    center=jnp.mean(v,axis=-1,keepdims=True)
    off=v-center
    rstd=lax.rsqrt(jnp.mean(off*off,axis=-1,keepdims=True)+eps)
    return off*rstd,rstd

def norm_back(gd,xhat,rstd):
    return rstd*(gd-jnp.mean(gd,axis=-1,keepdims=True)-xhat*jnp.mean(gd*xhat,axis=-1,keepdims=True))

def whole(shape): return pl.BlockSpec(shape,lambda *a: (0,)*len(shape),pipeline_mode=pl.Buffered(1))

def shard_copies(loads, pieces, targets, sem, row, col, which):
    for n, (src, dst, fr, fc, rows, cols, slot, at, column, width) in enumerate(loads):
        if dst not in which:
            continue
        if rows is None:
            yield pltpu.make_async_copy(pieces[src], targets[dst], sem.at[n])
            continue
        r0 = pl.multiple_of((row ^ fr) * rows, 16)
        c0 = pl.multiple_of((col ^ fc) * cols + column, 128)
        yield pltpu.make_async_copy(
            pieces[src].at[slot, :, pl.ds(at, width)], targets[dst].at[pl.ds(r0, rows), pl.ds(c0, width)], sem.at[n]
        )


def qkv_kernel(loads, pairs, info_ref, x_ref, vec_ref, own_ref, came_ref, *refs):
    count = max(load[0] for load in loads) + 1
    pieces, refs = refs[:count], refs[count:]
    nT_ref, o_ref, mem_ref, bT_ref, wq_ref, wq_s, wm_s, in_sem, out_sem = refs
    i = pl.program_id(0)
    D = wq_s.shape[0]
    w, half = D // pairs, pairs // 2
    outs = []
    for n in range(3 * pairs):
        kind, p, j = n // pairs, n % pairs // 2, n % 2
        at = kind * D + (j * half + p) * w
        copy = pltpu.make_async_copy(wq_s.at[:, at : at + w], wq_ref.at[:, n * w : (n + 1) * w], out_sem.at[n])
        outs.append(copy)

    @pl.when(i == 0)
    def _():
        for begin in (True, False):
            for copy in shard_copies(loads, pieces, (wq_s, wm_s), in_sem, info_ref[2], info_ref[3], (0, 1)):
                copy.start() if begin else copy.wait()
        for out in outs:
            out.start()
        basis = (own_ref[...] + came_ref[...].astype(jnp.float32)).astype(jnp.bfloat16)
        bT_ref[...] = basis.T
        mem_ref[...] = dot_nn(basis, wm_s[...]).astype(jnp.bfloat16)

    xhat, _ = norm_parts(x_ref[...].astype(jnp.float32))
    n = (xhat * vec_ref[0:1] + vec_ref[1:2]).astype(jnp.bfloat16)
    nT_ref[...] = n.T
    o_ref[...] = dot_nn(n, wq_s[...]).astype(jnp.bfloat16)

    @pl.when(i == pl.num_programs(0) - 1)
    def _():
        for out in outs:
            out.wait()


def project_qkv(info, x, vec, own_basis, came_basis, pieces, loads, pairs, vmem, rows=256):
    S, D = x.shape
    nb = own_basis.shape[0]
    bf, sd = jnp.bfloat16, jax.ShapeDtypeStruct
    hbm = pl.BlockSpec(memory_space=pl.ANY)
    return pl.pallas_call(
        functools.partial(qkv_kernel, loads, pairs),
        grid_spec=pltpu.PrefetchScalarGridSpec(
            num_scalar_prefetch=1,
            grid=(S // rows,),
            in_specs=[pl.BlockSpec((rows, D), lambda i, info: (i, 0)), whole((8, D)), whole((nb, D)), whole((nb, D))]
            + [hbm] * len(pieces),
            out_specs=[
                pl.BlockSpec((D, rows), lambda i, info: (0, i)), pl.BlockSpec((rows, 3 * D), lambda i, info: (i, 0)),
                whole((nb, 2 * D)), whole((D, nb)), hbm,
            ],
            scratch_shapes=[
                pltpu.VMEM((D, 3 * D), bf), pltpu.VMEM((D, 2 * D), bf),
                pltpu.SemaphoreType.DMA((len(loads),)), pltpu.SemaphoreType.DMA((3 * pairs,)),
            ],
        ),
        out_shape=[sd((D, S), bf), sd((S, 3 * D), bf), sd((nb, 2 * D), bf), sd((D, nb), bf), sd((D, 3 * D), bf)],
        compiler_params=pltpu.CompilerParams(vmem_limit_bytes=vmem),
        cost_estimate=pl.CostEstimate(
            flops=6 * S * D * D + 4 * nb * D * D, bytes_accessed=10 * S * D + 16 * D * D, transcendentals=0
        ),
        name="project_qkv",
    )(info, x, vec, own_basis, came_basis, *pieces)


def row_slot(fr, order):
    return sum(((fr >> bit) & 1) << i for i, (axis, bit) in enumerate(order[:-1]) if axis == "row")


def col_slot(fc, order):
    return sum(((fc >> bit) & 1) << i for i, (axis, bit) in enumerate(order[:-1]) if axis == "col")


class _Fixed:
    def __init__(self, sem):
        self.at = self
        self.sem = sem

    def __getitem__(self, index):
        return self.sem


def mlp_kernel(steps, chunk, loads, cut, info_ref, c_ref, x_ref, g_ref, vec_ref, bf_ref, *refs):
    count = max(load[0] for load in loads) + 1
    pieces, refs = refs[:count], refs[count:]
    out_ref, dmid_ref, dctx_ref, gv_ref, gb_ref = refs[:5]
    made = 3 if cut is None else 4
    grads, refs = refs[5 : 5 + made], refs[5 + made :]
    n_s, nT_s, dm_s, mid_s, acc_s, dn_s, hid_s, dp_s, wf_s, wo_s, wp_s, go_s, gf_s, gp_s, in_sem, out_sem, go_sem = refs
    f = pl.program_id(0)
    S, D = x_ref.shape
    fb = gf_s.shape[2]
    length, base, row, col = info_ref[0], info_ref[1], info_ref[2], info_ref[3]
    nchunk = S // chunk
    buf = f % 2
    fe, per_col = f, steps
    if cut is not None:
        fe, per_col = f ^ (row // (cut[0] // steps)), steps // cut[1]

    def valid_of(i):
        pos = base + i * chunk + lax.broadcasted_iota(jnp.int32, (chunk, 1), 0)
        return jnp.where(pos < length, 1.0, 0.0)

    targets = (wf_s, wo_s, wp_s)

    def arrive(which, rows=None, cols=None):
        if cut is None:
            for copy in shard_copies(loads, pieces, targets, in_sem, row, col, which):
                copy.wait()
            return
        n_rows, n_cols = cut[:2]
        seen = set()
        for src, dst, _, _, height, across, slot, at, _, width in loads:
            if dst not in which or dst in seen:
                continue
            seen.add(dst)
            for r in range(n_rows) if rows is None else rows:
                for c in range(n_cols) if cols is None else cols:
                    n = (dst * n_rows + r) * n_cols + c
                    pltpu.make_async_copy(
                        pieces[src].at[slot, :, pl.ds(at, width)], targets[dst].at[:height, :width], in_sem.at[n]
                    ).wait()

    def depart(which, only=None):
        for n, load in enumerate(loads):
            if load[1] in which:
                place = n
                if cut is not None:
                    place = (load[1] * cut[0] + (row ^ load[2])) * cut[1] + (col ^ load[3])
                copy = next(shard_copies([load], pieces, targets, _Fixed(in_sem.at[place]), row, col, which))
                if only is None:
                    copy.start()
                else:
                    pl.when((col ^ load[3]) == only)(copy.start)

    def block_copies(begin, buf=buf):
        if cut is None:
            copies = [
                pltpu.make_async_copy(gf_s.at[buf], grads[0].at[:, pl.ds(pl.multiple_of(fe * fb, 128), fb)], out_sem.at[buf, 0]),
                pltpu.make_async_copy(gp_s.at[buf], grads[2].at[pl.ds(pl.multiple_of(fe * fb, 16), fb), :], out_sem.at[buf, 1]),
            ]
            for copy in copies:
                copy.start() if begin else copy.wait()
            return
        n_rows, n_cols, order2, order3 = cut
        rows2, rows3 = D // n_rows, fb * steps // n_rows
        cols2, cols3 = fb * steps // n_cols, D // n_cols
        per = cols2 // fb
        c = fe // per
        at = pl.multiple_of((fe % per) * fb, 128)
        for fr in range(n_rows):
            slot = row_slot(fr, order2) + col_slot(c ^ col, order2)
            src = gf_s.at[buf, pl.ds(pl.multiple_of((row ^ fr) * rows2, 16), rows2), :]
            copy = pltpu.make_async_copy(src, grads[fr & 1].at[slot, :, pl.ds(at, fb)], out_sem.at[buf, fr])
            copy.start() if begin else copy.wait()
        n = n_rows
        for i in range(fb // rows3):
            rel = (fe * (fb // rows3) + i) ^ row
            for c in range(n_cols):
                slot = row_slot(rel, order3) + col_slot(c ^ col, order3)
                src = gp_s.at[buf, i * rows3 : (i + 1) * rows3, c * cols3 : (c + 1) * cols3]
                if begin:
                    for side in range(2):

                        @pl.when(rel & 1 == side)
                        def _():
                            pltpu.make_async_copy(src, grads[2 + side].at[slot], out_sem.at[buf, n]).start()
                else:
                    pltpu.make_async_copy(src, grads[2].at[0], out_sem.at[buf, n]).wait()
                n += 1

    @pl.when(f == 0)
    def _():
        depart((1,))
        if cut is None:
            depart((0, 2))
        else:
            depart((0,), fe // per_col)
        for i in range(nchunk):
            rs = slice(i * chunk, (i + 1) * chunk)
            dm_s[rs, :] = (g_ref[rs, :].astype(jnp.float32) * valid_of(i)).astype(jnp.bfloat16)
        acc_s[...] = jnp.zeros_like(acc_s)
        dn_s[...] = jnp.zeros_like(dn_s)
        if cut is not None:
            depart((2,))
            for c in range(1, cut[1]):
                depart((0,), fe // per_col ^ c)
        arrive((1,))
        for i in range(nchunk):
            rs = slice(i * chunk, (i + 1) * chunk)
            branch = dot_nn(c_ref[rs, :], wo_s[...]) + vec_ref[2:3]
            mid = x_ref[rs, :].astype(jnp.float32) + valid_of(i) * branch
            mid_s[rs, :] = mid
            xhat, _ = norm_parts(mid)
            n = (xhat * vec_ref[0:1] + vec_ref[1:2]).astype(jnp.bfloat16)
            n_s[rs, :] = n
            nT_s[:, rs] = n.T
        if cut is None:
            arrive((0, 2))

    if cut is not None:

        @pl.when(f % per_col == 0)
        def _():
            arrive((0,), None, [fe // per_col])

        each = cut[0] // steps
        arrive((2,), [fe * each + i for i in range(each)])

    @pl.when(f >= 2)
    def _():
        block_copies(False)

    cs = pl.ds(pl.multiple_of(fe * fb, 128), fb)
    wf = wf_s[:, cs]
    wp = wp_s[cs, :]
    c0 = math.sqrt(2.0 / math.pi)
    gb = jnp.zeros((1, fb), jnp.float32)
    for i in range(nchunk):
        rs = slice(i * chunk, (i + 1) * chunk)
        pre = dot_nn(n_s[rs, :], wf) + bf_ref[...]
        sq = pre * pre
        t = jnp.tanh(c0 * pre * (1.0 + 0.044715 * sq))
        hp = 0.5 * pre
        hid = hp + hp * t
        dgel = 0.5 + 0.5 * t + hp * (1.0 - t * t) * (c0 * (1.0 + (3 * 0.044715) * sq))
        hidb = hid.astype(jnp.bfloat16)
        hid_s[rs, :] = hidb
        acc_s[rs, :] += dot_nn(hidb, wp)
        dpb = (dot_nt(dm_s[rs, :], wp) * dgel).astype(jnp.bfloat16)
        dp_s[rs, :] = dpb
        gb = gb + jnp.sum(dpb.astype(jnp.float32), axis=0, keepdims=True)
        dn_s[rs, :] += dot_nt(dpb, wf)
    gb_ref[...] = jnp.broadcast_to(gb, gb_ref.shape)
    gf_s[buf] = dot_nn(nT_s[...], dp_s[...]).astype(jnp.bfloat16)
    gp_s[buf] = dot_tn(hid_s[...], dm_s[...]).astype(jnp.bfloat16)
    block_copies(True)

    @pl.when(f == steps - 1)
    def _():
        gg = jnp.zeros((1, D), jnp.float32)
        gbi, gbo, gbp = gg, gg, gg
        for i in range(nchunk):
            rs = slice(i * chunk, (i + 1) * chunk)
            valid = valid_of(i)
            mid = mid_s[rs, :]
            out_ref[rs, :] = (mid + valid * (acc_s[rs, :] + vec_ref[3:4])).astype(jnp.bfloat16)
            xhat, rstd = norm_parts(mid)
            dn = dn_s[rs, :]
            cot = dm_s[rs, :].astype(jnp.float32)
            dmid = cot + norm_back(dn * vec_ref[0:1], xhat, rstd)
            dmid_ref[rs, :] = dmid
            db = (valid * dmid).astype(jnp.bfloat16)
            gg = gg + jnp.sum(dn * xhat, axis=0, keepdims=True)
            gbi = gbi + jnp.sum(dn, axis=0, keepdims=True)
            gbo = gbo + jnp.sum(db.astype(jnp.float32), axis=0, keepdims=True)
            gbp = gbp + jnp.sum(cot, axis=0, keepdims=True)
            n_s[rs, :] = db
        go_s[...] = dot_tn(c_ref[...], n_s[...]).astype(jnp.bfloat16)
        copies = []
        if cut is None:
            copies.append(pltpu.make_async_copy(go_s, grads[1], go_sem.at[0]))
        else:
            n_rows, n_cols, order2, _ = cut
            rows, cols = D // n_rows, D // n_cols
            at = fb * steps // n_cols
            for fr in range(n_rows):
                for c in range(n_cols):
                    slot = row_slot(fr, order2) + col_slot(c ^ col, order2)
                    src = go_s.at[pl.ds(pl.multiple_of((row ^ fr) * rows, 16), rows), c * cols : (c + 1) * cols]
                    dst = grads[fr & 1].at[slot, :, at : at + cols]
                    copies.append(pltpu.make_async_copy(src, dst, go_sem.at[len(copies)]))
        for copy in copies:
            copy.start()
        for i in range(nchunk):
            rs = slice(i * chunk, (i + 1) * chunk)
            dctx_ref[rs, :] = dot_nt(n_s[rs, :], wo_s[...]).astype(jnp.bfloat16)
        gv_ref[...] = jnp.concatenate([gbo, gg, gbi, gbp, jnp.zeros((4, D), jnp.float32)], axis=0)
        for copy in copies:
            copy.wait()
        for slot in range(min(2, steps)):
            block_copies(False, slot)


def mlp_block(info, context, x, d_out, pieces, loads, vec, b_fc, cut, widths, vmem, fb=768, chunk=256):
    S, D = x.shape
    FF = b_fc.shape[1]
    steps = FF // fb
    bf, f32, sd = jnp.bfloat16, jnp.float32, jax.ShapeDtypeStruct
    hbm = pl.BlockSpec(memory_space=pl.ANY)
    if cut is None:
        grads = [sd((D, FF), bf), sd((D, D), bf), sd((FF, D), bf)]
        n_in, n_out, n_go = len(loads), 2, 1
    else:
        n_rows, n_cols = cut[:2]
        half = n_rows * n_cols // 2
        grads = [sd((half, D // n_rows, sum(widths)), bf)] * 2 + [sd((half, FF // n_rows, D // n_cols), bf)] * 2
        n_in = 3 * n_rows * n_cols
        n_out, n_go = n_rows + fb * n_rows // FF * n_cols, n_rows * n_cols
    if cut is None:
        at = lambda f, info: (0, f)
    else:
        at = lambda f, info: (0, f ^ (info[2] // (n_rows // steps)))
    spec = pltpu.PrefetchScalarGridSpec(
        num_scalar_prefetch=1,
        grid=(steps,),
        in_specs=[whole((S, D))] * 3 + [whole((8, D)), pl.BlockSpec((1, fb), at)] + [hbm] * len(pieces),
        out_specs=[whole((S, D))] * 3 + [whole((8, D)), pl.BlockSpec((8, fb), at)] + [hbm] * len(grads),
        scratch_shapes=[
            pltpu.VMEM((S, D), bf), pltpu.VMEM((D, S), bf), pltpu.VMEM((S, D), bf),
            pltpu.VMEM((S, D), f32), pltpu.VMEM((S, D), f32), pltpu.VMEM((S, D), f32),
            pltpu.VMEM((S, fb), bf), pltpu.VMEM((S, fb), bf),
            pltpu.VMEM((D, FF), bf), pltpu.VMEM((D, D), bf), pltpu.VMEM((FF, D), bf), pltpu.VMEM((D, D), bf),
            pltpu.VMEM((2, D, fb), bf), pltpu.VMEM((2, fb, D), bf),
            pltpu.SemaphoreType.DMA((n_in,)), pltpu.SemaphoreType.DMA((2, n_out)), pltpu.SemaphoreType.DMA((n_go,)),
        ],
    )
    return pl.pallas_call(
        functools.partial(mlp_kernel, steps, chunk, loads, cut),
        grid_spec=spec,
        out_shape=[sd((S, D), bf), sd((S, D), f32), sd((S, D), bf), sd((8, D), f32), sd((8, FF), f32)] + grads,
        compiler_params=pltpu.CompilerParams(vmem_limit_bytes=vmem, dimension_semantics=("arbitrary",)),
        cost_estimate=pl.CostEstimate(
            flops=12 * S * D * FF + 6 * S * D * D, bytes_accessed=8 * D * FF + 20 * S * D, transcendentals=S * FF
        ),
        name="mlp_block",
    )(info, context, x, d_out, vec, b_fc, *pieces)


def wgrad_kernel(cut, count, split, info_ref, nT_ref, bT_ref, *refs):
    n_rows, n_cols = cut
    parts, outs, (g_s, sem) = refs[: 5 * count], refs[5 * count : -2], refs[-2:]
    D = nT_ref.shape[0]
    rows, w = D // n_rows, parts[0].shape[1] // 2
    row, col = info_ref[2], info_ref[3]
    copies = []
    nT, bT = nT_ref[...], bT_ref[...]
    for c in range(n_cols):
        at = 0
        for p in range(count):
            q_ref, k_ref, v_ref, mk_ref, mv_ref = parts[5 * p : 5 * p + 5]
            if c == 0:
                terms = [(nT, q_ref[...]), (nT, k_ref[:, :w]), (bT, mk_ref[...])]
            else:
                terms = [(nT, k_ref[:, w:]), (nT, v_ref[...]), (bT, mv_ref[...])]
            for left, right in terms:
                g_s[c, :, at : at + right.shape[1]] = dot_nn(left, right).astype(jnp.bfloat16)
                at += right.shape[1]
        at = 0
        for i, (width, order) in enumerate(split):
            for fr in range(n_rows):
                slot = row_slot(fr, order) + col_slot(c ^ col, order)
                block = g_s.at[c, pl.ds(pl.multiple_of((row ^ fr) * rows, 16), rows), at : at + width]
                copies.append(pltpu.make_async_copy(block, outs[2 * i + (fr & 1)].at[slot], sem.at[len(copies)]))
                copies[-1].start()
            at += width
    for copy in copies:
        copy.wait()


def weight_grads(info, nT, bT, parts, n_rows, split, vmem):
    D, S = nT.shape
    nb, w, n_cols, count = bT.shape[1], parts[0][0].shape[1] // 2, 2, len(parts)
    rows = D // n_rows
    flat = [d for part in parts for d in part]
    bf, hbm = jnp.bfloat16, pl.BlockSpec(memory_space=pl.ANY)
    outs = []
    for width, _ in split:
        outs += [jax.ShapeDtypeStruct((n_rows * n_cols // 2, rows, width), bf)] * 2
    outs = pl.pallas_call(
        functools.partial(wgrad_kernel, (n_rows, n_cols), count, split),
        grid_spec=pltpu.PrefetchScalarGridSpec(
            num_scalar_prefetch=1,
            grid=(1,),
            in_specs=[whole(a.shape) for a in [nT, bT] + flat],
            out_specs=[hbm] * len(outs),
            scratch_shapes=[
                pltpu.VMEM((n_cols, D, 5 * w * count), bf), pltpu.SemaphoreType.DMA((n_rows * n_cols * len(split),)),
            ],
        ),
        out_shape=outs,
        compiler_params=pltpu.CompilerParams(vmem_limit_bytes=vmem),
        cost_estimate=pl.CostEstimate(
            flops=12 * S * D * w * count, bytes_accessed=14 * S * w * count + 2 * S * D + 20 * D * w * count, transcendentals=0
        ),
        name="weight_grads",
    )(info, nT, bT, *flat)
    return [Scatter(outs[2 * i], outs[2 * i + 1], order) for i, (_, order) in enumerate(split)]


def tokens_kernel(count,w_ref,x_ref,dm_ref,gain_ref,*refs):
    o_ref,gv_ref=refs[-2:]
    i=pl.program_id(0); D=x_ref.shape[1]; width=D//(2*count)
    dn=None
    for kind in range(3):
        for p in range(count):
            at=kind*D+2*p*width
            term=dot_nt(refs[3*p+kind][...],w_ref[:,at:at+2*width])
            dn=term if dn is None else dn+term
    xhat,rstd=norm_parts(x_ref[...].astype(jnp.float32))
    o_ref[...]=dm_ref[...]+norm_back(dn*gain_ref[...],xhat,rstd)
    @pl.when(i==0)
    def _(): gv_ref[...]=jnp.zeros_like(gv_ref)
    gv_ref[0:1]+=jnp.sum(dn*xhat,axis=0,keepdims=True)
    gv_ref[1:2]+=jnp.sum(dn,axis=0,keepdims=True)

def token_grad(parts,w,x,d_middle,gain,vmem,rows=256):
    S,D=x.shape; count=len(parts); width=D//count
    by_row=lambda width: pl.BlockSpec((rows,width),lambda i:(i,0))
    return pl.pallas_call(functools.partial(tokens_kernel,count),grid=(S//rows,),
        in_specs=[whole((D,3*D)),by_row(D),by_row(D),whole((1,D))]+[by_row(width)]*(3*count),
        out_specs=[by_row(D),pl.BlockSpec((8,D),lambda i:(0,0))],
        out_shape=[jax.ShapeDtypeStruct((S,D),jnp.float32),jax.ShapeDtypeStruct((8,D),jnp.float32)],
        compiler_params=pltpu.CompilerParams(vmem_limit_bytes=vmem),
        cost_estimate=pl.CostEstimate(flops=6*S*D*D,bytes_accessed=16*S*D+6*D*D,transcendentals=0),name="token_grad")(w,x,d_middle,gain,*[d for part in parts for d in part])


VMEM_BYTES = 58 << 20
MLP_VMEM_BYTES = 50 << 20
FIT_NODE_COUNT = 512
ridge = 0.5


def fit_constant(nb):
    centers = (np.arange(nb, dtype=np.float64) + 0.5) / nb
    times = (np.arange(FIT_NODE_COUNT, dtype=np.float64) + 0.5) / FIT_NODE_COUNT
    design = np.exp(-0.5 * (times[None, :] - centers[:, None]) ** 2 * (nb * nb))
    table = np.linalg.solve(design @ design.T + ridge * np.eye(nb), design).astype(np.float32)
    hi = table.astype(jnp.bfloat16)
    lo = (table - hi.astype(np.float32)).astype(jnp.bfloat16)
    return np.concatenate([hi, lo], axis=0)


def bits_of(n):
    count = n.bit_length() - 1
    assert 1 << count == n
    return count


def swap(block, stage):
    axis, bit = stage
    n = lax.axis_size(axis)
    return lax.ppermute(block, axis, [(i, i ^ (1 << bit)) for i in range(n)])


class Chain:
    def __init__(self):
        self.last = ()

    def wait(self, *values):
        got = lax.optimization_barrier(values + self.last)
        self.last = got[:1]
        return got[0] if len(values) == 1 else got[: len(values)]


def stage_lists():
    rows = bits_of(lax.axis_size("row"))
    cols = bits_of(lax.axis_size("col"))
    far = [("row", b) for b in range(rows - 1, 1, -1)]
    col = [("col", b) for b in range(cols - 1, -1, -1)]
    near = [("row", 1)] if rows > 1 else []
    return far, col, near, [("row", 0)]


def slot_offsets(order):
    table = []
    for slot in range(1 << len(order)):
        flips = {"row": 0, "col": 0}
        for i, (axis, bit) in enumerate(order):
            if slot >> i & 1:
                flips[axis] ^= 1 << bit
        table.append((flips["row"], flips["col"]))
    return table


def place_bits():
    rows, cols = bits_of(lax.axis_size("row")), bits_of(lax.axis_size("col"))
    return [("row", b) for b in range(rows - 1, -1, -1)] + [("col", b) for b in range(cols - 1, -1, -1)]


def by_place(slots, order):
    seen = order[::-1]
    dims = [seen.index(p) for p in place_bits()]
    split = slots.reshape((2,) * len(order) + slots.shape[1:])
    tail = range(len(order), split.ndim)
    return split.transpose(dims + list(tail)).reshape(slots.shape)


def by_slot(blocks, order):
    places = place_bits()
    dims = [places.index(p) for p in order[::-1]]
    split = blocks.reshape((2,) * len(order) + blocks.shape[1:])
    tail = range(len(order), split.ndim)
    return split.transpose(dims + list(tail)).reshape(blocks.shape)


def flipped(blocks, row, col):
    places = place_bits()
    split = blocks.reshape((2,) * len(places) + blocks.shape[1:])
    for dim, (axis, bit) in enumerate(places):
        mine = (row if axis == "row" else col) >> bit & 1
        split = jnp.where(mine == 1, jnp.flip(split, dim), split)
    return split.reshape(blocks.shape)


class Gather:
    def __init__(self, block, order, done=0):
        self.held, self.order, self.done = (block if done else block[None]), order, done

    def send(self):
        self.came = swap(self.held, self.order[self.done])
        return self

    def take(self, came):
        self.done += 1
        if self.done == len(self.order):
            self.came = came
        else:
            self.held = jnp.concatenate([self.held, came], axis=0)
        return self

    def halves(self, cut, orders):
        return [
            Gather(self.held[:, :, :cut], orders[0], self.done),
            Gather(self.held[:, :, cut:], orders[1], self.done),
        ]


def advance(chain, *gathers):
    got = chain.wait(*[g.came for g in gathers])
    got = got if len(gathers) > 1 else (got,)
    for g, came in zip(gathers, got):
        g.take(came)
        if g.done < len(g.order):
            g.send()


def copy_kernel(plans, place_ref, *refs):
    sem = refs[-1]
    copies = []
    for src, dst, fr, fc, rows, cols, slot, at, column, width, outward in plans:
        r = place_ref[0] ^ fr
        c = place_ref[1] ^ fc
        matrix, slots = (refs[dst], refs[src]) if outward else (refs[src], refs[dst])
        block = matrix.at[
            pl.ds(pl.multiple_of(r * rows, 8), rows), pl.ds(pl.multiple_of(c * cols + column, 128), width)
        ]
        piece = slots.at[slot, :, pl.ds(at, width)]
        pair = (piece, block) if outward else (block, piece)
        copies.append(pltpu.make_async_copy(*pair, sem.at[len(copies)]))
    for copy in copies:
        copy.start()
    for copy in copies:
        copy.wait()


def copy_call(plans, place, ins, out_shapes, resident, name):
    hbm = pl.BlockSpec(memory_space=pl.ANY)
    size = sum(math.prod(o.shape) for o in out_shapes)
    return pl.pallas_call(
        functools.partial(copy_kernel, plans),
        grid_spec=pltpu.PrefetchScalarGridSpec(
            num_scalar_prefetch=1,
            grid=(1,),
            in_specs=[hbm] * len(ins),
            out_specs=[whole(o.shape) if resident else hbm for o in out_shapes],
            scratch_shapes=[pltpu.SemaphoreType.DMA((len(plans),))],
        ),
        out_shape=out_shapes,
        compiler_params=pltpu.CompilerParams(vmem_limit_bytes=24 << 20),
        cost_estimate=pl.CostEstimate(flops=0, bytes_accessed=4 * size, transcendentals=0),
        name=name,
    )(place, *ins)


def ranges_of(layout, offset, width):
    found, at = [], 0
    for i, size in enumerate(layout):
        low, high = max(at, offset), min(at + size, offset + width)
        if low < high:
            found.append((i, low - offset, low - at, high - low))
        at += size
    return found


def assemble(place, gathers, layout, n_rows, n_cols):
    rows = gathers[0].held.shape[1]
    shapes = [jax.ShapeDtypeStruct((rows * n_rows, w * n_cols), jnp.bfloat16) for w in layout]
    pieces, plans, offset = [], [], 0
    aligned = rows % 8 == 0 and all(w % 128 == 0 for w in layout)
    if not aligned:
        full = []
        for g in gathers:
            slots = jnp.concatenate([g.held, g.came], axis=0)
            full.append(flipped(by_place(slots, g.order), place[0], place[1]))
        full = jnp.concatenate(full, axis=2)
        res, at = [], 0
        for w in layout:
            block = full[:, :, at : at + w].reshape(n_rows, n_cols, rows, w)
            res.append(block.transpose(0, 2, 1, 3).reshape(rows * n_rows, w * n_cols))
            at += w
        return res
    for g in gathers:
        table = slot_offsets(g.order)
        width = g.held.shape[2]
        for slot, (fr, fc) in enumerate(table):
            src = len(pieces) + slot // (len(table) // 2)
            for i, at, column, w in ranges_of(layout, offset, width):
                plans.append((src, i, fr, fc, rows, layout[i], slot % (len(table) // 2), at, column, w, True))
        pieces += [g.held, g.came]
        offset += width
    plans = [(p[0], len(pieces) + p[1]) + p[2:] for p in plans]
    return copy_call(plans, place, pieces, shapes, True, "assemble")


class Scatter:
    def __init__(self, keep, send, order):
        self.order, self.left = order, len(order)
        self.terms, self.out = [keep], send
        self.total = None

    def send(self):
        self.left -= 1
        self.came = swap(self.out, self.order[self.left])
        return self

    def take(self, came):
        self.terms.append(came)
        if self.left == 0:
            self.total = sum(t.astype(jnp.float32) for t in self.terms)[0]
            return self
        half = self.terms[0].shape[0] // 2
        self.out = sum(t[half:].astype(jnp.float32) for t in self.terms).astype(jnp.bfloat16)
        self.terms = [t[:half] for t in self.terms]
        return self


def onward(chain, *scatters):
    got = chain.wait(*[s.came for s in scatters])
    got = got if len(scatters) > 1 else (got,)
    for s, came in zip(scatters, got):
        s.take(came)
        if s.left:
            s.send()


def disperse(place, grads, cuts, n_rows, n_cols):
    rows = grads[0].shape[0] // n_rows
    blocks = [g.reshape(n_rows, rows, n_cols, -1).transpose(0, 2, 1, 3) for g in grads]
    joined = jnp.concatenate(blocks, axis=3).reshape(n_rows * n_cols, rows, -1)
    joined = flipped(joined, place[0], place[1])
    res, offset = [], 0
    for width, order in cuts:
        slots = by_slot(joined[:, :, offset : offset + width], order)
        res.append(Scatter(slots[: len(slots) // 2], slots[len(slots) // 2 :], order))
        offset += width
    return res


def shards(
    tokens, w_qkv, w_out, w_mem, w_fc, w_proj, gain_attn, bias_attn, gain_mlp, bias_mlp, b_out, b_fc, b_proj,
    w_loc, w_spread, past_states, sticky_pos, seq_lengths, d_out,
):
    bf, f32 = jnp.bfloat16, jnp.float32
    n_rows, n_cols = lax.axis_size("row"), lax.axis_size("col")
    row, col = lax.axis_index("row"), lax.axis_index("col")
    place = jnp.stack([row, col]).astype(jnp.int32)
    batches, _, span, feat = tokens.shape
    heads, nb = w_loc.shape[0], w_loc.shape[1] * n_rows * n_cols
    hidden = w_fc.shape[1] * n_cols
    assert batches == 2 and n_cols % 2 == 0
    side = col % 2
    own, other = side, 1 - side
    first = (col - side) * span
    far, along, near, core = stage_lists()
    zyx, zxy, yzx = far + along + near + core, far + near + along + core, along + far + near + core
    devices = n_rows * n_cols

    def pick(a, i):
        return lax.dynamic_index_in_dim(a, i, 0, keepdims=False)

    def to_chunk(mine, came):
        two = jnp.stack([mine, came])
        return jnp.where(side == 0, two, two[::-1]).reshape((2 * span,) + mine.shape[1:])

    def trade(a):
        return swap(a, ("col", 0))

    tokens, past, d_out = tokens[:, 0], past_states[:, 0], d_out[:, 0]
    sticky, lengths = sticky_pos[:, 0], seq_lengths[:, 0]
    length = pick(lengths, own)
    info = jnp.stack([length, first, row, col]).astype(jnp.int32)

    singles = [gain_attn, bias_attn, gain_mlp, bias_mlp, b_out, b_proj, b_fc]
    n_single, n_small = len(singles), len(singles) + heads
    rows_small = -(-n_small // 8) * 8
    both_w = jnp.concatenate([w_loc, w_spread], axis=1)

    def wide(v):
        v = v.reshape(-1, v.shape[-1])
        return jnp.pad(v, ((0, 0), (0, 128 - v.shape[1])))

    layout1 = [w_qkv.shape[1], w_mem.shape[1]]
    layout2 = [w_fc.shape[1], w_out.shape[1]]
    layout3 = [w_proj.shape[1]]
    width1 = sum(layout1)
    cut1 = (width1 // 128 + 1) // 2 * 128
    rows1 = w_qkv.shape[0]
    fb = 768
    direct = n_cols == 2 and all(w % 128 == 0 for w in layout1 + layout2 + layout3) and rows1 % 16 == 0
    steps = hidden // fb
    direct = direct and layout2[0] % fb == 0 and fb % w_proj.shape[0] == 0 and steps & (steps - 1) == 0

    def loads_of(gathers, layout, base, first):
        loads, pieces, offset = [], [], 0
        for g in gathers:
            table = slot_offsets(g.order)
            half, width = len(table) // 2, g.held.shape[2]
            for slot, (fr, fc) in enumerate(table):
                for i, at, column, w in ranges_of(layout, offset, width):
                    src = first + len(pieces) + slot // half
                    loads.append((src, base + i, fr, fc, g.held.shape[1], layout[i], slot % half, at, column, w))
            pieces += [g.held, g.came]
            offset += width
        return loads, pieces

    chain = Chain()
    g1 = Gather(jnp.concatenate([w_qkv, w_mem], axis=1), zyx).send()
    tokens_out, block2 = chain.wait(tokens, jnp.concatenate([w_fc, w_out], axis=1))
    came_tokens = trade(pick(tokens_out, other))
    g2 = Gather(block2, yzx).send()
    g3 = Gather(w_proj, zxy)
    flat = jnp.concatenate([wide(v) for v in singles + [both_w]])
    flat = jnp.pad(flat, ((0, rows_small - n_small), (0, 0)))
    g0 = None
    for _ in far[1:]:
        advance(chain, g1)
        if g0 is None:
            g0 = Gather(chain.wait(flat), zyx).send()
    g1.take(chain.wait(g1.came))
    g1a, g1b = g1.halves(cut1, (zyx, zxy))
    g1a.send()
    g1b.send()
    advance(chain, g0)
    g3.held = chain.wait(g3.held)
    g3.send()
    for _ in far[1:]:
        advance(chain, g3)
    for _ in along:
        advance(chain, g2)
    advance(chain, g0)
    advance(chain, g1b, g1a)

    fit = jnp.asarray(fit_constant(nb))
    here = col * span
    past, sticky = chain.wait(past, sticky)

    def basis_part(i):
        spots = pick(sticky, i) - here
        resident = (spots >= 0) & (spots < span)
        picked = jnp.take(past.reshape(-1, feat), jnp.clip(spots, 0, span - 1) + i * span, axis=0)
        parts = jnp.dot(fit * resident.astype(bf)[None, :], picked, preferred_element_type=f32)
        return parts[:nb] + parts[nb:]

    came_g3 = chain.wait(g3.came)
    if n_cols == 2:
        own_basis, basis_out = chain.wait(basis_part(own), basis_part(other).astype(bf))
    else:
        both = lax.psum(jnp.stack([basis_part(i).astype(bf) for i in range(2)]), "col")
        own_basis, came_basis = pick(both, own).astype(f32), jnp.zeros((nb, feat), bf)
    advance(chain, g0)
    for _ in far[1:]:
        advance(chain, g2)
    x = to_chunk(pick(tokens, own), chain.wait(came_tokens))
    while g1b.done < len(g1b.order) - 1:
        advance(chain, g1b, g1a)
    if n_cols == 2:
        came_basis = trade(chain.wait(basis_out))
    g3.take(chain.wait(came_g3)).send()
    came_out = trade(chain.wait(pick(d_out, other)))
    while g0.done < len(g0.order) - 1:
        advance(chain, g0)
    g0.came = chain.wait(g0.came)
    every = flipped(by_place(jnp.concatenate([g0.held, g0.came], axis=0), zyx), row, col)
    share, width = w_loc.shape[1], gain_attn.shape[0]

    def rows_of(first, count):
        return every[:, first : first + count, :width].transpose(1, 0, 2).reshape(count, feat).astype(f32)

    vec1 = jnp.pad(rows_of(0, 2), ((0, 6), (0, 0)))
    advance(chain, g2)
    x, vec1 = chain.wait(x, vec1)
    g1b.came, g1a.came, came_basis = chain.wait(g1b.came, g1a.came, came_basis)

    if direct:
        loads, pieces = loads_of([g1a, g1b], layout1, 0, 0)
    else:
        pieces = assemble(place, [g1a, g1b], layout1, n_rows, n_cols)
        loads = [(i, i) + (None,) * 8 for i in range(2)]
    nT, qkv, mem_kv, basisT, wq = project_qkv(info, x, vec1, own_basis, came_basis, pieces, loads, heads // 2, VMEM_BYTES)
    qkv, every = chain.wait(qkv, every)
    vec2 = jnp.pad(rows_of(2, 4), ((0, 4), (0, 0)))
    bfc = every[:, n_single - 1, : b_fc.shape[0]].astype(f32).reshape(1, -1)
    loc, spr = [
        every[:, n_single:n_small, at : at + share].transpose(1, 0, 2).reshape(heads // 2, 2, nb) for at in (0, share)
    ]
    wls = jnp.concatenate([loc, spr, jnp.zeros((heads // 2, 4, nb), bf)], axis=1)
    for _ in along[:1]:
        advance(chain, g3)
    g_other = chain.wait(came_out)
    halo = 0 if n_cols == 2 else WINDOW
    pairs = heads // 2
    route = [(i, i + 2) for i in range(n_cols - 2)]
    back = [(i + 2, i) for i in range(n_cols - 2)]
    if halo:
        before = lax.ppermute(qkv[-halo:, feat:], "col", route)
        kvx = jnp.concatenate([before, qkv[:, feat:]], axis=0)
        kv = (kvx, 0, kvx, pairs)
    else:
        kv = (qkv, pairs, qkv, 2 * pairs)
    mem_kv, g2.held, g3.held = chain.wait(mem_kv, g2.held, g3.held)
    context, lse = attention_forward(info, qkv, kv, halo, mem_kv, wls, heads, VMEM_BYTES)
    context = chain.wait(context)
    while g3.done < len(g3.order) - 1:
        advance(chain, g3)
    while g2.done < len(g2.order) - 1:
        advance(chain, g2)
    g_chunk = to_chunk(pick(d_out, own), g_other)
    g3.came, g2.came = chain.wait(g3.came, g2.came)

    if direct:
        loads, pieces = loads_of([g2], layout2, 0, 0)
        loads3, pieces3 = loads_of([g3], layout3, 2, len(pieces))
        loads = loads + loads3
        pieces = [pltpu.with_memory_space_constraint(piece, pltpu.VMEM) for piece in pieces + pieces3]
    else:
        wf, wo = assemble(place, [g2], layout2, n_rows, n_cols)
        wp = assemble(place, [g3], layout3, n_rows, n_cols)[0]
        pieces = [wf, wo, wp]
        loads = [(i, i) + (None,) * 8 for i in range(3)]
    output, d_middle, d_context, g_vec, g_bfc, *cut_grads = mlp_block(
        info, context, x, g_chunk, pieces, loads, vec2, bfc,
        (n_rows, n_cols, yzx, zxy) if direct else None, layout2, MLP_VMEM_BYTES, fb,
    )

    def from_chunk(chunk):
        halves = chunk.reshape(2, span, feat)
        return pick(halves, own), pick(halves, other)

    def paired(kept, came):
        two = jnp.stack([kept, came])
        return jnp.where(side == 0, two, two[::-1])[:, None]

    if direct:
        s2, s3 = Scatter(*cut_grads[:2], yzx), Scatter(*cut_grads[2:], zxy)
    else:
        s2 = disperse(place, cut_grads[:2], [(sum(layout2), yzx)], n_rows, n_cols)[0]
        s3 = disperse(place, cut_grads[2:], [(sum(layout3), zxy)], n_rows, n_cols)[0]
    s2.send()
    s3.send()
    d_context, s2.terms[0], s3.terms[0] = chain.wait(d_context, s2.terms[0], s3.terms[0])

    def taken(*scatters):
        got = chain.wait(*[s.came for s in scatters])
        for s, came in zip(scatters, got if len(scatters) > 1 else (got,)):
            s.take(came)
        outs = chain.wait(*[s.out for s in scatters])
        for s, out in zip(scatters, outs if len(scatters) > 1 else (outs,)):
            s.out = out
            s.send()

    count = pairs // 2
    mixed, parts = [], []
    kept_out, sent = from_chunk(output)
    d_context, sent = chain.wait(d_context, sent)
    came_output = trade(sent)
    for i in range(count):
        d_context = chain.wait(d_context)
        got = list(
            attention_backward(info, qkv, kv, halo, mem_kv, wls, lse, d_context, heads, VMEM_BYTES, i, 2, count)
        )
        got[0] = chain.wait(got[0])
        mixed.append(got)
        d_q, d_k, d_v, d_mk, d_mv, _ = got
        if halo:
            d_kv = jnp.concatenate([d_k, d_v], axis=1)
            ret = lax.ppermute(d_kv[:halo], "col", back)
            d_kv = d_kv[halo:].astype(f32) + jnp.pad(ret.astype(f32), ((2 * span - halo, 0), (0, 0)))
            d_kv = d_kv.astype(bf)
            d_k, d_v = jnp.split(d_kv, 2, axis=1)
        parts.append((d_q, d_k, d_v, d_mk, d_mv))
        if i == 0:
            came_output = chain.wait(came_output)
            taken(s2, s3)
        if i == count - 2 and direct:
            s1 = weight_grads(info, nT, basisT, parts, n_rows, [(len(parts) * 5 * (feat // pairs), zxy)], VMEM_BYTES)
            s1[0].send()
            s1[0].terms[0] = chain.wait(s1[0].terms[0])
    taken(s3)
    taken(s2)
    if direct:
        taken(s1[0])
    d_middle = chain.wait(d_middle)
    d_tok, g_vec1 = token_grad([p[:3] for p in parts], wq, x, d_middle, vec1[0:1], VMEM_BYTES)
    d_tok, g_vec1 = chain.wait(d_tok, g_vec1)
    taken(s3)
    taken(s2)
    kept_x, sent_x = from_chunk(d_tok)
    came_x = trade(chain.wait(sent_x.astype(bf)))
    nT = chain.wait(nT)
    if direct:
        s1 += weight_grads(info, nT, basisT, parts[-1:], n_rows, [(5 * (feat // pairs), zyx)], VMEM_BYTES)
        s1[1].send()
    else:
        ordered = [jnp.stack([p[k].reshape(p[k].shape[0], 2, -1) for p in parts], axis=2) for k in range(5)]
        ordered = [a.reshape(a.shape[0], feat) for a in ordered]
        g_qkv = jnp.dot(nT, jnp.concatenate(ordered[:3], axis=1), preferred_element_type=f32).astype(bf)
        g_mem = jnp.dot(basisT, jnp.concatenate(ordered[3:], axis=1), preferred_element_type=f32).astype(bf)
        s1 = disperse(place, [g_qkv, g_mem], [(cut1, zyx), (width1 - cut1, zxy)], n_rows, n_cols)
        for s_ in s1:
            s_.send()
    s1[-1].terms[0] = chain.wait(s1[-1].terms[0])
    by_pair = [m[5][j] for j in range(2) for m in mixed]
    total = jnp.concatenate([g_vec, g_vec1, g_bfc] + by_pair, axis=1)
    stages = core + far + along + near
    came = swap(total.astype(bf), stages.pop(0))
    last, early = s1[-1], s1[0]
    everyone = [last, early, s3, s2]
    plan = [last, early, None, last, last, early, s3, None, came_x, last, early, s2, None, early, s3, None, last, s2, None]
    while any(s_.total is None for s_ in everyone) or came is not None:
        s_ = plan.pop(0) if plan else next((s_ for s_ in everyone if s_.total is None), None)
        if s_ is came_x:
            came_x = chain.wait(came_x)
        elif s_ is None:
            if came is not None:
                total = total + chain.wait(came).astype(f32)
                came = swap(total.astype(bf), stages.pop(0)) if stages else None
        elif s_.left:
            onward(chain, s_)
        elif s_.total is None:
            s_.take(chain.wait(s_.came))
    index = row * n_cols + col

    def mine(block, first, width):
        return lax.dynamic_slice_in_dim(block, first + index * width, width, axis=1)

    g_bo, g_gain2, g_bias2, g_bp = mine(total, 0, gain_mlp.shape[0])[:4]
    g_gain1, g_bias1 = mine(total, feat, gain_attn.shape[0])[:2]
    g_bf = mine(total, 2 * feat, b_fc.shape[0])[0]
    per_pair = total[:, 2 * feat + hidden :].reshape(8, pairs, nb).transpose(1, 0, 2)
    g_loc = lax.dynamic_slice_in_dim(per_pair[:, 0:2].reshape(heads, nb), index * share, share, axis=1)
    g_spread = lax.dynamic_slice_in_dim(per_pair[:, 2:4].reshape(heads, nb), index * share, share, axis=1)
    outputs = paired(kept_out, came_output)
    grad_x = paired(kept_x, came_x.astype(f32))
    joined = jnp.concatenate([s_.total for s_ in s1], axis=1)
    if direct:
        w = feat // pairs
        n_qkv = layout1[0] // (count * w)
        blocks = joined.reshape(rows1, count, 5, w)
        grad_qkv = blocks[:, :, :n_qkv].transpose(0, 2, 1, 3).reshape(rows1, layout1[0])
        grad_mem = blocks[:, :, n_qkv:].transpose(0, 2, 1, 3).reshape(rows1, layout1[1])
    else:
        grad_qkv, grad_mem = joined[:, : layout1[0]], joined[:, layout1[0] :]
    grad_fc, grad_out = s2.total[:, : layout2[0]], s2.total[:, layout2[0] :]
    grad_proj = s3.total
    return (
        outputs, grad_x, grad_qkv, grad_out, grad_mem, grad_fc, grad_proj,
        g_gain1, g_bias1, g_gain2, g_bias2, g_bo, g_bf, g_bp, g_loc, g_spread,
    )


def solution(mesh):
    grid, both, tail = P("row", "col"), P(("row", "col")), P(None, ("row", "col"))
    act, rows = P(None, "row", "col", None), P(None, "row")
    return jax.shard_map(
        shards,
        mesh=mesh,
        in_specs=(act,) + (grid,) * 5 + (both,) * 7 + (tail,) * 2 + (act, P(None, "row", None), rows, act),
        out_specs=(act, act) + (grid,) * 5 + (both,) * 7 + (tail,) * 2,
        check_vma=False,
    )
```

```python
import functools
import math

import jax
import jax.numpy as jnp
import numpy as np
from jax import lax
from jax.experimental import pallas as pl
from jax.experimental.pallas import tpu as pltpu
from jax.sharding import PartitionSpec as P

WINDOW=512; TILE=256; masked=-1e30
var_scale=0.01
NT=(((1,),(1,)),((),()))
NN=(((1,),(0,)),((),()))

def dot_nt(a,b): return lax.dot_general(a,b,NT,preferred_element_type=jnp.float32)
def dot_nn(a,b): return lax.dot_general(a,b,NN,preferred_element_type=jnp.float32)

def split3(v):
    hi=v.astype(jnp.bfloat16); r=v-hi.astype(jnp.float32)
    mid=r.astype(jnp.bfloat16); lo=(r-mid.astype(jnp.float32)).astype(jnp.bfloat16)
    return hi,mid,lo

def lane_is_first(shape,half):
    return lax.broadcasted_iota(jnp.int32,shape,1)<half

def tile_biases(info_ref,first_key,has_far,has_mid):
    key=lax.broadcasted_iota(jnp.int32,(TILE,TILE),0)
    qry=lax.broadcasted_iota(jnp.int32,(TILE,TILE),1)
    tri=key<=qry
    length=info_ref[0]
    diag_pos=first_key+key
    far_pos=diag_pos-WINDOW
    near=jnp.where((diag_pos<length)|(key==qry),0.0,masked)
    far=jnp.where((far_pos>=0)&(far_pos<length),0.0,masked) if has_far else masked
    comb=jnp.where(tri,near,far)
    mid_pos=diag_pos-TILE
    mid=jnp.where((mid_pos>=0)&(mid_pos<length),0.0,masked)
    return comb,mid

def density_rows(wls,mk,half):
    vec=dot_nn(wls,mk)
    row=lax.broadcasted_iota(jnp.int32,vec.shape,0)
    lane=lax.broadcasted_iota(jnp.int32,vec.shape,1)
    return jnp.where((row%2==0)==(lane<half),vec,0.0)

def logits_of(vec,qb):
    hi,mid,lo=split3(vec)
    parts=dot_nt(jnp.concatenate([hi,mid,lo,lo],axis=0),qb)
    return (parts[16:24]+parts[8:16])+parts[0:8]

def spreads(logits,nb):
    location=1.0/(1.0+jnp.exp(-logits))
    soft=jnp.maximum(logits,0.0)+jnp.log1p(jnp.exp(-jnp.abs(logits)))
    spread=var_scale*soft+1.0/(nb*nb)
    return location,spread

def fwd_kernel(halo,half,info_ref,q_ref,k_ref,v_ref,mk_ref,mv_ref,wls_ref,ctx_ref,lse_ref,bias_ref):
    S=q_ref.shape[0]; nblk=S//TILE; nb=mk_ref.shape[0]; ht=halo//TILE
    @pl.when(pl.program_id(0)==0)
    def _():
        for i in range(nblk):
            comb,mid=tile_biases(info_ref,info_ref[1]+i*TILE,ht+i>=2,ht+i>=1)
            bias_ref[2*i]=comb; bias_ref[2*i+1]=mid
    tri=lax.broadcasted_iota(jnp.int32,(TILE,TILE),0)<=lax.broadcasted_iota(jnp.int32,(TILE,TILE),1)
    trib=jnp.where(tri,1.0,0.0).astype(jnp.bfloat16)
    lane=lax.broadcasted_iota(jnp.int32,(16,2*half),1)
    sides=[jnp.where(lane<half,1.0,0.0)[0:1].astype(jnp.bfloat16),jnp.where(lane<half,0.0,1.0)[0:1].astype(jnp.bfloat16)]
    centers=(lax.broadcasted_iota(jnp.int32,(nb,TILE),0).astype(jnp.float32)+0.5)/nb
    vec=density_rows(wls_ref[0],mk_ref[...],half)
    vT=v_ref[...].T
    mvT=mv_ref[...].T
    lse_ref[...]=jnp.zeros_like(lse_ref)
    for i in range(nblk):
        rows=slice(i*TILE,(i+1)*TILE)
        qb=q_ref[rows,:]*jnp.bfloat16(half**-0.5)
        d0=halo+i*TILE
        has_mid=ht+i>=1; has_far=ht+i>=2
        kd=k_ref[d0:d0+TILE,:]
        logits=logits_of(vec,qb)
        location,spread=spreads(logits,nb)
        nis=-0.5/spread
        norm=lax.rsqrt(2.0*math.pi*spread)*(1.0/nb)
        outs=[]
        for x in range(2):
            qx=qb*sides[x]
            vx=vT[x*half:(x+1)*half,:]
            sd=dot_nt(kd,qx)
            if has_far:
                sf=dot_nt(k_ref[d0-2*TILE:d0-TILE,:],qx)
                sc=jnp.where(tri,sd,sf)+bias_ref[2*i]
            else:
                sc=sd+bias_ref[2*i]
            top=jnp.max(sc,axis=0,keepdims=True)
            if has_mid:
                sm=dot_nt(k_ref[d0-TILE:d0,:],qx)+bias_ref[2*i+1]
                top=jnp.maximum(top,jnp.max(sm,axis=0,keepdims=True))
            ec=jnp.exp(sc-top)
            tot=jnp.sum(ec,axis=0,keepdims=True)
            ecl=ec.astype(jnp.bfloat16)
            if has_far:
                near=ecl*trib
                o=dot_nn(vx[:,d0:d0+TILE],near)+dot_nn(vx[:,d0-2*TILE:d0-TILE],ecl-near)
            else:
                o=dot_nn(vx[:,d0:d0+TILE],ecl)
            if has_mid:
                em=jnp.exp(sm-top)
                tot=tot+jnp.sum(em,axis=0,keepdims=True)
                o=o+dot_nn(vx[:,d0-TILE:d0],em.astype(jnp.bfloat16))
            lse_ref[0,x:x+1,rows]=top+jnp.log(tot)
            o=o*(1.0/tot)
            z=location[x:x+1]-centers
            e=jnp.exp(nis[2+x:3+x]*(z*z))
            r=dot_nn(mvT[x*half:(x+1)*half,:],e.astype(jnp.bfloat16))*norm[2+x:3+x]
            outs.append(o+r)
        ctx_ref[rows,:]=jnp.concatenate(outs,axis=0).T.astype(jnp.bfloat16)

def bwd_kernel(halo,half,info_ref,q_ref,k_ref,v_ref,mk_ref,mv_ref,wls_ref,lse_ref,do_ref,
               dq_ref,dk_ref,dv_ref,dmk_ref,dmv_ref,gls_ref,bias_ref,dk_acc,dv_acc):
    S=q_ref.shape[0]; nblk=S//TILE; nb=mk_ref.shape[0]; ht=halo//TILE
    @pl.when(pl.program_id(0)==0)
    def _():
        for i in range(nblk):
            comb,mid=tile_biases(info_ref,info_ref[1]+i*TILE,ht+i>=2,ht+i>=1)
            bias_ref[2*i]=comb; bias_ref[2*i+1]=mid
    tri=lax.broadcasted_iota(jnp.int32,(TILE,TILE),0)<=lax.broadcasted_iota(jnp.int32,(TILE,TILE),1)
    trib=jnp.where(tri,1.0,0.0).astype(jnp.bfloat16)
    lane=lax.broadcasted_iota(jnp.int32,(16,2*half),1)
    sides=[jnp.where(lane<half,1.0,0.0)[0:1].astype(jnp.bfloat16),jnp.where(lane<half,0.0,1.0)[0:1].astype(jnp.bfloat16)]
    centers=(lax.broadcasted_iota(jnp.int32,(nb,TILE),0).astype(jnp.float32)+0.5)/nb
    mk=mk_ref[...]; mv=mv_ref[...]
    vec=density_rows(wls_ref[0],mk,half)
    vecT=vec.T
    kT=k_ref[...].T
    dk_acc[...]=jnp.zeros_like(dk_acc); dv_acc[...]=jnp.zeros_like(dv_acc)
    dmv=jnp.zeros((nb,2*half),jnp.float32)
    dvec=jnp.zeros((8,2*half),jnp.float32)
    for i in range(nblk):
        rows=slice(i*TILE,(i+1)*TILE)
        qb=q_ref[rows,:]*jnp.bfloat16(half**-0.5)
        dob=do_ref[rows,:]
        d0=halo+i*TILE
        has_mid=ht+i>=1; has_far=ht+i>=2
        dg=slice(d0,d0+TILE); md=slice(d0-TILE,d0); fr=slice(d0-2*TILE,d0-TILE)
        logits=logits_of(vec,qb)
        location,spread=spreads(logits,nb)
        inv=1.0/spread
        nis=-0.5*inv
        norm=lax.rsqrt(2.0*math.pi*spread)*(1.0/nb)
        outs=[]; s0s=[]; s1s=[]; s2s=[]
        for x in range(2):
            qx=qb*sides[x]
            dox=dob*sides[x]
            kx=kT[x*half:(x+1)*half,:]
            lse=lse_ref[0,x:x+1,rows]
            sc=dot_nt(k_ref[dg,:],qx)
            dpc=dot_nt(v_ref[dg,:],dox)
            if has_far:
                sc=jnp.where(tri,sc,dot_nt(k_ref[fr,:],qx))
                dpc=jnp.where(tri,dpc,dot_nt(v_ref[fr,:],dox))
            pc=jnp.exp(sc+bias_ref[2*i]-lse)
            delta=jnp.sum(pc*dpc,axis=0,keepdims=True)
            if has_mid:
                sm=dot_nt(k_ref[md,:],qx)
                dpm=dot_nt(v_ref[md,:],dox)
                pm=jnp.exp(sm+bias_ref[2*i+1]-lse)
                delta=delta+jnp.sum(pm*dpm,axis=0,keepdims=True)
                dsm=(pm*(dpm-delta)).astype(jnp.bfloat16)
                dv_acc[md,:]+=dot_nn(pm.astype(jnp.bfloat16),dox)
                dk_acc[md,:]+=dot_nn(dsm,qx)
            dsc=(pc*(dpc-delta)).astype(jnp.bfloat16)
            pcl=pc.astype(jnp.bfloat16)
            if has_far:
                dsd=dsc*trib; dsf=dsc-dsd
                near=pcl*trib
                dv_acc[dg,:]+=dot_nn(near,dox)
                dv_acc[fr,:]+=dot_nn(pcl-near,dox)
                dk_acc[dg,:]+=dot_nn(dsd,qx)
                dk_acc[fr,:]+=dot_nn(dsf,qx)
                dq=dot_nn(kx[:,dg],dsd)+dot_nn(kx[:,fr],dsf)
            else:
                dv_acc[dg,:]+=dot_nn(pcl,dox)
                dk_acc[dg,:]+=dot_nn(dsc,qx)
                dq=dot_nn(kx[:,dg],dsc)
            if has_mid:
                dq=dq+dot_nn(kx[:,md],dsm)
            outs.append(dq)
            z=location[x:x+1]-centers
            e=jnp.exp(nis[2+x:3+x]*(z*z))
            g=dot_nt(mv,dox)*e
            gz=g*z
            s0s.append(jnp.sum(g,axis=0,keepdims=True))
            s1s.append(jnp.sum(gz,axis=0,keepdims=True))
            s2s.append(jnp.sum(gz*z,axis=0,keepdims=True))
            dmv=dmv+dot_nn((e*norm[2+x:3+x]).astype(jnp.bfloat16),dox)
        n2=norm[2:4]; i2=inv[2:4]
        s0=jnp.concatenate(s0s,axis=0); s1=jnp.concatenate(s1s,axis=0); s2=jnp.concatenate(s2s,axis=0)
        dloc=-(n2*i2)*s1
        dspr=n2*(0.5*i2)*(s2*i2-s0)
        l2=location[0:2]
        dll=dloc*l2*(1.0-l2)
        dsl=dspr*var_scale*location[2:4]
        dl=jnp.concatenate([dll,dsl,jnp.zeros((4,TILE),jnp.float32)],axis=0)
        hi=dl.astype(jnp.bfloat16); lo=(dl-hi.astype(jnp.float32)).astype(jnp.bfloat16)
        both=dot_nn(jnp.concatenate([hi,lo],axis=0),qb)
        dvec=dvec+(both[0:8]+both[8:16])
        for x in range(2):
            seg=slice(x*half,(x+1)*half)
            outs[x]=outs[x]+vecT[seg,x:x+1]*dl[x:x+1]+vecT[seg,2+x:3+x]*dl[2+x:3+x]
        dq_ref[rows,:]=(jnp.concatenate(outs,axis=0)*(half**-0.5)).T.astype(jnp.bfloat16)
    dk_ref[...]=dk_acc[...].astype(jnp.bfloat16)
    dv_ref[...]=dv_acc[...].astype(jnp.bfloat16)
    dmv_ref[...]=dmv.astype(jnp.bfloat16)
    row=lax.broadcasted_iota(jnp.int32,dvec.shape,0)
    lane=lax.broadcasted_iota(jnp.int32,dvec.shape,1)
    dvec=jnp.where((row%2==0)==(lane<half),dvec,0.0)
    hi=dvec.astype(jnp.bfloat16); lo=(dvec-hi.astype(jnp.float32)).astype(jnp.bfloat16)
    stack=jnp.concatenate([hi,lo],axis=0)
    gl=dot_nt(stack,mk)
    gls_ref[0]=gl[0:8]+gl[8:16]
    wT=wls_ref[0].astype(jnp.float32).T.astype(jnp.bfloat16)
    dmk_ref[...]=dot_nn(jnp.concatenate([wT,wT],axis=1),stack).astype(jnp.bfloat16)

def col_block(rows,width,first,stride=1):
    return pl.BlockSpec((rows,width),lambda p,info: (0,first+stride*p))

def attention_forward(info,qkv,kv,halo,mem_kv,wls,heads,vmem):
    S=qkv.shape[0]; pairs=heads//2; width=kv[0].shape[1]
    nb=mem_kv.shape[0]; feat=mem_kv.shape[1]//2; w=feat//pairs; half=w//2
    karr,koff,varr,voff=kv[0],kv[1],kv[2],kv[3]
    nblk=S//TILE
    spec=pltpu.PrefetchScalarGridSpec(num_scalar_prefetch=1,grid=(pairs,),
        in_specs=[col_block(S,w,0),col_block(halo+S,w,koff),col_block(halo+S,w,voff),col_block(nb,w,0),col_block(nb,w,pairs),
                  pl.BlockSpec((1,8,nb),lambda p,info:(p,0,0))],
        out_specs=[col_block(S,w,0),pl.BlockSpec((1,8,S),lambda p,info:(p,0,0))],
        scratch_shapes=[pltpu.VMEM((2*nblk,TILE,TILE),jnp.float32)])
    return pl.pallas_call(functools.partial(fwd_kernel,halo,half),grid_spec=spec,
        out_shape=[jax.ShapeDtypeStruct((S,feat),jnp.bfloat16),jax.ShapeDtypeStruct((pairs,8,S),jnp.float32)],
        compiler_params=pltpu.CompilerParams(vmem_limit_bytes=vmem,dimension_semantics=("arbitrary",)),
        cost_estimate=pl.CostEstimate(flops=24*S*S*feat//4,bytes_accessed=10*S*feat,transcendentals=heads*S*768),
        name="mix_forward")(info,qkv,karr,varr,mem_kv,mem_kv,wls)

def attention_backward(info,qkv,kv,halo,mem_kv,wls,lse,d_context,heads,vmem,begin,count,stride):
    S=qkv.shape[0]; pairs=heads//2
    nb=mem_kv.shape[0]; feat=mem_kv.shape[1]//2; w=feat//pairs; half=w//2
    karr,koff,varr,voff=kv
    nblk=S//TILE; bf=jnp.bfloat16
    spec=pltpu.PrefetchScalarGridSpec(num_scalar_prefetch=1,grid=(count,),
        in_specs=[col_block(S,w,begin,stride),col_block(halo+S,w,koff+begin,stride),col_block(halo+S,w,voff+begin,stride),
                  col_block(nb,w,begin,stride),col_block(nb,w,pairs+begin,stride),pl.BlockSpec((1,8,nb),lambda p,info:(begin+stride*p,0,0)),
                  pl.BlockSpec((1,8,S),lambda p,info:(begin+stride*p,0,0)),col_block(S,w,begin,stride)],
        out_specs=[col_block(S,w,0),col_block(halo+S,w,0),col_block(halo+S,w,0),col_block(nb,w,0),col_block(nb,w,0),
                   pl.BlockSpec((1,8,nb),lambda p,info:(p,0,0))],
        scratch_shapes=[pltpu.VMEM((2*nblk,TILE,TILE),jnp.float32),pltpu.VMEM((halo+S,w),jnp.float32),pltpu.VMEM((halo+S,w),jnp.float32)])
    part=count*w
    return pl.pallas_call(functools.partial(bwd_kernel,halo,half),grid_spec=spec,
        out_shape=[jax.ShapeDtypeStruct((S,part),bf),jax.ShapeDtypeStruct((halo+S,part),bf),jax.ShapeDtypeStruct((halo+S,part),bf),
                   jax.ShapeDtypeStruct((nb,part),bf),jax.ShapeDtypeStruct((nb,part),bf),jax.ShapeDtypeStruct((count,8,nb),jnp.float32)],
        compiler_params=pltpu.CompilerParams(vmem_limit_bytes=vmem,dimension_semantics=("arbitrary",)),
        cost_estimate=pl.CostEstimate(flops=30*S*S*part,bytes_accessed=20*S*part,transcendentals=2*count*S*768),
        name="mix_backward")(info,qkv,karr,varr,mem_kv,mem_kv,wls,lse,d_context)


eps=1e-5
TN=(((0,),(0,)),((),()))
def dot_tn(a,b): return lax.dot_general(a,b,TN,preferred_element_type=jnp.float32)

def norm_parts(v):
    center=jnp.mean(v,axis=-1,keepdims=True)
    off=v-center
    rstd=lax.rsqrt(jnp.mean(off*off,axis=-1,keepdims=True)+eps)
    return off*rstd,rstd

def norm_back(gd,xhat,rstd):
    return rstd*(gd-jnp.mean(gd,axis=-1,keepdims=True)-xhat*jnp.mean(gd*xhat,axis=-1,keepdims=True))

def whole(shape): return pl.BlockSpec(shape,lambda *a: (0,)*len(shape),pipeline_mode=pl.Buffered(1))

def shard_copies(loads, pieces, targets, sem, row, col, which):
    for n, (src, dst, fr, fc, rows, cols, slot, at, column, width) in enumerate(loads):
        if dst not in which:
            continue
        if rows is None:
            yield pltpu.make_async_copy(pieces[src], targets[dst], sem.at[n])
            continue
        r0 = pl.multiple_of((row ^ fr) * rows, 16)
        c0 = pl.multiple_of((col ^ fc) * cols + column, 128)
        yield pltpu.make_async_copy(
            pieces[src].at[slot, :, pl.ds(at, width)], targets[dst].at[pl.ds(r0, rows), pl.ds(c0, width)], sem.at[n]
        )


def qkv_kernel(loads, pairs, info_ref, x_ref, vec_ref, own_ref, came_ref, *refs):
    count = max(load[0] for load in loads) + 1
    pieces, refs = refs[:count], refs[count:]
    nT_ref, o_ref, mem_ref, bT_ref, wq_ref, wq_s, wm_s, in_sem, out_sem = refs
    i = pl.program_id(0)
    D = wq_s.shape[0]
    w, half = D // pairs, pairs // 2
    outs = []
    for n in range(3 * pairs):
        kind, p, j = n // pairs, n % pairs // 2, n % 2
        at = kind * D + (j * half + p) * w
        copy = pltpu.make_async_copy(wq_s.at[:, at : at + w], wq_ref.at[:, n * w : (n + 1) * w], out_sem.at[n])
        outs.append(copy)

    @pl.when(i == 0)
    def _():
        for begin in (True, False):
            for copy in shard_copies(loads, pieces, (wq_s, wm_s), in_sem, info_ref[2], info_ref[3], (0, 1)):
                copy.start() if begin else copy.wait()
        for out in outs:
            out.start()
        basis = (own_ref[...] + came_ref[...].astype(jnp.float32)).astype(jnp.bfloat16)
        bT_ref[...] = basis.T
        mem_ref[...] = dot_nn(basis, wm_s[...]).astype(jnp.bfloat16)

    xhat, _ = norm_parts(x_ref[...].astype(jnp.float32))
    n = (xhat * vec_ref[0:1] + vec_ref[1:2]).astype(jnp.bfloat16)
    nT_ref[...] = n.T
    o_ref[...] = dot_nn(n, wq_s[...]).astype(jnp.bfloat16)

    @pl.when(i == pl.num_programs(0) - 1)
    def _():
        for out in outs:
            out.wait()


def project_qkv(info, x, vec, own_basis, came_basis, pieces, loads, pairs, vmem, rows=256):
    S, D = x.shape
    nb = own_basis.shape[0]
    bf, sd = jnp.bfloat16, jax.ShapeDtypeStruct
    hbm = pl.BlockSpec(memory_space=pl.ANY)
    return pl.pallas_call(
        functools.partial(qkv_kernel, loads, pairs),
        grid_spec=pltpu.PrefetchScalarGridSpec(
            num_scalar_prefetch=1,
            grid=(S // rows,),
            in_specs=[pl.BlockSpec((rows, D), lambda i, info: (i, 0)), whole((8, D)), whole((nb, D)), whole((nb, D))]
            + [hbm] * len(pieces),
            out_specs=[
                pl.BlockSpec((D, rows), lambda i, info: (0, i)), pl.BlockSpec((rows, 3 * D), lambda i, info: (i, 0)),
                whole((nb, 2 * D)), whole((D, nb)), hbm,
            ],
            scratch_shapes=[
                pltpu.VMEM((D, 3 * D), bf), pltpu.VMEM((D, 2 * D), bf),
                pltpu.SemaphoreType.DMA((len(loads),)), pltpu.SemaphoreType.DMA((3 * pairs,)),
            ],
        ),
        out_shape=[sd((D, S), bf), sd((S, 3 * D), bf), sd((nb, 2 * D), bf), sd((D, nb), bf), sd((D, 3 * D), bf)],
        compiler_params=pltpu.CompilerParams(vmem_limit_bytes=vmem),
        cost_estimate=pl.CostEstimate(
            flops=6 * S * D * D + 4 * nb * D * D, bytes_accessed=10 * S * D + 16 * D * D, transcendentals=0
        ),
        name="project_qkv",
    )(info, x, vec, own_basis, came_basis, *pieces)


def row_slot(fr, order):
    return sum(((fr >> bit) & 1) << i for i, (axis, bit) in enumerate(order[:-1]) if axis == "row")


def col_slot(fc, order):
    return sum(((fc >> bit) & 1) << i for i, (axis, bit) in enumerate(order[:-1]) if axis == "col")


class _Fixed:
    def __init__(self, sem):
        self.at = self
        self.sem = sem

    def __getitem__(self, index):
        return self.sem


def mlp_kernel(steps, chunk, loads, cut, info_ref, c_ref, x_ref, g_ref, vec_ref, bf_ref, *refs):
    count = max(load[0] for load in loads) + 1
    pieces, refs = refs[:count], refs[count:]
    out_ref, dmid_ref, dctx_ref, gv_ref, gb_ref = refs[:5]
    made = 3 if cut is None else 4
    grads, refs = refs[5 : 5 + made], refs[5 + made :]
    n_s, nT_s, dm_s, mid_s, acc_s, dn_s, hid_s, dp_s, wf_s, wo_s, wp_s, go_s, gf_s, gp_s, in_sem, out_sem, go_sem = refs
    f = pl.program_id(0)
    S, D = x_ref.shape
    fb = gf_s.shape[2]
    length, base, row, col = info_ref[0], info_ref[1], info_ref[2], info_ref[3]
    nchunk = S // chunk
    buf = f % 2
    fe, per_col = f, steps
    if cut is not None:
        fe, per_col = f ^ (row // (cut[0] // steps)), steps // cut[1]

    def valid_of(i):
        pos = base + i * chunk + lax.broadcasted_iota(jnp.int32, (chunk, 1), 0)
        return jnp.where(pos < length, 1.0, 0.0)

    targets = (wf_s, wo_s, wp_s)

    def arrive(which, rows=None, cols=None):
        if cut is None:
            for copy in shard_copies(loads, pieces, targets, in_sem, row, col, which):
                copy.wait()
            return
        n_rows, n_cols = cut[:2]
        seen = set()
        for src, dst, _, _, height, across, slot, at, _, width in loads:
            if dst not in which or dst in seen:
                continue
            seen.add(dst)
            for r in range(n_rows) if rows is None else rows:
                for c in range(n_cols) if cols is None else cols:
                    n = (dst * n_rows + r) * n_cols + c
                    pltpu.make_async_copy(
                        pieces[src].at[slot, :, pl.ds(at, width)], targets[dst].at[:height, :width], in_sem.at[n]
                    ).wait()

    def depart(which, only=None):
        for n, load in enumerate(loads):
            if load[1] in which:
                place = n
                if cut is not None:
                    place = (load[1] * cut[0] + (row ^ load[2])) * cut[1] + (col ^ load[3])
                copy = next(shard_copies([load], pieces, targets, _Fixed(in_sem.at[place]), row, col, which))
                if only is None:
                    copy.start()
                else:
                    pl.when((col ^ load[3]) == only)(copy.start)

    def block_copies(begin, buf=buf):
        if cut is None:
            copies = [
                pltpu.make_async_copy(gf_s.at[buf], grads[0].at[:, pl.ds(pl.multiple_of(fe * fb, 128), fb)], out_sem.at[buf, 0]),
                pltpu.make_async_copy(gp_s.at[buf], grads[2].at[pl.ds(pl.multiple_of(fe * fb, 16), fb), :], out_sem.at[buf, 1]),
            ]
            for copy in copies:
                copy.start() if begin else copy.wait()
            return
        n_rows, n_cols, order2, order3 = cut
        rows2, rows3 = D // n_rows, fb * steps // n_rows
        cols2, cols3 = fb * steps // n_cols, D // n_cols
        per = cols2 // fb
        c = fe // per
        at = pl.multiple_of((fe % per) * fb, 128)
        for fr in range(n_rows):
            slot = row_slot(fr, order2) + col_slot(c ^ col, order2)
            src = gf_s.at[buf, pl.ds(pl.multiple_of((row ^ fr) * rows2, 16), rows2), :]
            copy = pltpu.make_async_copy(src, grads[fr & 1].at[slot, :, pl.ds(at, fb)], out_sem.at[buf, fr])
            copy.start() if begin else copy.wait()
        n = n_rows
        for i in range(fb // rows3):
            rel = (fe * (fb // rows3) + i) ^ row
            for c in range(n_cols):
                slot = row_slot(rel, order3) + col_slot(c ^ col, order3)
                src = gp_s.at[buf, i * rows3 : (i + 1) * rows3, c * cols3 : (c + 1) * cols3]
                if begin:
                    for side in range(2):

                        @pl.when(rel & 1 == side)
                        def _():
                            pltpu.make_async_copy(src, grads[2 + side].at[slot], out_sem.at[buf, n]).start()
                else:
                    pltpu.make_async_copy(src, grads[2].at[0], out_sem.at[buf, n]).wait()
                n += 1

    @pl.when(f == 0)
    def _():
        depart((1,))
        if cut is None:
            depart((0, 2))
        else:
            depart((0,), fe // per_col)
        for i in range(nchunk):
            rs = slice(i * chunk, (i + 1) * chunk)
            dm_s[rs, :] = (g_ref[rs, :].astype(jnp.float32) * valid_of(i)).astype(jnp.bfloat16)
        acc_s[...] = jnp.zeros_like(acc_s)
        dn_s[...] = jnp.zeros_like(dn_s)
        if cut is not None:
            depart((2,))
            for c in range(1, cut[1]):
                depart((0,), fe // per_col ^ c)
        arrive((1,))
        for i in range(nchunk):
            rs = slice(i * chunk, (i + 1) * chunk)
            branch = dot_nn(c_ref[rs, :], wo_s[...]) + vec_ref[2:3]
            mid = x_ref[rs, :].astype(jnp.float32) + valid_of(i) * branch
            mid_s[rs, :] = mid
            xhat, _ = norm_parts(mid)
            n = (xhat * vec_ref[0:1] + vec_ref[1:2]).astype(jnp.bfloat16)
            n_s[rs, :] = n
            nT_s[:, rs] = n.T
        if cut is None:
            arrive((0, 2))

    if cut is not None:

        @pl.when(f % per_col == 0)
        def _():
            arrive((0,), None, [fe // per_col])

        each = cut[0] // steps
        arrive((2,), [fe * each + i for i in range(each)])

    @pl.when(f >= 2)
    def _():
        block_copies(False)

    cs = pl.ds(pl.multiple_of(fe * fb, 128), fb)
    wf = wf_s[:, cs]
    wp = wp_s[cs, :]
    c0 = math.sqrt(2.0 / math.pi)
    gb = jnp.zeros((1, fb), jnp.float32)
    for i in range(nchunk):
        rs = slice(i * chunk, (i + 1) * chunk)
        pre = dot_nn(n_s[rs, :], wf) + bf_ref[...]
        sq = pre * pre
        t = jnp.tanh(c0 * pre * (1.0 + 0.044715 * sq))
        hp = 0.5 * pre
        hid = hp + hp * t
        dgel = 0.5 + 0.5 * t + hp * (1.0 - t * t) * (c0 * (1.0 + (3 * 0.044715) * sq))
        hidb = hid.astype(jnp.bfloat16)
        hid_s[rs, :] = hidb
        acc_s[rs, :] += dot_nn(hidb, wp)
        dpb = (dot_nt(dm_s[rs, :], wp) * dgel).astype(jnp.bfloat16)
        dp_s[rs, :] = dpb
        gb = gb + jnp.sum(dpb.astype(jnp.float32), axis=0, keepdims=True)
        dn_s[rs, :] += dot_nt(dpb, wf)
    gb_ref[...] = jnp.broadcast_to(gb, gb_ref.shape)
    gf_s[buf] = dot_nn(nT_s[...], dp_s[...]).astype(jnp.bfloat16)
    gp_s[buf] = dot_tn(hid_s[...], dm_s[...]).astype(jnp.bfloat16)
    block_copies(True)

    @pl.when(f == steps - 1)
    def _():
        gg = jnp.zeros((1, D), jnp.float32)
        gbi, gbo, gbp = gg, gg, gg
        for i in range(nchunk):
            rs = slice(i * chunk, (i + 1) * chunk)
            valid = valid_of(i)
            mid = mid_s[rs, :]
            out_ref[rs, :] = (mid + valid * (acc_s[rs, :] + vec_ref[3:4])).astype(jnp.bfloat16)
            xhat, rstd = norm_parts(mid)
            dn = dn_s[rs, :]
            cot = dm_s[rs, :].astype(jnp.float32)
            dmid = cot + norm_back(dn * vec_ref[0:1], xhat, rstd)
            dmid_ref[rs, :] = dmid
            db = (valid * dmid).astype(jnp.bfloat16)
            gg = gg + jnp.sum(dn * xhat, axis=0, keepdims=True)
            gbi = gbi + jnp.sum(dn, axis=0, keepdims=True)
            gbo = gbo + jnp.sum(db.astype(jnp.float32), axis=0, keepdims=True)
            gbp = gbp + jnp.sum(cot, axis=0, keepdims=True)
            n_s[rs, :] = db
        go_s[...] = dot_tn(c_ref[...], n_s[...]).astype(jnp.bfloat16)
        copies = []
        if cut is None:
            copies.append(pltpu.make_async_copy(go_s, grads[1], go_sem.at[0]))
        else:
            n_rows, n_cols, order2, _ = cut
            rows, cols = D // n_rows, D // n_cols
            at = fb * steps // n_cols
            for fr in range(n_rows):
                for c in range(n_cols):
                    slot = row_slot(fr, order2) + col_slot(c ^ col, order2)
                    src = go_s.at[pl.ds(pl.multiple_of((row ^ fr) * rows, 16), rows), c * cols : (c + 1) * cols]
                    dst = grads[fr & 1].at[slot, :, at : at + cols]
                    copies.append(pltpu.make_async_copy(src, dst, go_sem.at[len(copies)]))
        for copy in copies:
            copy.start()
        for i in range(nchunk):
            rs = slice(i * chunk, (i + 1) * chunk)
            dctx_ref[rs, :] = dot_nt(n_s[rs, :], wo_s[...]).astype(jnp.bfloat16)
        gv_ref[...] = jnp.concatenate([gbo, gg, gbi, gbp, jnp.zeros((4, D), jnp.float32)], axis=0)
        for copy in copies:
            copy.wait()
        for slot in range(min(2, steps)):
            block_copies(False, slot)


def mlp_block(info, context, x, d_out, pieces, loads, vec, b_fc, cut, widths, vmem, fb=768, chunk=256):
    S, D = x.shape
    FF = b_fc.shape[1]
    steps = FF // fb
    bf, f32, sd = jnp.bfloat16, jnp.float32, jax.ShapeDtypeStruct
    hbm = pl.BlockSpec(memory_space=pl.ANY)
    if cut is None:
        grads = [sd((D, FF), bf), sd((D, D), bf), sd((FF, D), bf)]
        n_in, n_out, n_go = len(loads), 2, 1
    else:
        n_rows, n_cols = cut[:2]
        half = n_rows * n_cols // 2
        grads = [sd((half, D // n_rows, sum(widths)), bf)] * 2 + [sd((half, FF // n_rows, D // n_cols), bf)] * 2
        n_in = 3 * n_rows * n_cols
        n_out, n_go = n_rows + fb * n_rows // FF * n_cols, n_rows * n_cols
    if cut is None:
        at = lambda f, info: (0, f)
    else:
        at = lambda f, info: (0, f ^ (info[2] // (n_rows // steps)))
    spec = pltpu.PrefetchScalarGridSpec(
        num_scalar_prefetch=1,
        grid=(steps,),
        in_specs=[whole((S, D))] * 3 + [whole((8, D)), pl.BlockSpec((1, fb), at)] + [hbm] * len(pieces),
        out_specs=[whole((S, D))] * 3 + [whole((8, D)), pl.BlockSpec((8, fb), at)] + [hbm] * len(grads),
        scratch_shapes=[
            pltpu.VMEM((S, D), bf), pltpu.VMEM((D, S), bf), pltpu.VMEM((S, D), bf),
            pltpu.VMEM((S, D), f32), pltpu.VMEM((S, D), f32), pltpu.VMEM((S, D), f32),
            pltpu.VMEM((S, fb), bf), pltpu.VMEM((S, fb), bf),
            pltpu.VMEM((D, FF), bf), pltpu.VMEM((D, D), bf), pltpu.VMEM((FF, D), bf), pltpu.VMEM((D, D), bf),
            pltpu.VMEM((2, D, fb), bf), pltpu.VMEM((2, fb, D), bf),
            pltpu.SemaphoreType.DMA((n_in,)), pltpu.SemaphoreType.DMA((2, n_out)), pltpu.SemaphoreType.DMA((n_go,)),
        ],
    )
    return pl.pallas_call(
        functools.partial(mlp_kernel, steps, chunk, loads, cut),
        grid_spec=spec,
        out_shape=[sd((S, D), bf), sd((S, D), f32), sd((S, D), bf), sd((8, D), f32), sd((8, FF), f32)] + grads,
        compiler_params=pltpu.CompilerParams(vmem_limit_bytes=vmem, dimension_semantics=("arbitrary",)),
        cost_estimate=pl.CostEstimate(
            flops=12 * S * D * FF + 6 * S * D * D, bytes_accessed=8 * D * FF + 20 * S * D, transcendentals=S * FF
        ),
        name="mlp_block",
    )(info, context, x, d_out, vec, b_fc, *pieces)


def wgrad_kernel(cut, count, split, info_ref, nT_ref, bT_ref, *refs):
    n_rows, n_cols = cut
    parts, outs, (g_s, sem) = refs[: 5 * count], refs[5 * count : -2], refs[-2:]
    D = nT_ref.shape[0]
    rows, w = D // n_rows, parts[0].shape[1] // 2
    row, col = info_ref[2], info_ref[3]
    copies = []
    nT, bT = nT_ref[...], bT_ref[...]
    for c in range(n_cols):
        at = 0
        for p in range(count):
            q_ref, k_ref, v_ref, mk_ref, mv_ref = parts[5 * p : 5 * p + 5]
            if c == 0:
                terms = [(nT, q_ref[...]), (nT, k_ref[:, :w]), (bT, mk_ref[...])]
            else:
                terms = [(nT, k_ref[:, w:]), (nT, v_ref[...]), (bT, mv_ref[...])]
            for left, right in terms:
                g_s[c, :, at : at + right.shape[1]] = dot_nn(left, right).astype(jnp.bfloat16)
                at += right.shape[1]
        at = 0
        for i, (width, order) in enumerate(split):
            for fr in range(n_rows):
                slot = row_slot(fr, order) + col_slot(c ^ col, order)
                block = g_s.at[c, pl.ds(pl.multiple_of((row ^ fr) * rows, 16), rows), at : at + width]
                copies.append(pltpu.make_async_copy(block, outs[2 * i + (fr & 1)].at[slot], sem.at[len(copies)]))
                copies[-1].start()
            at += width
    for copy in copies:
        copy.wait()


def weight_grads(info, nT, bT, parts, n_rows, split, vmem):
    D, S = nT.shape
    nb, w, n_cols, count = bT.shape[1], parts[0][0].shape[1] // 2, 2, len(parts)
    rows = D // n_rows
    flat = [d for part in parts for d in part]
    bf, hbm = jnp.bfloat16, pl.BlockSpec(memory_space=pl.ANY)
    outs = []
    for width, _ in split:
        outs += [jax.ShapeDtypeStruct((n_rows * n_cols // 2, rows, width), bf)] * 2
    outs = pl.pallas_call(
        functools.partial(wgrad_kernel, (n_rows, n_cols), count, split),
        grid_spec=pltpu.PrefetchScalarGridSpec(
            num_scalar_prefetch=1,
            grid=(1,),
            in_specs=[whole(a.shape) for a in [nT, bT] + flat],
            out_specs=[hbm] * len(outs),
            scratch_shapes=[
                pltpu.VMEM((n_cols, D, 5 * w * count), bf), pltpu.SemaphoreType.DMA((n_rows * n_cols * len(split),)),
            ],
        ),
        out_shape=outs,
        compiler_params=pltpu.CompilerParams(vmem_limit_bytes=vmem),
        cost_estimate=pl.CostEstimate(
            flops=12 * S * D * w * count, bytes_accessed=14 * S * w * count + 2 * S * D + 20 * D * w * count, transcendentals=0
        ),
        name="weight_grads",
    )(info, nT, bT, *flat)
    return [Scatter(outs[2 * i], outs[2 * i + 1], order) for i, (_, order) in enumerate(split)]


def tokens_kernel(count,w_ref,x_ref,dm_ref,gain_ref,*refs):
    o_ref,gv_ref=refs[-2:]
    i=pl.program_id(0); D=x_ref.shape[1]; width=D//(2*count)
    dn=None
    for kind in range(3):
        for p in range(count):
            at=kind*D+2*p*width
            term=dot_nt(refs[3*p+kind][...],w_ref[:,at:at+2*width])
            dn=term if dn is None else dn+term
    xhat,rstd=norm_parts(x_ref[...].astype(jnp.float32))
    o_ref[...]=dm_ref[...]+norm_back(dn*gain_ref[0:1],xhat,rstd)
    @pl.when(i==0)
    def _(): gv_ref[...]=jnp.zeros_like(gv_ref)
    gv_ref[0:1]+=jnp.sum(dn*xhat,axis=0,keepdims=True)
    gv_ref[1:2]+=jnp.sum(dn,axis=0,keepdims=True)

def token_grad(parts,w,x,d_middle,gain,vmem,rows=256):
    S,D=x.shape; count=len(parts); width=D//count
    by_row=lambda width: pl.BlockSpec((rows,width),lambda i:(i,0))
    return pl.pallas_call(functools.partial(tokens_kernel,count),grid=(S//rows,),
        in_specs=[whole((D,3*D)),by_row(D),by_row(D),whole((8,D))]+[by_row(width)]*(3*count),
        out_specs=[by_row(D),pl.BlockSpec((8,D),lambda i:(0,0))],
        out_shape=[jax.ShapeDtypeStruct((S,D),jnp.float32),jax.ShapeDtypeStruct((8,D),jnp.float32)],
        compiler_params=pltpu.CompilerParams(vmem_limit_bytes=vmem),
        cost_estimate=pl.CostEstimate(flops=6*S*D*D,bytes_accessed=16*S*D+6*D*D,transcendentals=0),name="token_grad")(w,x,d_middle,gain,*[d for part in parts for d in part])


VMEM_BYTES = 58 << 20
MLP_VMEM_BYTES = 50 << 20
FIT_NODE_COUNT = 512
ridge = 0.5


def fit_constant(nb):
    centers = (np.arange(nb, dtype=np.float64) + 0.5) / nb
    times = (np.arange(FIT_NODE_COUNT, dtype=np.float64) + 0.5) / FIT_NODE_COUNT
    design = np.exp(-0.5 * (times[None, :] - centers[:, None]) ** 2 * (nb * nb))
    table = np.linalg.solve(design @ design.T + ridge * np.eye(nb), design).astype(np.float32)
    hi = table.astype(jnp.bfloat16)
    lo = (table - hi.astype(np.float32)).astype(jnp.bfloat16)
    return np.concatenate([hi, lo], axis=0)


def bits_of(n):
    count = n.bit_length() - 1
    assert 1 << count == n
    return count


def swap(block, stage):
    axis, bit = stage
    n = lax.axis_size(axis)
    return lax.ppermute(block, axis, [(i, i ^ (1 << bit)) for i in range(n)])


class Chain:
    def __init__(self):
        self.last = ()

    def wait(self, *values):
        got = lax.optimization_barrier(values + self.last)
        self.last = got[:1]
        return got[0] if len(values) == 1 else got[: len(values)]


def stage_lists():
    rows = bits_of(lax.axis_size("row"))
    cols = bits_of(lax.axis_size("col"))
    far = [("row", b) for b in range(rows - 1, 1, -1)]
    col = [("col", b) for b in range(cols - 1, -1, -1)]
    near = [("row", 1)] if rows > 1 else []
    return far, col, near, [("row", 0)]


def slot_offsets(order):
    table = []
    for slot in range(1 << len(order)):
        flips = {"row": 0, "col": 0}
        for i, (axis, bit) in enumerate(order):
            if slot >> i & 1:
                flips[axis] ^= 1 << bit
        table.append((flips["row"], flips["col"]))
    return table


def place_bits():
    rows, cols = bits_of(lax.axis_size("row")), bits_of(lax.axis_size("col"))
    return [("row", b) for b in range(rows - 1, -1, -1)] + [("col", b) for b in range(cols - 1, -1, -1)]


def by_place(slots, order):
    seen = order[::-1]
    dims = [seen.index(p) for p in place_bits()]
    split = slots.reshape((2,) * len(order) + slots.shape[1:])
    tail = range(len(order), split.ndim)
    return split.transpose(dims + list(tail)).reshape(slots.shape)


def by_slot(blocks, order):
    places = place_bits()
    dims = [places.index(p) for p in order[::-1]]
    split = blocks.reshape((2,) * len(order) + blocks.shape[1:])
    tail = range(len(order), split.ndim)
    return split.transpose(dims + list(tail)).reshape(blocks.shape)


def flipped(blocks, row, col):
    places = place_bits()
    split = blocks.reshape((2,) * len(places) + blocks.shape[1:])
    for dim, (axis, bit) in enumerate(places):
        mine = (row if axis == "row" else col) >> bit & 1
        split = jnp.where(mine == 1, jnp.flip(split, dim), split)
    return split.reshape(blocks.shape)


class Gather:
    def __init__(self, block, order, done=0):
        self.held, self.order, self.done = (block if done else block[None]), order, done

    def send(self):
        self.came = swap(self.held, self.order[self.done])
        return self

    def take(self, came):
        self.done += 1
        if self.done == len(self.order):
            self.came = came
        else:
            self.held = jnp.concatenate([self.held, came], axis=0)
        return self

    def halves(self, cut, orders):
        return [
            Gather(self.held[:, :, :cut], orders[0], self.done),
            Gather(self.held[:, :, cut:], orders[1], self.done),
        ]


def advance(chain, *gathers):
    got = chain.wait(*[g.came for g in gathers])
    got = got if len(gathers) > 1 else (got,)
    for g, came in zip(gathers, got):
        g.take(came)
        if g.done < len(g.order):
            g.send()


def copy_kernel(plans, place_ref, *refs):
    sem = refs[-1]
    copies = []
    for src, dst, fr, fc, rows, cols, slot, at, column, width, outward in plans:
        r = place_ref[0] ^ fr
        c = place_ref[1] ^ fc
        matrix, slots = (refs[dst], refs[src]) if outward else (refs[src], refs[dst])
        block = matrix.at[
            pl.ds(pl.multiple_of(r * rows, 8), rows), pl.ds(pl.multiple_of(c * cols + column, 128), width)
        ]
        piece = slots.at[slot, :, pl.ds(at, width)]
        pair = (piece, block) if outward else (block, piece)
        copies.append(pltpu.make_async_copy(*pair, sem.at[len(copies)]))
    for copy in copies:
        copy.start()
    for copy in copies:
        copy.wait()


def copy_call(plans, place, ins, out_shapes, resident, name):
    hbm = pl.BlockSpec(memory_space=pl.ANY)
    size = sum(math.prod(o.shape) for o in out_shapes)
    return pl.pallas_call(
        functools.partial(copy_kernel, plans),
        grid_spec=pltpu.PrefetchScalarGridSpec(
            num_scalar_prefetch=1,
            grid=(1,),
            in_specs=[hbm] * len(ins),
            out_specs=[whole(o.shape) if resident else hbm for o in out_shapes],
            scratch_shapes=[pltpu.SemaphoreType.DMA((len(plans),))],
        ),
        out_shape=out_shapes,
        compiler_params=pltpu.CompilerParams(vmem_limit_bytes=24 << 20),
        cost_estimate=pl.CostEstimate(flops=0, bytes_accessed=4 * size, transcendentals=0),
        name=name,
    )(place, *ins)


def ranges_of(layout, offset, width):
    found, at = [], 0
    for i, size in enumerate(layout):
        low, high = max(at, offset), min(at + size, offset + width)
        if low < high:
            found.append((i, low - offset, low - at, high - low))
        at += size
    return found


def assemble(place, gathers, layout, n_rows, n_cols):
    rows = gathers[0].held.shape[1]
    shapes = [jax.ShapeDtypeStruct((rows * n_rows, w * n_cols), jnp.bfloat16) for w in layout]
    pieces, plans, offset = [], [], 0
    aligned = rows % 8 == 0 and all(w % 128 == 0 for w in layout)
    if not aligned:
        full = []
        for g in gathers:
            slots = jnp.concatenate([g.held, g.came], axis=0)
            full.append(flipped(by_place(slots, g.order), place[0], place[1]))
        full = jnp.concatenate(full, axis=2)
        res, at = [], 0
        for w in layout:
            block = full[:, :, at : at + w].reshape(n_rows, n_cols, rows, w)
            res.append(block.transpose(0, 2, 1, 3).reshape(rows * n_rows, w * n_cols))
            at += w
        return res
    for g in gathers:
        table = slot_offsets(g.order)
        width = g.held.shape[2]
        for slot, (fr, fc) in enumerate(table):
            src = len(pieces) + slot // (len(table) // 2)
            for i, at, column, w in ranges_of(layout, offset, width):
                plans.append((src, i, fr, fc, rows, layout[i], slot % (len(table) // 2), at, column, w, True))
        pieces += [g.held, g.came]
        offset += width
    plans = [(p[0], len(pieces) + p[1]) + p[2:] for p in plans]
    return copy_call(plans, place, pieces, shapes, True, "assemble")


class Scatter:
    def __init__(self, keep, send, order):
        self.order, self.left = order, len(order)
        self.terms, self.out = [keep], send
        self.total = None

    def send(self):
        self.left -= 1
        self.came = swap(self.out, self.order[self.left])
        return self

    def take(self, came):
        self.terms.append(came)
        if self.left == 0:
            self.total = sum(t.astype(jnp.float32) for t in self.terms)[0]
            return self
        half = self.terms[0].shape[0] // 2
        self.out = sum(t[half:].astype(jnp.float32) for t in self.terms).astype(jnp.bfloat16)
        self.terms = [t[:half] for t in self.terms]
        return self


def onward(chain, *scatters):
    got = chain.wait(*[s.came for s in scatters])
    got = got if len(scatters) > 1 else (got,)
    for s, came in zip(scatters, got):
        s.take(came)
        if s.left:
            s.send()


def disperse(place, grads, cuts, n_rows, n_cols):
    rows = grads[0].shape[0] // n_rows
    blocks = [g.reshape(n_rows, rows, n_cols, -1).transpose(0, 2, 1, 3) for g in grads]
    joined = jnp.concatenate(blocks, axis=3).reshape(n_rows * n_cols, rows, -1)
    joined = flipped(joined, place[0], place[1])
    res, offset = [], 0
    for width, order in cuts:
        slots = by_slot(joined[:, :, offset : offset + width], order)
        res.append(Scatter(slots[: len(slots) // 2], slots[len(slots) // 2 :], order))
        offset += width
    return res


def shards(
    tokens, w_qkv, w_out, w_mem, w_fc, w_proj, gain_attn, bias_attn, gain_mlp, bias_mlp, b_out, b_fc, b_proj,
    w_loc, w_spread, past_states, sticky_pos, seq_lengths, d_out,
):
    bf, f32 = jnp.bfloat16, jnp.float32
    n_rows, n_cols = lax.axis_size("row"), lax.axis_size("col")
    row, col = lax.axis_index("row"), lax.axis_index("col")
    place = jnp.stack([row, col]).astype(jnp.int32)
    batches, _, span, feat = tokens.shape
    heads, nb = w_loc.shape[0], w_loc.shape[1] * n_rows * n_cols
    hidden = w_fc.shape[1] * n_cols
    assert batches == 2 and n_cols % 2 == 0
    side = col % 2
    own, other = side, 1 - side
    first = (col - side) * span
    far, along, near, core = stage_lists()
    zyx, zxy, yzx = far + along + near + core, far + near + along + core, along + far + near + core
    devices = n_rows * n_cols

    def pick(a, i):
        return lax.dynamic_index_in_dim(a, i, 0, keepdims=False)

    def to_chunk(mine, came):
        two = jnp.stack([mine, came])
        return jnp.where(side == 0, two, two[::-1]).reshape((2 * span,) + mine.shape[1:])

    def trade(a):
        return swap(a, ("col", 0))

    tokens, past, d_out = tokens[:, 0], past_states[:, 0], d_out[:, 0]
    sticky, lengths = sticky_pos[:, 0], seq_lengths[:, 0]
    length = pick(lengths, own)
    info = jnp.stack([length, first, row, col]).astype(jnp.int32)

    singles = [gain_attn, bias_attn, gain_mlp, bias_mlp, b_out, b_proj, b_fc]
    n_single, n_small = len(singles), len(singles) + heads
    rows_small = -(-n_small // 8) * 8
    both_w = jnp.concatenate([w_loc, w_spread], axis=1)

    def wide(v):
        v = v.reshape(-1, v.shape[-1])
        return jnp.pad(v, ((0, 0), (0, 128 - v.shape[1])))

    layout1 = [w_qkv.shape[1], w_mem.shape[1]]
    layout2 = [w_fc.shape[1], w_out.shape[1]]
    layout3 = [w_proj.shape[1]]
    width1 = sum(layout1)
    cut1 = (width1 // 128 + 1) // 2 * 128
    rows1 = w_qkv.shape[0]
    fb = 768
    direct = n_cols == 2 and all(w % 128 == 0 for w in layout1 + layout2 + layout3) and rows1 % 16 == 0
    steps = hidden // fb
    direct = direct and layout2[0] % fb == 0 and fb % w_proj.shape[0] == 0 and steps & (steps - 1) == 0

    def loads_of(gathers, layout, base, first):
        loads, pieces, offset = [], [], 0
        for g in gathers:
            table = slot_offsets(g.order)
            half, width = len(table) // 2, g.held.shape[2]
            for slot, (fr, fc) in enumerate(table):
                for i, at, column, w in ranges_of(layout, offset, width):
                    src = first + len(pieces) + slot // half
                    loads.append((src, base + i, fr, fc, g.held.shape[1], layout[i], slot % half, at, column, w))
            pieces += [g.held, g.came]
            offset += width
        return loads, pieces

    chain = Chain()
    g1 = Gather(jnp.concatenate([w_qkv, w_mem], axis=1), zyx).send()
    tokens_out, block2 = chain.wait(tokens, jnp.concatenate([w_fc, w_out], axis=1))
    came_tokens = trade(pick(tokens_out, other))
    g2 = Gather(block2, yzx).send()
    g3 = Gather(w_proj, zxy)
    flat = jnp.concatenate([wide(v) for v in singles + [both_w]])
    flat = jnp.pad(flat, ((0, rows_small - n_small), (0, 0)))
    g0 = None
    for _ in far[1:]:
        advance(chain, g1)
        if g0 is None:
            g0 = Gather(chain.wait(flat), zyx).send()
    g1.take(chain.wait(g1.came))
    g1a, g1b = g1.halves(cut1, (zyx, zxy))
    g1a.send()
    g1b.send()
    advance(chain, g0)
    g3.held = chain.wait(g3.held)
    g3.send()
    for _ in far[1:]:
        advance(chain, g3)
    for _ in along:
        advance(chain, g2)
    advance(chain, g0)
    advance(chain, g1b, g1a)

    fit = jnp.asarray(fit_constant(nb))
    here = col * span
    past, sticky = chain.wait(past, sticky)

    def basis_part(i):
        spots = pick(sticky, i) - here
        resident = (spots >= 0) & (spots < span)
        picked = jnp.take(past.reshape(-1, feat), jnp.clip(spots, 0, span - 1) + i * span, axis=0)
        parts = jnp.dot(fit * resident.astype(bf)[None, :], picked, preferred_element_type=f32)
        return parts[:nb] + parts[nb:]

    came_g3 = chain.wait(g3.came)
    if n_cols == 2:
        own_basis, basis_out = chain.wait(basis_part(own), basis_part(other).astype(bf))
    else:
        both = lax.psum(jnp.stack([basis_part(i).astype(bf) for i in range(2)]), "col")
        own_basis, came_basis = pick(both, own).astype(f32), jnp.zeros((nb, feat), bf)
    advance(chain, g0)
    for _ in far[1:]:
        advance(chain, g2)
    x = to_chunk(pick(tokens, own), chain.wait(came_tokens))
    while g1b.done < len(g1b.order) - 1:
        advance(chain, g1b, g1a)
    if n_cols == 2:
        came_basis = trade(chain.wait(basis_out))
    g3.take(chain.wait(came_g3)).send()
    came_out = trade(chain.wait(pick(d_out, other)))
    while g0.done < len(g0.order) - 1:
        advance(chain, g0)
    g0.came = chain.wait(g0.came)
    every = flipped(by_place(jnp.concatenate([g0.held, g0.came], axis=0), zyx), row, col)
    share, width = w_loc.shape[1], gain_attn.shape[0]

    def rows_of(first, count):
        return every[:, first : first + count, :width].transpose(1, 0, 2).reshape(count, feat).astype(f32)

    vec1 = jnp.pad(rows_of(0, 2), ((0, 6), (0, 0)))
    advance(chain, g2)
    x, vec1 = chain.wait(x, vec1)
    g1b.came, g1a.came, came_basis = chain.wait(g1b.came, g1a.came, came_basis)

    if direct:
        loads, pieces = loads_of([g1a, g1b], layout1, 0, 0)
    else:
        pieces = assemble(place, [g1a, g1b], layout1, n_rows, n_cols)
        loads = [(i, i) + (None,) * 8 for i in range(2)]
    nT, qkv, mem_kv, basisT, wq = project_qkv(info, x, vec1, own_basis, came_basis, pieces, loads, heads // 2, VMEM_BYTES)
    qkv, every = chain.wait(qkv, every)
    vec2 = jnp.pad(rows_of(2, 4), ((0, 4), (0, 0)))
    bfc = every[:, n_single - 1, : b_fc.shape[0]].astype(f32).reshape(1, -1)
    loc, spr = [
        every[:, n_single:n_small, at : at + share].transpose(1, 0, 2).reshape(heads // 2, 2, nb) for at in (0, share)
    ]
    wls = jnp.concatenate([loc, spr, jnp.zeros((heads // 2, 4, nb), bf)], axis=1)
    for _ in along[:1]:
        advance(chain, g3)
    g_other = chain.wait(came_out)
    halo = 0 if n_cols == 2 else WINDOW
    pairs = heads // 2
    route = [(i, i + 2) for i in range(n_cols - 2)]
    back = [(i + 2, i) for i in range(n_cols - 2)]
    if halo:
        before = lax.ppermute(qkv[-halo:, feat:], "col", route)
        kvx = jnp.concatenate([before, qkv[:, feat:]], axis=0)
        kv = (kvx, 0, kvx, pairs)
    else:
        kv = (qkv, pairs, qkv, 2 * pairs)
    mem_kv, g2.held, g3.held = chain.wait(mem_kv, g2.held, g3.held)
    context, lse = attention_forward(info, qkv, kv, halo, mem_kv, wls, heads, VMEM_BYTES)
    context = chain.wait(context)
    while g3.done < len(g3.order) - 1:
        advance(chain, g3)
    while g2.done < len(g2.order) - 1:
        advance(chain, g2)
    g_chunk = to_chunk(pick(d_out, own), g_other)
    g3.came, g2.came = chain.wait(g3.came, g2.came)

    if direct:
        loads, pieces = loads_of([g2], layout2, 0, 0)
        loads3, pieces3 = loads_of([g3], layout3, 2, len(pieces))
        loads = loads + loads3
        pieces = [pltpu.with_memory_space_constraint(piece, pltpu.VMEM) for piece in pieces + pieces3]
    else:
        wf, wo = assemble(place, [g2], layout2, n_rows, n_cols)
        wp = assemble(place, [g3], layout3, n_rows, n_cols)[0]
        pieces = [wf, wo, wp]
        loads = [(i, i) + (None,) * 8 for i in range(3)]
    output, d_middle, d_context, g_vec, g_bfc, *cut_grads = mlp_block(
        info, context, x, g_chunk, pieces, loads, vec2, bfc,
        (n_rows, n_cols, yzx, zxy) if direct else None, layout2, MLP_VMEM_BYTES, fb,
    )

    def from_chunk(chunk):
        halves = chunk.reshape(2, span, feat)
        return pick(halves, own), pick(halves, other)

    def paired(kept, came):
        two = jnp.stack([kept, came])
        return jnp.where(side == 0, two, two[::-1])[:, None]

    if direct:
        s2, s3 = Scatter(*cut_grads[:2], yzx), Scatter(*cut_grads[2:], zxy)
    else:
        s2 = disperse(place, cut_grads[:2], [(sum(layout2), yzx)], n_rows, n_cols)[0]
        s3 = disperse(place, cut_grads[2:], [(sum(layout3), zxy)], n_rows, n_cols)[0]
    s2.send()
    s3.send()
    d_context, s2.terms[0], s3.terms[0] = chain.wait(d_context, s2.terms[0], s3.terms[0])

    def taken(*scatters):
        got = chain.wait(*[s.came for s in scatters])
        for s, came in zip(scatters, got if len(scatters) > 1 else (got,)):
            s.take(came)
        outs = chain.wait(*[s.out for s in scatters])
        for s, out in zip(scatters, outs if len(scatters) > 1 else (outs,)):
            s.out = out
            s.send()

    count = pairs // 2
    mixed, parts = [], []
    kept_out, sent = from_chunk(output)
    d_context, sent = chain.wait(d_context, sent)
    came_output = trade(sent)
    for i in range(count):
        d_context = chain.wait(d_context)
        got = list(
            attention_backward(info, qkv, kv, halo, mem_kv, wls, lse, d_context, heads, VMEM_BYTES, i, 2, count)
        )
        got[0] = chain.wait(got[0])
        mixed.append(got)
        d_q, d_k, d_v, d_mk, d_mv, _ = got
        if halo:
            d_kv = jnp.concatenate([d_k, d_v], axis=1)
            ret = lax.ppermute(d_kv[:halo], "col", back)
            d_kv = d_kv[halo:].astype(f32) + jnp.pad(ret.astype(f32), ((2 * span - halo, 0), (0, 0)))
            d_kv = d_kv.astype(bf)
            d_k, d_v = jnp.split(d_kv, 2, axis=1)
        parts.append((d_q, d_k, d_v, d_mk, d_mv))
        if i == 0:
            came_output = chain.wait(came_output)
            taken(s2, s3)
        if i == count - 2 and direct:
            s1 = weight_grads(info, nT, basisT, parts, n_rows, [(len(parts) * 5 * (feat // pairs), zxy)], VMEM_BYTES)
            s1[0].send()
            s1[0].terms[0] = chain.wait(s1[0].terms[0])
    taken(s3)
    taken(s2)
    if direct:
        taken(s1[0])
    d_middle = chain.wait(d_middle)
    d_tok, g_vec1 = token_grad([p[:3] for p in parts], wq, x, d_middle, vec1, VMEM_BYTES)
    d_tok, g_vec1 = chain.wait(d_tok, g_vec1)
    taken(s3)
    taken(s2)
    kept_x, sent_x = from_chunk(d_tok)
    came_x = trade(chain.wait(sent_x.astype(bf)))
    nT = chain.wait(nT)
    if direct:
        s1 += weight_grads(info, nT, basisT, parts[-1:], n_rows, [(5 * (feat // pairs), zyx)], VMEM_BYTES)
        s1[1].send()
    else:
        ordered = [jnp.stack([p[k].reshape(p[k].shape[0], 2, -1) for p in parts], axis=2) for k in range(5)]
        ordered = [a.reshape(a.shape[0], feat) for a in ordered]
        g_qkv = jnp.dot(nT, jnp.concatenate(ordered[:3], axis=1), preferred_element_type=f32).astype(bf)
        g_mem = jnp.dot(basisT, jnp.concatenate(ordered[3:], axis=1), preferred_element_type=f32).astype(bf)
        s1 = disperse(place, [g_qkv, g_mem], [(cut1, zyx), (width1 - cut1, zxy)], n_rows, n_cols)
        for s_ in s1:
            s_.send()
    s1[-1].terms[0] = chain.wait(s1[-1].terms[0])
    by_pair = [m[5][j] for j in range(2) for m in mixed]
    total = jnp.concatenate([g_vec, g_vec1, g_bfc] + by_pair, axis=1)
    stages = core + far + along + near
    came = swap(total.astype(bf), stages.pop(0))
    kept_out, came_output = chain.wait(kept_out, came_output)
    last, early = s1[-1], s1[0]
    everyone = [last, early, s3, s2]
    plan = [last, early, None, last, early, s3, None, last, came_x, early, s2, None, last, early, s3, None, last, s2, None]
    while any(s_.total is None for s_ in everyone) or came is not None:
        s_ = plan.pop(0) if plan else next((s_ for s_ in everyone if s_.total is None), None)
        if s_ is came_x:
            came_x = chain.wait(came_x)
        elif s_ is None:
            if came is not None:
                total = total + chain.wait(came).astype(f32)
                came = swap(total.astype(bf), stages.pop(0)) if stages else None
        elif s_.left:
            onward(chain, s_)
        elif s_.total is None:
            s_.take(chain.wait(s_.came))
    index = row * n_cols + col

    def mine(block, first, width):
        return lax.dynamic_slice_in_dim(block, first + index * width, width, axis=1)

    g_bo, g_gain2, g_bias2, g_bp = mine(total, 0, gain_mlp.shape[0])[:4]
    g_gain1, g_bias1 = mine(total, feat, gain_attn.shape[0])[:2]
    g_bf = mine(total, 2 * feat, b_fc.shape[0])[0]
    per_pair = total[:, 2 * feat + hidden :].reshape(8, pairs, nb).transpose(1, 0, 2)
    g_loc = lax.dynamic_slice_in_dim(per_pair[:, 0:2].reshape(heads, nb), index * share, share, axis=1)
    g_spread = lax.dynamic_slice_in_dim(per_pair[:, 2:4].reshape(heads, nb), index * share, share, axis=1)
    outputs = paired(kept_out, came_output)
    grad_x = paired(kept_x, came_x.astype(f32))
    joined = jnp.concatenate([s_.total for s_ in s1], axis=1)
    if direct:
        w = feat // pairs
        n_qkv = layout1[0] // (count * w)
        blocks = joined.reshape(rows1, count, 5, w)
        grad_qkv = blocks[:, :, :n_qkv].transpose(0, 2, 1, 3).reshape(rows1, layout1[0])
        grad_mem = blocks[:, :, n_qkv:].transpose(0, 2, 1, 3).reshape(rows1, layout1[1])
    else:
        grad_qkv, grad_mem = joined[:, : layout1[0]], joined[:, layout1[0] :]
    grad_fc, grad_out = s2.total[:, : layout2[0]], s2.total[:, layout2[0] :]
    grad_proj = s3.total
    return (
        outputs, grad_x, grad_qkv, grad_out, grad_mem, grad_fc, grad_proj,
        g_gain1, g_bias1, g_gain2, g_bias2, g_bo, g_bf, g_bp, g_loc, g_spread,
    )


def solution(mesh):
    grid, both, tail = P("row", "col"), P(("row", "col")), P(None, ("row", "col"))
    act, rows = P(None, "row", "col", None), P(None, "row")
    return jax.shard_map(
        shards,
        mesh=mesh,
        in_specs=(act,) + (grid,) * 5 + (both,) * 7 + (tail,) * 2 + (act, P(None, "row", None), rows, act),
        out_specs=(act, act) + (grid,) * 5 + (both,) * 7 + (tail,) * 2,
        check_vma=False,
    )
```
